32 devices in a mesh: dp: 16 (over z, y, x), tensor: 2 (over core).
Axes of the slice: x: 2, y: 2, z: 4, core: 2. Of those that a mesh axis runs over, the one named last changes fastest.
Arguments:
- video_input: bfloat16 [16, 8, 197, 768], P('dp', 'tensor'), may hold values from -6 to 6
- text_input: bfloat16 [16384, 512], P(('dp', 'tensor')), may hold values from -6 to 6
- caption_lengths: int32 [16, 64], P('dp'), may hold values from 1 to 77, 1024 in all within a row
- video_first_gain: bfloat16 [768], replicated, may hold values from 0.5 to 1.5
- video_first_shift: bfloat16 [768], replicated, may hold values from -1.25 to 1.25
- video_message_weight: bfloat16 [768, 768], replicated, may hold values from -0.21875 to 0.21875
- video_message_bias: bfloat16 [768], replicated, may hold values from -1.25 to 1.25
- video_message_gain: bfloat16 [768], replicated, may hold values from 0.5 to 1.5
- video_message_shift: bfloat16 [768], replicated, may hold values from -1.25 to 1.25
- video_message_attend_weight: bfloat16 [768, 3, 768], replicated, may hold values from -0.21875 to 0.21875
- video_message_attend_bias: bfloat16 [2, 768], replicated, may hold values from -1.25 to 1.25
- video_message_out_weight: bfloat16 [768, 768], replicated, may hold values from -0.625 to 0.625
- video_message_out_bias: bfloat16 [768], replicated, may hold values from -1.25 to 1.25
- video_attend_weight: bfloat16 [768, 3, 768], P(None, None, 'tensor'), may hold values from -0.21875 to 0.21875
- video_attend_bias: bfloat16 [2, 768], P(None, 'tensor'), may hold values from -1.25 to 1.25
- video_output_weight: bfloat16 [768, 768], P('tensor'), may hold values from -0.875 to 0.875
- video_output_bias: bfloat16 [768], replicated, may hold values from -1.25 to 1.25
- video_final_gain: bfloat16 [768], replicated, may hold values from 0.5 to 1.5
- video_final_shift: bfloat16 [768], replicated, may hold values from -1.25 to 1.25
- video_expand_weight: bfloat16 [768, 3072], P(None, 'tensor'), may hold values from -0.21875 to 0.21875
- video_expand_bias: bfloat16 [3072], P('tensor'), may hold values from -1.25 to 1.25
- video_reduce_weight: bfloat16 [3072, 768], P('tensor'), may hold values from -0.109375 to 0.109375
- video_reduce_bias: bfloat16 [768], replicated, may hold values from -1.25 to 1.25
- text_first_gain: bfloat16 [512], replicated, may hold values from 0.5 to 1.5
- text_first_shift: bfloat16 [512], replicated, may hold values from -1.25 to 1.25
- text_attend_weight: bfloat16 [512, 3, 512], P(None, None, 'tensor'), may hold values from -0.25 to 0.25
- text_attend_bias: bfloat16 [2, 512], P(None, 'tensor'), may hold values from -1.25 to 1.25
- text_output_weight: bfloat16 [512, 512], P('tensor'), may hold values from -0.5 to 0.5
- text_output_bias: bfloat16 [512], replicated, may hold values from -1.25 to 1.25
- text_final_gain: bfloat16 [512], replicated, may hold values from 0.5 to 1.5
- text_final_shift: bfloat16 [512], replicated, may hold values from -1.25 to 1.25
- text_expand_weight: bfloat16 [512, 2048], P(None, 'tensor'), may hold values from -0.25 to 0.25
- text_expand_bias: bfloat16 [2048], P('tensor'), may hold values from -1.25 to 1.25
- text_reduce_weight: bfloat16 [2048, 512], P('tensor'), may hold values from -0.125 to 0.125
- text_reduce_bias: bfloat16 [512], replicated, may hold values from -1.25 to 1.25
- video_out_grad: bfloat16 [16, 8, 197, 768], P('dp', 'tensor'), may hold values from -6 to 6
- message_out_grad: bfloat16 [16, 8, 768], P('dp', 'tensor'), may hold values from -6 to 6
- text_out_grad: bfloat16 [16384, 512], P(('dp', 'tensor')), may hold values from -6 to 6
Outputs:
- video_output: bfloat16 [16, 8, 197, 768], P('dp', 'tensor')
- message_output: bfloat16 [16, 8, 768], P('dp', 'tensor')
- text_output: bfloat16 [16384, 512], P(('dp', 'tensor'))
- video_input_grad: bfloat16 [16, 8, 197, 768], P('dp', 'tensor')
- text_input_grad: bfloat16 [16384, 512], P(('dp', 'tensor'))
- grad_video_first_gain: float32 [768], replicated
- grad_video_first_shift: float32 [768], replicated
- grad_video_message_weight: float32 [768, 768], replicated
- grad_video_message_bias: float32 [768], replicated
- grad_video_message_gain: float32 [768], replicated
- grad_video_message_shift: float32 [768], replicated
- grad_video_message_attend_weight: float32 [768, 3, 768], replicated
- grad_video_message_attend_bias: float32 [2, 768], replicated
- grad_video_message_out_weight: float32 [768, 768], replicated
- grad_video_message_out_bias: float32 [768], replicated
- grad_video_attend_weight: float32 [768, 3, 768], P(None, None, 'tensor')
- grad_video_attend_bias: float32 [2, 768], P(None, 'tensor')
- grad_video_output_weight: float32 [768, 768], P('tensor')
- grad_video_output_bias: float32 [768], replicated
- grad_video_final_gain: float32 [768], replicated
- grad_video_final_shift: float32 [768], replicated
- grad_video_expand_weight: float32 [768, 3072], P(None, 'tensor')
- grad_video_expand_bias: float32 [3072], P('tensor')
- grad_video_reduce_weight: float32 [3072, 768], P('tensor')
- grad_video_reduce_bias: float32 [768], replicated
- grad_text_first_gain: float32 [512], replicated
- grad_text_first_shift: float32 [512], replicated
- grad_text_attend_weight: float32 [512, 3, 512], P(None, None, 'tensor')
- grad_text_attend_bias: float32 [2, 512], P(None, 'tensor')
- grad_text_output_weight: float32 [512, 512], P('tensor')
- grad_text_output_bias: float32 [512], replicated
- grad_text_final_gain: float32 [512], replicated
- grad_text_final_shift: float32 [512], replicated
- grad_text_expand_weight: float32 [512, 2048], P(None, 'tensor')
- grad_text_expand_bias: float32 [2048], P('tensor')
- grad_text_reduce_weight: float32 [2048, 512], P('tensor')
- grad_text_reduce_bias: float32 [512], replicated
The draws below stay inside these ranges and needn't reach their ends.
Inputs may be any that keep to these rules, and one draw needn't show every extreme that they name: Each row of caption_lengths holds the lengths of the 64 captions packed in order into one pack; each row sums to 1024 and its longest caption has exactly 77 tokens.
All inputs are finite; a program needn't handle non-finite values.
Results may differ from the reference program's by a relative error of at most 0.02.
Values may be sent and summed in bfloat16 or wider, within the bound.
No kernel may reach another device: no remote copies, remote signals or barrier semaphores. Data moves between devices by JAX's collectives and lax.ppermute only.
A program may use at most 256 MiB of HBM per device.

```python
import math
from functools import partial
import jax
import jax.numpy as jnp
import numpy as np
from jax import lax

D = 768
HD = 64
FF = 3072
P_SIZE = 197
F = 8
DT = 512
FT = 2048
MAXLEN = 77
TXT_DEV = 1024
CAPS = 64
PACKS = 16
NV = 16
NT = 16384


def level_of(stream_key, dims, shards, low, high):
    def one(dim, shards_of):
        heights = jax.random.uniform(jax.random.fold_in(jax.random.fold_in(stream_key, 6), dim), (shards_of,), jnp.float32, low / len(shards), high / len(shards))
        return jnp.repeat(jnp.exp(heights), dims[dim] // shards_of).reshape((-1,) + (1,) * (len(dims) - dim - 1))

    level = one(*shards[0])
    for cut in shards[1:]:
        level = level * one(*cut)
    return level


def profile(count, total, bound, lean):
    loads = [(1 << 20) // math.isqrt(grade ** lean) + 1 for grade in range(2, count + 1)]
    surplus, given = total - bound - (count - 1), [1] * (count - 1)
    while surplus > 0:
        candidates = [i for i in range(count - 1) if given[i] < bound]
        whole, left = sum([loads[i] for i in candidates]), surplus
        for i in candidates:
            extra = min(bound - given[i], max(1, left * loads[i] // whole), surplus)
            given[i] = given[i] + extra
            surplus = surplus - extra
    return np.array([bound] + given)


def uneven_parts(key, count, total, reach, skew):
    if count == 2:
        one = jax.random.randint(key, (), max(1, total - reach), min(reach, total - 1) + 1)
        return jnp.stack([one, total - one])
    sizes = jnp.asarray(profile(count, total, reach, skew), jnp.int32)
    couples = (count - 1) // 2
    donor, taker = sizes[1:1 + 2 * couples:2], sizes[2:2 + 2 * couples:2]
    slack = jnp.minimum(donor - 1, reach - taker)
    moved = jax.random.randint(jax.random.fold_in(key, 1), (couples,), 0, 1 << 20) % (slack + 1)
    sizes = sizes.at[1:1 + 2 * couples:2].set(donor - moved).at[2:2 + 2 * couples:2].set(taker + moved)
    return sizes[jax.random.permutation(jax.random.fold_in(key, 2), count)]


def noise(rng, shape, width, reach, shards=(), kind=jnp.bfloat16):
    result = jax.random.normal(rng, shape, jnp.float32) * width
    if len(shards) > 0:
        result = level_of(rng, shape, shards, -0.22, 0.18) * result
    return jnp.clip(result, min=-reach, max=reach).astype(kind)


def setup_inputs(seed: int = 0) -> dict:
    arg_keys = jax.random.split(jax.random.key(seed), 39)
    video_input = noise(arg_keys[0], (NV, F, P_SIZE, D), 1.0, 6.0, ((0, 16), (1, 2)))
    text_input = noise(arg_keys[1], (NT, DT), 1.0, 6.0, ((0, 32),))
    caption_lengths = jax.vmap(lambda own: uneven_parts(own, CAPS, TXT_DEV, MAXLEN, 2))(jax.random.split(arg_keys[2], PACKS)).reshape((PACKS, CAPS)).astype(jnp.int32)
    video_first_gain = jnp.clip(1.0 + 0.1 * jax.random.normal(arg_keys[3], (D,), jnp.float32), 0.5, 1.5).astype(jnp.bfloat16)
    video_first_shift = noise(arg_keys[4], (D,), 0.2, 1.25)
    video_message_weight = noise(arg_keys[5], (D, D), D ** -0.5, 0.21875)
    video_message_bias = noise(arg_keys[6], (D,), 0.2, 1.25)
    video_message_gain = jnp.clip(1.0 + 0.1 * jax.random.normal(arg_keys[7], (D,), jnp.float32), 0.5, 1.5).astype(jnp.bfloat16)
    video_message_shift = noise(arg_keys[8], (D,), 0.2, 1.25)
    video_message_attend_weight = noise(arg_keys[9], (D, 3, D), D ** -0.5, 0.21875)
    video_message_attend_bias = noise(arg_keys[10], (2, D), 0.2, 1.25)
    video_message_out_weight = noise(arg_keys[11], (D, D), (D // 8) ** -0.5, 0.625)
    video_message_out_bias = noise(arg_keys[12], (D,), 0.2, 1.25)
    video_attend_weight = noise(arg_keys[13], (D, 3, D), D ** -0.5, 0.21875, ((2, 2),))
    video_attend_bias = noise(arg_keys[14], (2, D), 0.2, 1.25, ((1, 2),))
    video_output_weight = noise(arg_keys[15], (D, D), (D // 16) ** -0.5, 0.875, ((0, 2),))
    video_output_bias = noise(arg_keys[16], (D,), 0.2, 1.25)
    video_final_gain = jnp.clip(1.0 + 0.1 * jax.random.normal(arg_keys[17], (D,), jnp.float32), 0.5, 1.5).astype(jnp.bfloat16)
    video_final_shift = noise(arg_keys[18], (D,), 0.2, 1.25)
    video_expand_weight = noise(arg_keys[19], (D, FF), D ** -0.5, 0.21875, ((1, 2),))
    video_expand_bias = noise(arg_keys[20], (FF,), 0.2, 1.25, ((0, 2),))
    video_reduce_weight = noise(arg_keys[21], (FF, D), FF ** -0.5, 0.109375, ((0, 2),))
    video_reduce_bias = noise(arg_keys[22], (D,), 0.2, 1.25)
    text_first_gain = jnp.clip(1.0 + 0.1 * jax.random.normal(arg_keys[23], (DT,), jnp.float32), 0.5, 1.5).astype(jnp.bfloat16)
    text_first_shift = noise(arg_keys[24], (DT,), 0.2, 1.25)
    text_attend_weight = noise(arg_keys[25], (DT, 3, DT), DT ** -0.5, 0.25, ((2, 2),))
    text_attend_bias = noise(arg_keys[26], (2, DT), 0.2, 1.25, ((1, 2),))
    text_output_weight = noise(arg_keys[27], (DT, DT), (DT // 4) ** -0.5, 0.5, ((0, 2),))
    text_output_bias = noise(arg_keys[28], (DT,), 0.2, 1.25)
    text_final_gain = jnp.clip(1.0 + 0.1 * jax.random.normal(arg_keys[29], (DT,), jnp.float32), 0.5, 1.5).astype(jnp.bfloat16)
    text_final_shift = noise(arg_keys[30], (DT,), 0.2, 1.25)
    text_expand_weight = noise(arg_keys[31], (DT, FT), DT ** -0.5, 0.25, ((1, 2),))
    text_expand_bias = noise(arg_keys[32], (FT,), 0.2, 1.25, ((0, 2),))
    text_reduce_weight = noise(arg_keys[33], (FT, DT), FT ** -0.5, 0.125, ((0, 2),))
    text_reduce_bias = noise(arg_keys[34], (DT,), 0.2, 1.25)
    video_out_grad = noise(arg_keys[35], (NV, F, P_SIZE, D), 1.0, 6.0, ((0, 16), (1, 2)))
    message_out_grad = noise(arg_keys[36], (NV, F, D), 1.0, 6.0, ((0, 16), (1, 2)))
    text_out_grad = noise(arg_keys[37], (NT, DT), 1.0, 6.0, ((0, 32),))
    return dict(video_input=video_input, text_input=text_input, caption_lengths=caption_lengths, video_first_gain=video_first_gain, video_first_shift=video_first_shift, video_message_weight=video_message_weight, video_message_bias=video_message_bias, video_message_gain=video_message_gain, video_message_shift=video_message_shift, video_message_attend_weight=video_message_attend_weight, video_message_attend_bias=video_message_attend_bias, video_message_out_weight=video_message_out_weight, video_message_out_bias=video_message_out_bias, video_attend_weight=video_attend_weight, video_attend_bias=video_attend_bias, video_output_weight=video_output_weight, video_output_bias=video_output_bias, video_final_gain=video_final_gain, video_final_shift=video_final_shift, video_expand_weight=video_expand_weight, video_expand_bias=video_expand_bias, video_reduce_weight=video_reduce_weight, video_reduce_bias=video_reduce_bias, text_first_gain=text_first_gain, text_first_shift=text_first_shift, text_attend_weight=text_attend_weight, text_attend_bias=text_attend_bias, text_output_weight=text_output_weight, text_output_bias=text_output_bias, text_final_gain=text_final_gain, text_final_shift=text_final_shift, text_expand_weight=text_expand_weight, text_expand_bias=text_expand_bias, text_reduce_weight=text_reduce_weight, text_reduce_bias=text_reduce_bias, video_out_grad=video_out_grad, message_out_grad=message_out_grad, text_out_grad=text_out_grad)


@jax.custom_vjp
def low(v):
    return lax.optimization_barrier(v.astype(jnp.bfloat16)).astype(jnp.float32)

@jax.custom_vjp
def low_back(v):
    return v

def low_keep(v):
    return (low(v), None)

def low_pass(kept, grad):
    return (grad,)

def back_keep(v):
    return (v, None)

def back_low(kept, grad):
    return (low(grad),)
low.defvjp(low_keep, low_pass)
low_back.defvjp(back_keep, back_low)

def product(left, right):
    return jnp.tensordot(left, right, axes=1, precision=lax.Precision.HIGHEST)

def norm_rows(inputs, gain_row, shift_row):
    centre = inputs - lax.optimization_barrier(jnp.mean(inputs, axis=-1, keepdims=True))
    inverse = lax.rsqrt(lax.optimization_barrier(jnp.mean(centre * centre, axis=-1, keepdims=True)) + 1e-05)
    return centre * inverse * gain_row + shift_row

def project_heads(normed, attend_weight, attend_bias):
    full_bias = jnp.stack([attend_bias[0], jnp.zeros_like(attend_bias[0]), attend_bias[1]])
    mixed = jnp.einsum('...d,dcm->...cm', normed, attend_weight, precision=lax.Precision.HIGHEST)
    return low(low_back(mixed + full_bias))

def feed_forward(resid, final_gain, final_shift, expand_weight, expand_bias, reduce_weight, reduce_bias):
    normed = low(norm_rows(resid, final_gain, final_shift))
    hidden = low_back(product(normed, expand_weight) + expand_bias)
    active = low(hidden * jax.nn.sigmoid(1.702 * hidden))
    return resid + low_back(product(active, reduce_weight)) + reduce_bias

def attend_messages(mixed):
    heads_all = mixed.reshape(mixed.shape[:3] + (-1, HD))
    scores = low_back(jnp.einsum('vfhe,vghe->vhfg', heads_all[:, :, 0], heads_all[:, :, 1], precision=lax.Precision.HIGHEST) * 0.125)
    weights = low(jax.nn.softmax(scores, axis=-1))
    output = jnp.einsum('vhfg,vghe->vfhe', weights, heads_all[:, :, 2], precision=lax.Precision.HIGHEST)
    return low(low_back(output)).reshape(mixed.shape[0], mixed.shape[1], -1)

def attend_frame(mixed):
    row_count = mixed.shape[0]
    heads_all = mixed.reshape(row_count, 3, -1, HD)
    scores = low_back(jnp.einsum('qhe,khe->hqk', heads_all[:, 0], heads_all[:, 1], precision=lax.Precision.HIGHEST) * 0.125)
    weights = low(jax.nn.softmax(scores, axis=-1))
    output = jnp.einsum('hqk,khe->qhe', weights, heads_all[:, 2], precision=lax.Precision.HIGHEST)
    return low(low_back(output)).reshape(row_count, -1)

def attend_pack(operands):
    mixed, segment_ids = operands
    length = mixed.shape[0]
    heads_all = mixed.reshape(length, 3, -1, HD)
    positions = jnp.arange(length, dtype=jnp.int32)
    allowed = (segment_ids[:, None] == segment_ids[None, :]) & (positions[None, :] <= positions[:, None])
    scores = low_back(jnp.einsum('qhe,khe->hqk', heads_all[:, 0], heads_all[:, 1], precision=lax.Precision.HIGHEST) * 0.125)
    scores = jnp.where(allowed[None], scores, -1000000000.0)
    weights = low(jax.nn.softmax(scores, axis=-1))
    output = jnp.einsum('hqk,khe->qhe', weights, heads_all[:, 2], precision=lax.Precision.HIGHEST)
    return low(low_back(output)).reshape(length, -1)

def video_layer(video, first_gain, first_shift, message_weight, message_bias, message_gain, message_shift, message_attend_weight, message_attend_bias, message_out_weight, message_out_bias, attend_weight, attend_bias, output_weight, output_bias, final_gain, final_shift, expand_weight, expand_bias, reduce_weight, reduce_bias):
    messages = low_back(product(video[:, :, 0], message_weight)) + message_bias
    message_mixed = project_heads(low(norm_rows(messages, message_gain, message_shift)), message_attend_weight, message_attend_bias)
    tokens = messages + low_back(product(attend_messages(message_mixed), message_out_weight)) + message_out_bias
    rows = jnp.concatenate([video, tokens[:, :, None]], axis=2)
    mixed = project_heads(low(norm_rows(rows, first_gain, first_shift)), attend_weight, attend_bias)
    shape = mixed.shape
    attended = lax.map(jax.checkpoint(attend_frame), mixed.reshape((-1,) + shape[2:]))
    attended = attended.reshape(shape[:3] + (-1,))
    resid = rows + low_back(product(attended, output_weight)) + output_bias
    trunk = resid[:, :, :P_SIZE]
    final = feed_forward(trunk, final_gain, final_shift, expand_weight, expand_bias, reduce_weight, reduce_bias)
    return (final, resid[:, :, P_SIZE])

def text_layer(segments, text, first_gain, first_shift, attend_weight, attend_bias, output_weight, output_bias, final_gain, final_shift, expand_weight, expand_bias, reduce_weight, reduce_bias):
    mixed = project_heads(low(norm_rows(text, first_gain, first_shift)), attend_weight, attend_bias)
    packed = mixed.reshape(PACKS, TXT_DEV, 3, -1)
    attended = lax.map(jax.checkpoint(attend_pack), (packed, segments)).reshape(text.shape[0], -1)
    resid = text + low_back(product(attended, output_weight)) + output_bias
    return feed_forward(resid, final_gain, final_shift, expand_weight, expand_bias, reduce_weight, reduce_bias)

def reference(video_input, text_input, caption_lengths, video_first_gain, video_first_shift, video_message_weight, video_message_bias, video_message_gain, video_message_shift, video_message_attend_weight, video_message_attend_bias, video_message_out_weight, video_message_out_bias, video_attend_weight, video_attend_bias, video_output_weight, video_output_bias, video_final_gain, video_final_shift, video_expand_weight, video_expand_bias, video_reduce_weight, video_reduce_bias, text_first_gain, text_first_shift, text_attend_weight, text_attend_bias, text_output_weight, text_output_bias, text_final_gain, text_final_shift, text_expand_weight, text_expand_bias, text_reduce_weight, text_reduce_bias, video_out_grad, message_out_grad, text_out_grad):
    video_params = tuple((argument.astype(jnp.float32) for argument in (video_input, video_first_gain, video_first_shift, video_message_weight, video_message_bias, video_message_gain, video_message_shift, video_message_attend_weight, video_message_attend_bias, video_message_out_weight, video_message_out_bias, video_attend_weight, video_attend_bias, video_output_weight, video_output_bias, video_final_gain, video_final_shift, video_expand_weight, video_expand_bias, video_reduce_weight, video_reduce_bias)))
    video_final, video_pull = jax.vjp(video_layer, *video_params)
    video_grads = video_pull((video_out_grad.astype(jnp.float32), message_out_grad.astype(jnp.float32)))
    caption_ends = jnp.cumsum(caption_lengths, axis=1).astype(jnp.int32)
    positions = jnp.arange(TXT_DEV, dtype=jnp.int32)
    segments = lax.optimization_barrier(jnp.sum((positions[None, :, None] >= caption_ends[:, None, :]).astype(jnp.int32), axis=2)).astype(jnp.int32)
    text_params = tuple((argument.astype(jnp.float32) for argument in (text_input, text_first_gain, text_first_shift, text_attend_weight, text_attend_bias, text_output_weight, text_output_bias, text_final_gain, text_final_shift, text_expand_weight, text_expand_bias, text_reduce_weight, text_reduce_bias)))
    text_final, text_pull = jax.vjp(partial(text_layer, segments), *text_params)
    text_grads = text_pull(text_out_grad.astype(jnp.float32))
    return (video_final[0].astype(jnp.bfloat16), video_final[1].astype(jnp.bfloat16), text_final.astype(jnp.bfloat16), video_grads[0].astype(jnp.bfloat16), text_grads[0].astype(jnp.bfloat16), video_grads[1], video_grads[2], video_grads[3], video_grads[4], video_grads[5], video_grads[6], video_grads[7], video_grads[8], video_grads[9], video_grads[10], video_grads[11], video_grads[12], video_grads[13], video_grads[14], video_grads[15], video_grads[16], video_grads[17], video_grads[18], video_grads[19], video_grads[20], text_grads[1], text_grads[2], text_grads[3], text_grads[4], text_grads[5], text_grads[6], text_grads[7], text_grads[8], text_grads[9], text_grads[10], text_grads[11], text_grads[12])
```

```python
import jax
import jax.numpy as jnp
from jax import lax
from jax.sharding import PartitionSpec as P

HD = 64
MAXLEN = 77


def norm_forward(inputs, gain_row, shift_row):
    centre = inputs - jnp.mean(inputs, axis=-1, keepdims=True)
    inverse = lax.rsqrt(jnp.mean(centre * centre, axis=-1, keepdims=True) + 1e-05)
    unit_rows = centre * inverse
    return (unit_rows * gain_row + shift_row, unit_rows, inverse)


def norm_backward(grad_out, unit_rows, inverse, gain_row):
    scaled = grad_out * gain_row
    grad_in = inverse * (
        scaled
        - jnp.mean(scaled, axis=-1, keepdims=True)
        - unit_rows * jnp.mean(scaled * unit_rows, axis=-1, keepdims=True)
    )
    columns = grad_out.shape[-1]
    gain_grad = jnp.sum((grad_out * unit_rows).reshape(-1, columns), axis=0)
    shift_grad = jnp.sum(grad_out.reshape(-1, columns), axis=0)
    return (grad_in, gain_grad, shift_grad)


def gelu_parts(hidden):
    logistic = jax.nn.sigmoid(1.702 * hidden)
    return (hidden * logistic, logistic + 1.702 * hidden * logistic * (1.0 - logistic))


def full_bias(attend_bias):
    bias_rows = attend_bias.astype(jnp.float32)
    return jnp.stack([bias_rows[0], jnp.zeros_like(bias_rows[0]), bias_rows[1]])


def row_sums(values):
    return jnp.sum(values.reshape(-1, values.shape[-1]), axis=0)


def video_scores(queries, key_rows):
    return (
        jnp.einsum("vfrhe,vfkhe->vfhrk", queries, key_rows, preferred_element_type=jnp.float32)
        * 0.125
    )


def text_scores(query_block, key_block, segment_ids, block_start, key_start):
    block_rows = query_block.shape[0]
    window = key_block.shape[0]
    positions = block_start + jnp.arange(block_rows, dtype=jnp.int32)
    query_segments = lax.dynamic_slice_in_dim(segment_ids, block_start, block_rows)
    key_positions = key_start + jnp.arange(window, dtype=jnp.int32)
    key_segments = lax.dynamic_slice_in_dim(segment_ids, key_start, window)
    allowed = (query_segments[:, None] == key_segments[None, :]) & (
        key_positions[None, :] <= positions[:, None]
    )
    scores = (
        jnp.einsum("qhe,khe->hqk", query_block, key_block, preferred_element_type=jnp.float32)
        * 0.125
    )
    return jnp.where(allowed[None], scores, -1000000000.0)


def reduce_low(values, axes):
    sums = lax.psum(tuple(value.astype(jnp.bfloat16) for value in values), axes)
    return tuple(value.astype(jnp.float32) for value in sums)


def reduce_packed(values, axes):
    packed = lax.psum(jnp.concatenate([value.reshape(-1) for value in values]), axes)
    results = []
    start = 0
    for value in values:
        results.append(packed[start : start + value.size].reshape(value.shape))
        start += value.size
    return tuple(results)


def on_device(
    video_input,
    text_input,
    caption_lengths,
    video_first_gain,
    video_first_shift,
    video_message_weight,
    video_message_bias,
    video_message_gain,
    video_message_shift,
    video_message_attend_weight,
    video_message_attend_bias,
    video_message_out_weight,
    video_message_out_bias,
    video_attend_weight,
    video_attend_bias,
    video_output_weight,
    video_output_bias,
    video_final_gain,
    video_final_shift,
    video_expand_weight,
    video_expand_bias,
    video_reduce_weight,
    video_reduce_bias,
    text_first_gain,
    text_first_shift,
    text_attend_weight,
    text_attend_bias,
    text_output_weight,
    text_output_bias,
    text_final_gain,
    text_final_shift,
    text_expand_weight,
    text_expand_bias,
    text_reduce_weight,
    text_reduce_bias,
    video_out_grad,
    message_out_grad,
    text_out_grad,
):
    token_count = video_input.shape[2]
    frames_here = video_input.shape[1]
    class_rows = video_input[:, :, 0, :]
    message_here = jnp.einsum(
        "vfd,de->vfe", class_rows, video_message_weight, preferred_element_type=jnp.float32
    ) + video_message_bias.astype(jnp.float32)
    message_all = lax.all_gather(message_here, "tensor", axis=1, tiled=True)
    message_gain_row = video_message_gain.astype(jnp.float32)
    message_normed, message_unit, message_inverse = norm_forward(
        message_all, message_gain_row, video_message_shift.astype(jnp.float32)
    )
    message_normed_low = message_normed.astype(jnp.bfloat16)
    message_mixed = (
        jnp.einsum(
            "vfd,dcm->vfcm",
            message_normed_low,
            video_message_attend_weight,
            preferred_element_type=jnp.float32,
        )
        + full_bias(video_message_attend_bias)
    ).astype(jnp.bfloat16)
    message_heads = message_mixed.reshape(message_mixed.shape[:3] + (-1, HD))
    message_queries = message_heads[:, :, 0]
    message_keys = message_heads[:, :, 1]
    message_values = message_heads[:, :, 2]
    message_scores = (
        jnp.einsum(
            "vfhe,vghe->vhfg", message_queries, message_keys, preferred_element_type=jnp.float32
        )
        * 0.125
    )
    message_probs = jax.nn.softmax(message_scores, axis=-1)
    message_probs_low = message_probs.astype(jnp.bfloat16)
    message_attended = jnp.einsum(
        "vhfg,vghe->vfhe", message_probs_low, message_values, preferred_element_type=jnp.float32
    ).astype(jnp.bfloat16)
    message_attended = message_attended.reshape(message_attended.shape[:2] + (-1,))
    message_tokens = (
        message_all
        + jnp.einsum(
            "vfm,md->vfd",
            message_attended,
            video_message_out_weight,
            preferred_element_type=jnp.float32,
        )
        + video_message_out_bias.astype(jnp.float32)
    )
    frame_start = lax.axis_index("tensor") * frames_here
    tokens_here = lax.dynamic_slice_in_dim(message_tokens, frame_start, frames_here, 1)
    video_rows = jnp.concatenate([video_input.astype(jnp.float32), tokens_here[:, :, None]], axis=2)
    video_normed, video_unit_one, video_inverse_one = norm_forward(
        video_rows, video_first_gain.astype(jnp.float32), video_first_shift.astype(jnp.float32)
    )
    text_rows = text_input.astype(jnp.float32)
    text_normed, text_unit_one, text_inverse_one = norm_forward(
        text_rows, text_first_gain.astype(jnp.float32), text_first_shift.astype(jnp.float32)
    )
    video_first_full, text_first_full = (
        lax.all_gather(video_normed.astype(jnp.bfloat16), "tensor", axis=1, tiled=True),
        lax.all_gather(text_normed.astype(jnp.bfloat16), "tensor", axis=0, tiled=True),
    )
    video_mixed = (
        jnp.einsum(
            "vfrd,dcm->vfrcm",
            video_first_full,
            video_attend_weight,
            preferred_element_type=jnp.float32,
        )
        + full_bias(video_attend_bias)
    ).astype(jnp.bfloat16)
    video_heads = video_mixed.reshape(video_mixed.shape[:4] + (-1, HD))
    video_queries = video_heads[:, :, :, 0]
    video_key_rows = video_heads[:, :, :, 1]
    video_value_rows = video_heads[:, :, :, 2]
    scores_now = video_scores(video_queries, video_key_rows)
    row_max = jnp.max(scores_now, axis=-1, keepdims=True)
    video_logsum = row_max + jnp.log(jnp.sum(jnp.exp(scores_now - row_max), axis=-1, keepdims=True))
    video_probs = jnp.exp(scores_now - video_logsum).astype(jnp.bfloat16)
    video_attended = jnp.einsum(
        "vfhrk,vfkhe->vfrhe", video_probs, video_value_rows, preferred_element_type=jnp.float32
    ).astype(jnp.bfloat16)
    video_attended = video_attended.reshape(video_attended.shape[:3] + (-1,))
    text_length = text_first_full.shape[0]
    block_rows = min(512, text_length)
    block_count = text_length // block_rows
    key_extra = -(-(MAXLEN - 1) // 128) * 128
    window = min(block_rows + key_extra, text_length)
    starts = jnp.arange(block_count, dtype=jnp.int32) * block_rows
    caption_ends = jnp.cumsum(caption_lengths[0])
    positions = jnp.arange(text_length, dtype=jnp.int32)
    text_segments = jnp.sum((positions[:, None] >= caption_ends[None, :]).astype(jnp.int32), axis=1)
    text_mixed = (
        jnp.einsum(
            "sd,dcm->scm", text_first_full, text_attend_weight, preferred_element_type=jnp.float32
        )
        + full_bias(text_attend_bias)
    ).astype(jnp.bfloat16)
    text_heads = text_mixed.reshape(text_length, 3, -1, HD)
    text_key_rows = text_heads[:, 1]
    text_value_rows = text_heads[:, 2]
    query_blocks = text_heads[:, 0].reshape((block_count, block_rows) + text_heads.shape[2:])

    def window_start(block_start):
        return jnp.clip(block_start - key_extra, 0, text_length - window)

    def text_forward_block(operands):
        query_block, block_start = operands
        key_start = window_start(block_start)
        key_block = lax.dynamic_slice_in_dim(text_key_rows, key_start, window)
        value_block = lax.dynamic_slice_in_dim(text_value_rows, key_start, window)
        scores = text_scores(query_block, key_block, text_segments, block_start, key_start)
        block_max = jnp.max(scores, axis=-1, keepdims=True)
        logsum = block_max + jnp.log(jnp.sum(jnp.exp(scores - block_max), axis=-1, keepdims=True))
        probs = jnp.exp(scores - logsum).astype(jnp.bfloat16)
        output = jnp.einsum(
            "hqk,khe->qhe", probs, value_block, preferred_element_type=jnp.float32
        ).astype(jnp.bfloat16)
        return (output, logsum)

    text_outputs, text_logsums = lax.map(text_forward_block, (query_blocks, starts))
    text_attended = text_outputs.reshape(text_length, -1)
    video_partial = jnp.einsum(
        "vfrm,md->vfrd", video_attended, video_output_weight, preferred_element_type=jnp.float32
    )
    text_partial = jnp.dot(text_attended, text_output_weight, preferred_element_type=jnp.float32)
    video_attend_sum, text_attend_sum = (
        lax.psum_scatter(
            video_partial.astype(jnp.bfloat16), "tensor", scatter_dimension=1, tiled=True
        ).astype(jnp.float32),
        lax.psum_scatter(
            text_partial.astype(jnp.bfloat16), "tensor", scatter_dimension=0, tiled=True
        ).astype(jnp.float32),
    )
    video_resid = video_rows + video_attend_sum + video_output_bias.astype(jnp.float32)
    text_resid = text_rows + text_attend_sum + text_output_bias.astype(jnp.float32)
    video_trunk = video_resid[:, :, :token_count]
    message_output = video_resid[:, :, token_count].astype(jnp.bfloat16)
    video_second, video_unit_two, video_inverse_two = norm_forward(
        video_trunk, video_final_gain.astype(jnp.float32), video_final_shift.astype(jnp.float32)
    )
    text_second, text_unit_two, text_inverse_two = norm_forward(
        text_resid, text_final_gain.astype(jnp.float32), text_final_shift.astype(jnp.float32)
    )
    video_second_full, text_second_full = (
        lax.all_gather(video_second.astype(jnp.bfloat16), "tensor", axis=1, tiled=True),
        lax.all_gather(text_second.astype(jnp.bfloat16), "tensor", axis=0, tiled=True),
    )
    video_hidden = jnp.einsum(
        "vfrd,dn->vfrn", video_second_full, video_expand_weight, preferred_element_type=jnp.float32
    ) + video_expand_bias.astype(jnp.float32)
    video_active_full, video_slope = gelu_parts(video_hidden)
    video_active = video_active_full.astype(jnp.bfloat16)
    text_hidden = jnp.dot(
        text_second_full, text_expand_weight, preferred_element_type=jnp.float32
    ) + text_expand_bias.astype(jnp.float32)
    text_active_full, text_slope = gelu_parts(text_hidden)
    text_active = text_active_full.astype(jnp.bfloat16)
    video_mlp_partial = jnp.einsum(
        "vfrn,nd->vfrd", video_active, video_reduce_weight, preferred_element_type=jnp.float32
    )
    text_mlp_partial = jnp.dot(text_active, text_reduce_weight, preferred_element_type=jnp.float32)
    video_mlp_sum, text_mlp_sum = (
        lax.psum_scatter(
            video_mlp_partial.astype(jnp.bfloat16), "tensor", scatter_dimension=1, tiled=True
        ).astype(jnp.float32),
        lax.psum_scatter(
            text_mlp_partial.astype(jnp.bfloat16), "tensor", scatter_dimension=0, tiled=True
        ).astype(jnp.float32),
    )
    video_final = video_trunk + video_mlp_sum + video_reduce_bias.astype(jnp.float32)
    text_final = text_resid + text_mlp_sum + text_reduce_bias.astype(jnp.float32)
    video_output = video_final.astype(jnp.bfloat16)
    text_output = text_final.astype(jnp.bfloat16)
    video_cot_full, text_cot_full = (
        lax.all_gather(video_out_grad, "tensor", axis=1, tiled=True),
        lax.all_gather(text_out_grad, "tensor", axis=0, tiled=True),
    )
    grad_video_reduce_bias = row_sums(video_out_grad.astype(jnp.float32))
    grad_text_reduce_bias = row_sums(text_out_grad.astype(jnp.float32))
    grad_video_reduce_weight = jnp.einsum(
        "vfrn,vfrd->nd", video_active, video_cot_full, preferred_element_type=jnp.float32
    )
    grad_text_reduce_weight = jnp.einsum(
        "sn,sd->nd", text_active, text_cot_full, preferred_element_type=jnp.float32
    )
    video_grad_hidden = (
        jnp.einsum(
            "vfrd,nd->vfrn", video_cot_full, video_reduce_weight, preferred_element_type=jnp.float32
        )
        * video_slope
    ).astype(jnp.bfloat16)
    text_grad_hidden = (
        jnp.einsum(
            "sd,nd->sn", text_cot_full, text_reduce_weight, preferred_element_type=jnp.float32
        )
        * text_slope
    ).astype(jnp.bfloat16)
    grad_video_expand_bias = row_sums(video_grad_hidden.astype(jnp.float32))
    grad_text_expand_bias = row_sums(text_grad_hidden.astype(jnp.float32))
    grad_video_expand_weight = jnp.einsum(
        "vfrd,vfrn->dn", video_second_full, video_grad_hidden, preferred_element_type=jnp.float32
    )
    grad_text_expand_weight = jnp.einsum(
        "sd,sn->dn", text_second_full, text_grad_hidden, preferred_element_type=jnp.float32
    )
    video_grad_second = jnp.einsum(
        "vfrn,dn->vfrd", video_grad_hidden, video_expand_weight, preferred_element_type=jnp.float32
    )
    text_grad_second = jnp.einsum(
        "sn,dn->sd", text_grad_hidden, text_expand_weight, preferred_element_type=jnp.float32
    )
    video_back_second, text_back_second = (
        lax.psum_scatter(
            video_grad_second.astype(jnp.bfloat16), "tensor", scatter_dimension=1, tiled=True
        ).astype(jnp.float32),
        lax.psum_scatter(
            text_grad_second.astype(jnp.bfloat16), "tensor", scatter_dimension=0, tiled=True
        ).astype(jnp.float32),
    )
    video_norm_grad, grad_video_final_gain, grad_video_final_shift = norm_backward(
        video_back_second, video_unit_two, video_inverse_two, video_final_gain.astype(jnp.float32)
    )
    text_norm_grad, grad_text_final_gain, grad_text_final_shift = norm_backward(
        text_back_second, text_unit_two, text_inverse_two, text_final_gain.astype(jnp.float32)
    )
    video_grad_trunk = video_out_grad.astype(jnp.float32) + video_norm_grad
    video_grad_resid = jnp.concatenate(
        [video_grad_trunk, message_out_grad.astype(jnp.float32)[:, :, None]], axis=2
    )
    text_grad_resid = text_out_grad.astype(jnp.float32) + text_norm_grad
    grad_video_output_bias = row_sums(video_grad_resid)
    grad_text_output_bias = row_sums(text_grad_resid)
    video_resid_full, text_resid_full = (
        lax.all_gather(video_grad_resid.astype(jnp.bfloat16), "tensor", axis=1, tiled=True),
        lax.all_gather(text_grad_resid.astype(jnp.bfloat16), "tensor", axis=0, tiled=True),
    )
    grad_video_output_weight = jnp.einsum(
        "vfrm,vfrd->md", video_attended, video_resid_full, preferred_element_type=jnp.float32
    )
    grad_text_output_weight = jnp.einsum(
        "sm,sd->md", text_attended, text_resid_full, preferred_element_type=jnp.float32
    )
    video_grad_attended = jnp.einsum(
        "vfrd,md->vfrm", video_resid_full, video_output_weight, preferred_element_type=jnp.float32
    ).astype(jnp.bfloat16)
    video_grad_attended = video_grad_attended.reshape(video_grad_attended.shape[:3] + (-1, HD))
    text_grad_attended = jnp.einsum(
        "sd,md->sm", text_resid_full, text_output_weight, preferred_element_type=jnp.float32
    ).astype(jnp.bfloat16)
    video_weights = jnp.exp(video_scores(video_queries, video_key_rows) - video_logsum)
    video_weights_low = video_weights.astype(jnp.bfloat16)
    video_grad_values = jnp.einsum(
        "vfhrk,vfrhe->vfkhe",
        video_weights_low,
        video_grad_attended,
        preferred_element_type=jnp.float32,
    )
    video_grad_probs = jnp.einsum(
        "vfrhe,vfkhe->vfhrk",
        video_grad_attended,
        video_value_rows,
        preferred_element_type=jnp.float32,
    )
    video_row_dot = jnp.sum(video_weights * video_grad_probs, axis=-1, keepdims=True)
    video_grad_scores = (video_weights * (video_grad_probs - video_row_dot)).astype(jnp.bfloat16)
    video_grad_queries = (
        jnp.einsum(
            "vfhrk,vfkhe->vfrhe",
            video_grad_scores,
            video_key_rows,
            preferred_element_type=jnp.float32,
        )
        * 0.125
    )
    video_grad_keys = (
        jnp.einsum(
            "vfhrk,vfrhe->vfkhe",
            video_grad_scores,
            video_queries,
            preferred_element_type=jnp.float32,
        )
        * 0.125
    )
    video_grad_mixed = jnp.stack([video_grad_queries, video_grad_keys, video_grad_values], axis=3)
    video_grad_mixed = video_grad_mixed.reshape(video_grad_mixed.shape[:4] + (-1,)).astype(
        jnp.bfloat16
    )
    grad_blocks = text_grad_attended.reshape((block_count, block_rows, -1, HD))

    def text_backward_block(carried, operands):
        grad_key_rows, grad_value_rows = carried
        query_block, grad_block, logsum, block_start = operands
        key_start = window_start(block_start)
        key_block = lax.dynamic_slice_in_dim(text_key_rows, key_start, window)
        value_block = lax.dynamic_slice_in_dim(text_value_rows, key_start, window)
        weights = jnp.exp(
            text_scores(query_block, key_block, text_segments, block_start, key_start) - logsum
        )
        value_term = jnp.einsum(
            "hqk,qhe->khe",
            weights.astype(jnp.bfloat16),
            grad_block,
            preferred_element_type=jnp.float32,
        )
        grad_value_rows = lax.dynamic_update_slice_in_dim(
            grad_value_rows,
            lax.dynamic_slice_in_dim(grad_value_rows, key_start, window) + value_term,
            key_start,
            0,
        )
        grad_probs = jnp.einsum(
            "qhe,khe->hqk", grad_block, value_block, preferred_element_type=jnp.float32
        )
        row_dot = jnp.sum(weights * grad_probs, axis=-1, keepdims=True)
        grad_scores = (weights * (grad_probs - row_dot)).astype(jnp.bfloat16)
        grad_query = (
            jnp.einsum("hqk,khe->qhe", grad_scores, key_block, preferred_element_type=jnp.float32)
            * 0.125
        )
        key_term = (
            jnp.einsum("hqk,qhe->khe", grad_scores, query_block, preferred_element_type=jnp.float32)
            * 0.125
        )
        grad_key_rows = lax.dynamic_update_slice_in_dim(
            grad_key_rows,
            lax.dynamic_slice_in_dim(grad_key_rows, key_start, window) + key_term,
            key_start,
            0,
        )
        return ((grad_key_rows, grad_value_rows), grad_query)

    zero_rows = jnp.zeros(text_key_rows.shape, jnp.float32)
    (text_grad_keys, text_grad_values), text_grad_query_blocks = lax.scan(
        text_backward_block,
        (zero_rows, zero_rows),
        (query_blocks, grad_blocks, text_logsums, starts),
    )
    text_grad_queries = text_grad_query_blocks.reshape(text_grad_keys.shape)
    text_grad_mixed = jnp.stack([text_grad_queries, text_grad_keys, text_grad_values], axis=1)
    text_grad_mixed = text_grad_mixed.reshape(text_length, 3, -1).astype(jnp.bfloat16)
    video_mixed_sums = jnp.sum(
        video_grad_mixed.astype(jnp.float32).reshape((-1,) + video_grad_mixed.shape[3:]), axis=0
    )
    grad_video_attend_bias = jnp.stack([video_mixed_sums[0], video_mixed_sums[2]])
    text_mixed_sums = jnp.sum(text_grad_mixed.astype(jnp.float32), axis=0)
    grad_text_attend_bias = jnp.stack([text_mixed_sums[0], text_mixed_sums[2]])
    grad_video_attend_weight = jnp.einsum(
        "vfrd,vfrcm->dcm", video_first_full, video_grad_mixed, preferred_element_type=jnp.float32
    )
    grad_text_attend_weight = jnp.einsum(
        "sd,scm->dcm", text_first_full, text_grad_mixed, preferred_element_type=jnp.float32
    )
    video_grad_first = jnp.einsum(
        "vfrcm,dcm->vfrd", video_grad_mixed, video_attend_weight, preferred_element_type=jnp.float32
    )
    text_grad_first = jnp.einsum(
        "scm,dcm->sd", text_grad_mixed, text_attend_weight, preferred_element_type=jnp.float32
    )
    video_back_first, text_back_first = (
        lax.psum_scatter(
            video_grad_first.astype(jnp.bfloat16), "tensor", scatter_dimension=1, tiled=True
        ).astype(jnp.float32),
        lax.psum_scatter(
            text_grad_first.astype(jnp.bfloat16), "tensor", scatter_dimension=0, tiled=True
        ).astype(jnp.float32),
    )
    video_norm_first, grad_video_first_gain, grad_video_first_shift = norm_backward(
        video_back_first, video_unit_one, video_inverse_one, video_first_gain.astype(jnp.float32)
    )
    text_norm_first, grad_text_first_gain, grad_text_first_shift = norm_backward(
        text_back_first, text_unit_one, text_inverse_one, text_first_gain.astype(jnp.float32)
    )
    video_grad_rows = video_grad_resid + video_norm_first
    text_grad_rows = text_grad_resid + text_norm_first
    token_grad_here = video_grad_rows[:, :, token_count]
    token_grad_all = lax.dynamic_update_slice_in_dim(
        jnp.zeros(message_tokens.shape, jnp.float32), token_grad_here, frame_start, 1
    )
    grad_video_message_out_bias = row_sums(token_grad_all)
    token_low = token_grad_all.astype(jnp.bfloat16)
    grad_video_message_out_weight = jnp.einsum(
        "vfm,vfd->md", message_attended, token_low, preferred_element_type=jnp.float32
    )
    message_grad_attended = jnp.einsum(
        "vfd,md->vfm", token_low, video_message_out_weight, preferred_element_type=jnp.float32
    ).astype(jnp.bfloat16)
    message_grad_attended = message_grad_attended.reshape(
        message_grad_attended.shape[:2] + (-1, HD)
    )
    message_grad_values = jnp.einsum(
        "vhfg,vfhe->vghe",
        message_probs_low,
        message_grad_attended,
        preferred_element_type=jnp.float32,
    )
    message_grad_probs = jnp.einsum(
        "vfhe,vghe->vhfg", message_grad_attended, message_values, preferred_element_type=jnp.float32
    )
    message_row_dot = jnp.sum(message_probs * message_grad_probs, axis=-1, keepdims=True)
    message_grad_scores = (message_probs * (message_grad_probs - message_row_dot)).astype(
        jnp.bfloat16
    )
    message_grad_queries = (
        jnp.einsum(
            "vhfg,vghe->vfhe", message_grad_scores, message_keys, preferred_element_type=jnp.float32
        )
        * 0.125
    )
    message_grad_keys = (
        jnp.einsum(
            "vhfg,vfhe->vghe",
            message_grad_scores,
            message_queries,
            preferred_element_type=jnp.float32,
        )
        * 0.125
    )
    message_grad_mixed = jnp.stack(
        [message_grad_queries, message_grad_keys, message_grad_values], axis=2
    )
    message_grad_mixed = message_grad_mixed.reshape(message_grad_mixed.shape[:3] + (-1,)).astype(
        jnp.bfloat16
    )
    message_mixed_sums = jnp.sum(
        message_grad_mixed.astype(jnp.float32).reshape((-1,) + message_grad_mixed.shape[2:]), axis=0
    )
    grad_video_message_attend_bias = jnp.stack([message_mixed_sums[0], message_mixed_sums[2]])
    grad_video_message_attend_weight = jnp.einsum(
        "vfd,vfcm->dcm", message_normed_low, message_grad_mixed, preferred_element_type=jnp.float32
    )
    message_grad_normed = jnp.einsum(
        "vfcm,dcm->vfd",
        message_grad_mixed,
        video_message_attend_weight,
        preferred_element_type=jnp.float32,
    )
    message_norm_grad, grad_video_message_gain, grad_video_message_shift = norm_backward(
        message_grad_normed, message_unit, message_inverse, message_gain_row
    )
    grad_message_here = lax.psum_scatter(
        token_grad_all + message_norm_grad, "tensor", scatter_dimension=1, tiled=True
    )
    grad_video_message_bias = row_sums(grad_message_here)
    message_low = grad_message_here.astype(jnp.bfloat16)
    grad_video_message_weight = jnp.einsum(
        "vfd,vfe->de", class_rows, message_low, preferred_element_type=jnp.float32
    )
    class_grad = jnp.einsum(
        "vfe,de->vfd", message_low, video_message_weight, preferred_element_type=jnp.float32
    )
    video_input_grad = (
        video_grad_rows[:, :, :token_count].at[:, :, 0].add(class_grad).astype(jnp.bfloat16)
    )
    text_input_grad = text_grad_rows.astype(jnp.bfloat16)
    (
        grad_video_attend_weight,
        grad_video_output_weight,
        grad_video_expand_weight,
        grad_video_reduce_weight,
        grad_text_attend_weight,
        grad_text_output_weight,
        grad_text_expand_weight,
        grad_text_reduce_weight,
    ) = reduce_low(
        (
            grad_video_attend_weight,
            grad_video_output_weight,
            grad_video_expand_weight,
            grad_video_reduce_weight,
            grad_text_attend_weight,
            grad_text_output_weight,
            grad_text_expand_weight,
            grad_text_reduce_weight,
        ),
        "dp",
    )
    (
        grad_video_message_weight,
        grad_video_message_attend_weight,
        grad_video_message_out_weight,
    ) = reduce_low(
        (
            grad_video_message_weight,
            grad_video_message_attend_weight,
            grad_video_message_out_weight,
        ),
        ("dp", "tensor"),
    )
    (
        grad_video_attend_bias,
        grad_video_expand_bias,
        grad_text_attend_bias,
        grad_text_expand_bias,
    ) = reduce_packed(
        (
            grad_video_attend_bias,
            grad_video_expand_bias,
            grad_text_attend_bias,
            grad_text_expand_bias,
        ),
        "dp",
    )
    (
        grad_video_first_gain,
        grad_video_first_shift,
        grad_video_message_bias,
        grad_video_message_gain,
        grad_video_message_shift,
        grad_video_message_attend_bias,
        grad_video_message_out_bias,
        grad_video_output_bias,
        grad_video_final_gain,
        grad_video_final_shift,
        grad_video_reduce_bias,
        grad_text_first_gain,
        grad_text_first_shift,
        grad_text_output_bias,
        grad_text_final_gain,
        grad_text_final_shift,
        grad_text_reduce_bias,
    ) = reduce_packed(
        (
            grad_video_first_gain,
            grad_video_first_shift,
            grad_video_message_bias,
            grad_video_message_gain,
            grad_video_message_shift,
            grad_video_message_attend_bias,
            grad_video_message_out_bias,
            grad_video_output_bias,
            grad_video_final_gain,
            grad_video_final_shift,
            grad_video_reduce_bias,
            grad_text_first_gain,
            grad_text_first_shift,
            grad_text_output_bias,
            grad_text_final_gain,
            grad_text_final_shift,
            grad_text_reduce_bias,
        ),
        ("dp", "tensor"),
    )
    return (
        video_output,
        message_output,
        text_output,
        video_input_grad,
        text_input_grad,
        grad_video_first_gain,
        grad_video_first_shift,
        grad_video_message_weight,
        grad_video_message_bias,
        grad_video_message_gain,
        grad_video_message_shift,
        grad_video_message_attend_weight,
        grad_video_message_attend_bias,
        grad_video_message_out_weight,
        grad_video_message_out_bias,
        grad_video_attend_weight,
        grad_video_attend_bias,
        grad_video_output_weight,
        grad_video_output_bias,
        grad_video_final_gain,
        grad_video_final_shift,
        grad_video_expand_weight,
        grad_video_expand_bias,
        grad_video_reduce_weight,
        grad_video_reduce_bias,
        grad_text_first_gain,
        grad_text_first_shift,
        grad_text_attend_weight,
        grad_text_attend_bias,
        grad_text_output_weight,
        grad_text_output_bias,
        grad_text_final_gain,
        grad_text_final_shift,
        grad_text_expand_weight,
        grad_text_expand_bias,
        grad_text_reduce_weight,
        grad_text_reduce_bias,
    )


def solution(mesh):
    in_specs = (
        P("dp", "tensor", None, None),
        P(("dp", "tensor"), None),
        P("dp", None),
        P(),
        P(),
        P(),
        P(),
        P(),
        P(),
        P(),
        P(),
        P(),
        P(),
        P(None, None, "tensor"),
        P(None, "tensor"),
        P("tensor", None),
        P(),
        P(),
        P(),
        P(None, "tensor"),
        P("tensor"),
        P("tensor", None),
        P(),
        P(),
        P(),
        P(None, None, "tensor"),
        P(None, "tensor"),
        P("tensor", None),
        P(),
        P(),
        P(),
        P(None, "tensor"),
        P("tensor"),
        P("tensor", None),
        P(),
        P("dp", "tensor", None, None),
        P("dp", "tensor", None),
        P(("dp", "tensor"), None),
    )
    out_specs = (
        P("dp", "tensor", None, None),
        P("dp", "tensor", None),
        P(("dp", "tensor"), None),
        P("dp", "tensor", None, None),
        P(("dp", "tensor"), None),
        P(),
        P(),
        P(),
        P(),
        P(),
        P(),
        P(),
        P(),
        P(),
        P(),
        P(None, None, "tensor"),
        P(None, "tensor"),
        P("tensor", None),
        P(),
        P(),
        P(),
        P(None, "tensor"),
        P("tensor"),
        P("tensor", None),
        P(),
        P(),
        P(),
        P(None, None, "tensor"),
        P(None, "tensor"),
        P("tensor", None),
        P(),
        P(),
        P(),
        P(None, "tensor"),
        P("tensor"),
        P("tensor", None),
        P(),
    )
    return jax.shard_map(
        on_device, mesh=mesh, in_specs=in_specs, out_specs=out_specs, check_vma=False
    )
```

```python
import functools
import jax
import jax.numpy as jnp
from jax import lax
from jax.experimental import pallas as pl
from jax.experimental.pallas import tpu as pltpu
from jax.sharding import PartitionSpec as P

HD = 64
MAXLEN = 77
LANES = 128
NEGATIVE = -1000000000.0
F32 = jnp.float32
BF16 = jnp.bfloat16
PARAMS = pltpu.CompilerParams(vmem_limit_bytes=60 << 20)


def nt(left, right):
    return lax.dot_general(left, right, (((1,), (1,)), ((), ())), preferred_element_type=F32)


def tn(left, right):
    return lax.dot_general(left, right, (((0,), (0,)), ((), ())), preferred_element_type=F32)


def mm(left, right):
    return jnp.dot(left, right, preferred_element_type=F32)


def unit_of(rows):
    centre = rows - jnp.mean(rows, axis=-1, keepdims=True)
    inverse = lax.rsqrt(jnp.mean(centre * centre, axis=-1, keepdims=True) + 1e-05)
    return centre * inverse, inverse


def norm_back(grad_out, unit_rows, inverse, gain_row):
    scaled = grad_out * gain_row
    return inverse * (
        scaled
        - jnp.mean(scaled, axis=-1, keepdims=True)
        - unit_rows * jnp.mean(scaled * unit_rows, axis=-1, keepdims=True)
    )


def column_sum(values):
    return jnp.sum(values, axis=0, keepdims=True)


def row_is(shape, row):
    return lax.broadcasted_iota(jnp.int32, shape, 0) == row


def low_half():
    return lax.broadcasted_iota(jnp.int32, (1, LANES), 1) < HD


def head_masks():
    first = low_half().astype(F32)
    return first.astype(BF16), (1.0 - first).astype(BF16)


def whole(array):
    return pl.BlockSpec(array.shape, lambda *_: (0,) * array.ndim)


def rows_block(rows, columns, offset=0):
    return pl.BlockSpec((rows, columns), lambda i: (i + offset, 0))


def cost(flops, arrays, outs):
    moved = sum(a.size * a.dtype.itemsize for a in arrays) + sum(
        a.size * jnp.dtype(a.dtype).itemsize for a in outs
    )
    return pl.CostEstimate(flops=int(flops), transcendentals=0, bytes_accessed=int(moved))


def call(body, grid, ins, in_specs, outs, out_specs, scratch=(), flops=0, name=None):
    return pl.pallas_call(
        body,
        grid=grid,
        in_specs=in_specs,
        out_specs=out_specs,
        out_shape=outs,
        scratch_shapes=list(scratch),
        compiler_params=PARAMS,
        cost_estimate=cost(flops, ins, outs),
        name=name,
    )(*ins)


def shape_of(shape, dtype):
    return jax.ShapeDtypeStruct(shape, dtype)


def video_first(frames_rows, tokens, gain, shift, token_row):
    frames, rows, width = frames_rows.shape

    def body(x_ref, token_ref, gain_ref, shift_ref, rows_ref, first_ref):
        x = x_ref[0].astype(F32)
        x = jnp.where(row_is(x.shape, token_row), token_ref[0], x)
        rows_ref[...] = x
        unit, _ = unit_of(x)
        first_ref[...] = (unit * gain_ref[...] + shift_ref[...]).astype(BF16)

    ins = (frames_rows, tokens, gain, shift)
    return call(
        body,
        (frames,),
        ins,
        [
            pl.BlockSpec((1, rows, width), lambda i: (i, 0, 0)),
            pl.BlockSpec((1, 1, width), lambda i: (i, 0, 0)),
            whole(gain),
            whole(shift),
        ],
        [shape_of((frames * rows, width), F32), shape_of((frames * rows, width), BF16)],
        [rows_block(rows, width), rows_block(rows, width)],
        name="video_first",
    )


def text_first(rows_in, gain, shift, block):
    rows, width = rows_in.shape

    def body(x_ref, gain_ref, shift_ref, first_ref):
        unit, _ = unit_of(x_ref[...].astype(F32))
        first_ref[...] = (unit * gain_ref[...] + shift_ref[...]).astype(BF16)

    ins = (rows_in, gain, shift)
    return call(
        body,
        (rows // block,),
        ins,
        [rows_block(block, width), whole(gain), whole(shift)],
        [shape_of((rows, width), BF16)],
        [rows_block(block, width)],
        name="text_first",
    )[0]


def masked(scores, plan, group, segments):
    if plan["keys"] is not None:
        columns = lax.broadcasted_iota(jnp.int32, scores.shape, 1)
        return jnp.where(columns < plan["keys"], scores, NEGATIVE)
    query_start, queries, key_start, keys, _ = group
    column_ref, row_ref = segments
    same = (
        column_ref[query_start : query_start + queries, :]
        == row_ref[:, key_start : key_start + keys]
    )
    columns = lax.broadcasted_iota(jnp.int32, scores.shape, 1) + key_start
    positions = lax.broadcasted_iota(jnp.int32, scores.shape, 0) + query_start
    return jnp.where(same & (columns <= positions), scores, NEGATIVE)


def attention_forward(first, weight, bias, plan, segments, name):
    rows, width = first.shape
    heads_width = weight.shape[2]
    steps = heads_width // LANES
    out_rows = plan["out_rows"]

    def body(x_ref, w_ref, b_ref, *rest):
        segment_refs, (mixed_ref, out_ref, lse_ref, wide_ref) = rest[:-4], rest[-4:]
        for part in range(3):
            wide_ref[:, part * LANES : (part + 1) * LANES] = w_ref[part]
        mixed = mm(x_ref[...], wide_ref[...])
        for part in range(3):
            mixed_ref[part] = (
                mixed[:, part * LANES : (part + 1) * LANES] + b_ref[part : part + 1, :]
            ).astype(BF16)
        masks = head_masks()
        lower = low_half()
        for group in plan["groups"]:
            query_start, queries, key_start, keys, out_start = group
            q = mixed_ref[0, query_start : query_start + queries, :] * jnp.asarray(0.125, BF16)
            k = mixed_ref[1, key_start : key_start + keys, :]
            v = mixed_ref[2, key_start : key_start + keys, :]
            outs, sums = [], []
            for mask in masks:
                scores = masked(nt(q * mask, k), plan, group, segment_refs)
                top = jnp.max(scores, axis=-1, keepdims=True)
                powers = jnp.exp(scores - top)
                total = jnp.sum(powers, axis=-1, keepdims=True)
                probs = (powers * (1.0 / total)).astype(BF16)
                outs.append(mm(probs, v))
                sums.append(top + jnp.log(total))
            out_ref[out_start : out_start + queries, :] = jnp.where(lower, outs[0], outs[1]).astype(
                BF16
            )
            lse_ref[out_start : out_start + queries, :] = jnp.where(lower, sums[0], sums[1])

    ins = (first, weight, bias) + segments
    return call(
        body,
        (steps,),
        ins,
        [
            whole(first),
            pl.BlockSpec((3, width, LANES), lambda i: (0, 0, i)),
            pl.BlockSpec((3, LANES), lambda i: (0, i)),
        ]
        + [whole(s) for s in segments],
        [
            shape_of((3, rows, heads_width), BF16),
            shape_of((out_rows, heads_width), BF16),
            shape_of((out_rows, heads_width), F32),
        ],
        [
            pl.BlockSpec((3, rows, LANES), lambda i: (0, 0, i)),
            pl.BlockSpec((out_rows, LANES), lambda i: (0, i)),
            pl.BlockSpec((out_rows, LANES), lambda i: (0, i)),
        ],
        scratch=[pltpu.VMEM((width, 3 * LANES), BF16)],
        flops=2 * rows * width * 3 * heads_width * 2,
        name=name,
    )


def attention_backward(
    low, out_weight, attended, first, weight, mixed, lse, plan, segments, name
):
    rows, width = first.shape
    out_rows = plan["out_rows"]
    heads_width = weight.shape[2]
    steps = heads_width // LANES
    shared = plan["keys"] is None

    def body(low_ref, ow_ref, att_ref, x_ref, w_ref, mixed_ref, lse_ref, *rest):
        segment_refs = rest[: len(segments)]
        (
            out_grad_ref,
            weight_grad_ref,
            bias_ref,
            first_grad_ref,
            wide_ref,
            turned_ref,
            grad_ref,
            key_ref,
            value_ref,
        ) = rest[len(segments) :]
        step = pl.program_id(0)

        @pl.when(step == 0)
        def _():
            turned_ref[...] = x_ref[...].T
            first_grad_ref[...] = jnp.zeros_like(first_grad_ref)

        for part in range(3):
            wide_ref[:, part * LANES : (part + 1) * LANES] = w_ref[part]
        low_rows = low_ref[...]
        grad_out = nt(low_rows, ow_ref[...]).astype(BF16)
        out_grad_ref[...] = tn(att_ref[...], low_rows).astype(BF16)
        if shared:
            grad_ref[...] = jnp.zeros_like(grad_ref)
            key_ref[...] = jnp.zeros_like(key_ref)
            value_ref[...] = jnp.zeros_like(value_ref)
        masks = head_masks()
        lower = low_half()
        for group in plan["groups"]:
            query_start, queries, key_start, keys, out_start = group
            q = mixed_ref[0, query_start : query_start + queries, :] * jnp.asarray(0.125, BF16)
            k = mixed_ref[1, key_start : key_start + keys, :]
            v = mixed_ref[2, key_start : key_start + keys, :]
            g = grad_out[out_start : out_start + queries, :]
            query_grads, key_grad, value_grad = [], None, None
            for head, mask in enumerate(masks):
                query_head, grad_head = q * mask, g * mask
                scores = masked(nt(query_head, k), plan, group, segment_refs)
                column = lse_ref[out_start : out_start + queries, head * HD : head * HD + 1]
                probs = jnp.exp(scores - column)
                grad_probs = nt(grad_head, v)
                dots = jnp.sum(probs * grad_probs, axis=-1, keepdims=True)
                grad_scores = (probs * (grad_probs - dots)).astype(BF16)
                query_grads.append(mm(grad_scores, k))
                key_term = tn(grad_scores, query_head)
                value_term = tn(probs.astype(BF16), grad_head)
                key_grad = key_term if key_grad is None else key_grad + key_term
                value_grad = value_term if value_grad is None else value_grad + value_term
            query_grad = jnp.where(lower, query_grads[0], query_grads[1]) * 0.125
            grad_ref[query_start : query_start + queries, :LANES] = query_grad.astype(BF16)
            span = slice(key_start, key_start + keys)
            if shared:
                key_ref[span, :] += key_grad
                value_ref[span, :] += value_grad
            else:
                grad_ref[span, LANES : 2 * LANES] = key_grad.astype(BF16)
                grad_ref[span, 2 * LANES :] = value_grad.astype(BF16)
        if shared:
            grad_ref[:, LANES : 2 * LANES] = key_ref[...].astype(BF16)
            grad_ref[:, 2 * LANES :] = value_ref[...].astype(BF16)
        grads = grad_ref[...]
        weight_grads = mm(turned_ref[...], grads)
        sums = column_sum(grads.astype(F32))
        for part in range(3):
            weight_grad_ref[part] = weight_grads[:, part * LANES : (part + 1) * LANES].astype(BF16)
        bias_ref[0:1, :] = sums[:, :LANES]
        bias_ref[1:2, :] = sums[:, 2 * LANES :]
        first_grad_ref[...] += nt(grads, wide_ref[...])

    ins = (low, out_weight, attended, first, weight, mixed, lse) + segments
    return call(
        body,
        (steps,),
        ins,
        [
            whole(low),
            pl.BlockSpec((LANES, width), lambda i: (i, 0)),
            pl.BlockSpec((out_rows, LANES), lambda i: (0, i)),
            whole(first),
            pl.BlockSpec((3, width, LANES), lambda i: (0, 0, i)),
            pl.BlockSpec((3, rows, LANES), lambda i: (0, 0, i)),
            pl.BlockSpec((out_rows, LANES), lambda i: (0, i)),
        ]
        + [whole(s) for s in segments],
        [
            shape_of((heads_width, width), BF16),
            shape_of((3, width, heads_width), BF16),
            shape_of((2, heads_width), F32),
            shape_of((rows, width), F32),
        ],
        [
            pl.BlockSpec((LANES, width), lambda i: (i, 0)),
            pl.BlockSpec((3, width, LANES), lambda i: (0, 0, i)),
            pl.BlockSpec((2, LANES), lambda i: (0, i)),
            pl.BlockSpec((rows, width), lambda i: (0, 0)),
        ],
        scratch=[
            pltpu.VMEM((width, 3 * LANES), BF16),
            pltpu.VMEM((width, rows), BF16),
            pltpu.VMEM((rows, 3 * LANES), BF16),
            pltpu.VMEM((rows, LANES), F32),
            pltpu.VMEM((rows, LANES), F32),
        ],
        flops=2 * rows * width * 8 * heads_width * 2,
        name=name,
    )


def project_norm(parts, weights, rows_in, bias, gain, shift, block, offset, name):
    out_rows, half = parts[0].shape
    width = bias.shape[1]

    def body(a_ref, b_ref, wa_ref, wb_ref, rows_ref, bias_ref, gain_ref, shift_ref, res_ref, out_ref):
        resid = (
            rows_ref[...].astype(F32)
            + mm(a_ref[...], wa_ref[...])
            + mm(b_ref[...], wb_ref[...])
            + bias_ref[...]
        )
        res_ref[...] = resid
        unit, _ = unit_of(resid)
        out_ref[...] = (unit * gain_ref[...] + shift_ref[...]).astype(BF16)

    ins = (*parts, *weights, rows_in, bias, gain, shift)
    return call(
        body,
        (out_rows // block,),
        ins,
        [
            rows_block(block, half),
            rows_block(block, half),
            whole(weights[0]),
            whole(weights[1]),
            rows_block(block, width, offset),
            whole(bias),
            whole(gain),
            whole(shift),
        ],
        [shape_of((out_rows, width), F32), shape_of((out_rows, width), BF16)],
        [rows_block(block, width), rows_block(block, width)],
        flops=4 * out_rows * half * width,
        name=name,
    )


def feed_forward(second, cot, expand, expand_bias, reduce, chunk, name):
    rows, width = second.shape
    units = expand.shape[1]

    def body(x_ref, cot_ref, e_ref, b_ref, r_ref, *rest):
        ge_ref, gr_ref, gb_ref, out_ref, back_ref, turned_ref = rest

        @pl.when(pl.program_id(0) == 0)
        def _():
            turned_ref[...] = x_ref[...].T
            out_ref[...] = jnp.zeros_like(out_ref)
            back_ref[...] = jnp.zeros_like(back_ref)

        cot_rows = cot_ref[...]
        hidden = mm(x_ref[...], e_ref[...]) + b_ref[...]
        grad_active = nt(cot_rows, r_ref[...])
        logistic = 1.0 / (1.0 + jnp.exp(-1.702 * hidden))
        active = (hidden * logistic).astype(BF16)
        slope = logistic + 1.702 * hidden * logistic * (1.0 - logistic)
        grad_hidden = grad_active * slope
        grad_low = grad_hidden.astype(BF16)
        gb_ref[...] = column_sum(grad_low.astype(F32))
        out_ref[...] += mm(active, r_ref[...])
        back_ref[...] += nt(grad_low, e_ref[...])
        gr_ref[...] = tn(active, cot_rows).astype(BF16)
        ge_ref[...] = mm(turned_ref[...], grad_low).astype(BF16)

    ins = (second, cot, expand, expand_bias, reduce)
    return call(
        body,
        (units // chunk,),
        ins,
        [
            whole(second),
            whole(cot),
            pl.BlockSpec((width, chunk), lambda i: (0, i)),
            pl.BlockSpec((1, chunk), lambda i: (0, i)),
            pl.BlockSpec((chunk, width), lambda i: (i, 0)),
        ],
        [
            shape_of((width, units), BF16),
            shape_of((units, width), BF16),
            shape_of((1, units), F32),
            shape_of((rows, width), F32),
            shape_of((rows, width), F32),
        ],
        [
            pl.BlockSpec((width, chunk), lambda i: (0, i)),
            pl.BlockSpec((chunk, width), lambda i: (i, 0)),
            pl.BlockSpec((1, chunk), lambda i: (0, i)),
            pl.BlockSpec((rows, width), lambda i: (0, 0)),
            pl.BlockSpec((rows, width), lambda i: (0, 0)),
        ],
        scratch=[pltpu.VMEM((width, rows), BF16)],
        flops=12 * rows * width * units,
        name=name,
    )


def resid_back(resid, outs, backs, cot, token_grads, gain, reduce_bias, block, token_row, name):
    rows, width = resid.shape

    def body(res_ref, oa_ref, ob_ref, ba_ref, bb_ref, cot_ref, *rest):
        if token_row is None:
            gain_ref, rb_ref, final_ref, grad_ref, low_ref, sums_ref = rest
        else:
            token_ref, gain_ref, rb_ref, final_ref, grad_ref, low_ref, sums_ref = rest

        @pl.when(pl.program_id(0) == 0)
        def _():
            sums_ref[...] = jnp.zeros_like(sums_ref)

        resid_rows = res_ref[...]
        final_ref[...] = (resid_rows + oa_ref[...] + ob_ref[...] + rb_ref[...]).astype(BF16)
        back = ba_ref[...] + bb_ref[...]
        unit, inverse = unit_of(resid_rows)
        cot_rows = cot_ref[...].astype(F32)
        sums_ref[0:1, :] += column_sum(cot_rows)
        sums_ref[1:2, :] += column_sum(back * unit)
        sums_ref[2:3, :] += column_sum(back)
        if token_row is not None:
            cot_rows = jnp.where(row_is(cot_rows.shape, token_row), token_ref[0], cot_rows)
        grad = cot_rows + norm_back(back, unit, inverse, gain_ref[...])
        sums_ref[3:4, :] += column_sum(grad)
        grad_ref[...] = grad
        low_ref[...] = grad.astype(BF16)

    ins = (resid, *outs, *backs, cot)
    specs = [rows_block(block, width)] * 6
    if token_row is not None:
        ins += (token_grads,)
        specs.append(pl.BlockSpec((1, 1, width), lambda i: (i, 0, 0)))
    ins += (gain, reduce_bias)
    specs += [whole(gain), whole(reduce_bias)]
    return call(
        body,
        (rows // block,),
        ins,
        specs,
        [
            shape_of((rows, width), BF16),
            shape_of((rows, width), F32),
            shape_of((rows, width), BF16),
            shape_of((4, width), F32),
        ],
        [rows_block(block, width)] * 3 + [pl.BlockSpec((4, width), lambda i: (0, 0))],
        name=name,
    )


def video_rows_back(rows_in, firsts, grad_resid, gain, block, token_row):
    rows, width = rows_in.shape
    frames = rows // block

    def body(rows_ref, fa_ref, fb_ref, grad_ref, gain_ref, out_ref, edge_ref, sums_ref):
        @pl.when(pl.program_id(0) == 0)
        def _():
            sums_ref[...] = jnp.zeros_like(sums_ref)

        unit, inverse = unit_of(rows_ref[...])
        back = fa_ref[...] + fb_ref[...]
        sums_ref[0:1, :] += column_sum(back * unit)
        sums_ref[1:2, :] += column_sum(back)
        grad = grad_ref[...] + norm_back(back, unit, inverse, gain_ref[...])
        out_ref[...] = grad.astype(BF16)
        edge_ref[0, 0:1, :] = grad[0:1, :]
        edge_ref[0, 1:2, :] = grad[token_row : token_row + 1, :]

    ins = (rows_in, *firsts, grad_resid, gain)
    return call(
        body,
        (frames,),
        ins,
        [rows_block(block, width)] * 4 + [whole(gain)],
        [
            shape_of((rows, width), BF16),
            shape_of((frames, 2, width), F32),
            shape_of((2, width), F32),
        ],
        [
            rows_block(block, width),
            pl.BlockSpec((1, 2, width), lambda i: (i, 0, 0)),
            pl.BlockSpec((2, width), lambda i: (0, 0)),
        ],
        name="video_rows_back",
    )


def text_rows_back(rows_in, firsts, grad_resid, gain, block):
    rows, width = rows_in.shape
    ahead = (rows - grad_resid.shape[0]) // block

    def body(rows_ref, fa_ref, fb_ref, grad_ref, gain_ref, out_ref, sums_ref):
        step = pl.program_id(0)

        @pl.when(step == 0)
        def _():
            sums_ref[...] = jnp.zeros_like(sums_ref)

        unit, inverse = unit_of(rows_ref[...].astype(F32))
        back = fa_ref[...] + fb_ref[...]
        sums_ref[0:1, :] += column_sum(back * unit)
        sums_ref[1:2, :] += column_sum(back)
        own = jnp.where(step >= ahead, 1.0, 0.0)
        out_ref[...] = grad_ref[...] * own + norm_back(back, unit, inverse, gain_ref[...])

    ins = (rows_in, *firsts, grad_resid, gain)
    return call(
        body,
        (rows // block,),
        ins,
        [rows_block(block, width)] * 3
        + [
            pl.BlockSpec((block, width), lambda i: (jnp.maximum(i - ahead, 0), 0)),
            whole(gain),
        ],
        [shape_of((rows, width), F32), shape_of((2, width), F32)],
        [rows_block(block, width), pl.BlockSpec((2, width), lambda i: (0, 0))],
        name="text_rows_back",
    )


def head_rows(values, heads):
    lanes = lax.broadcasted_iota(jnp.int32, values.shape, 1) // HD
    return jnp.concatenate(
        [jnp.where(lanes == head, values, 0.0) for head in range(heads)], axis=0
    ).astype(BF16)


def fold_heads(values, heads, rows):
    lanes = lax.broadcasted_iota(jnp.int32, (rows, values.shape[1]), 1) // HD
    total = jnp.zeros((rows, values.shape[1]), F32)
    for head in range(heads):
        total = total + jnp.where(lanes == head, values[head * rows : (head + 1) * rows], 0.0)
    return total


def message_probs(mixed_ref, heads):
    query_rows = head_rows(mixed_ref[0].astype(F32) * 0.125, heads)
    scores = nt(query_rows, mixed_ref[1])
    top = jnp.max(scores, axis=-1, keepdims=True)
    powers = jnp.exp(scores - top)
    return query_rows, powers * (1.0 / jnp.sum(powers, axis=-1, keepdims=True))


def messages_forward(messages, gain, shift, weight, bias, out_weight, out_bias):
    rows, width = messages.shape
    heads = width // HD

    def body(m_ref, gain_ref, shift_ref, w_ref, b_ref, ow_ref, ob_ref, n_ref, mixed_ref, a_ref, t_ref):
        messages_now = m_ref[...]
        unit, _ = unit_of(messages_now)
        normed = (unit * gain_ref[...] + shift_ref[...]).astype(BF16)
        n_ref[...] = normed
        for part in range(3):
            mixed_ref[part] = (mm(normed, w_ref[part]) + b_ref[part : part + 1, :]).astype(BF16)
        _, probs = message_probs(mixed_ref, heads)
        attended = fold_heads(mm(probs.astype(BF16), mixed_ref[2]), heads, rows).astype(BF16)
        a_ref[...] = attended
        t_ref[...] = messages_now + mm(attended, ow_ref[...]) + ob_ref[...]

    ins = (messages, gain, shift, weight, bias, out_weight, out_bias)
    outs = [
        shape_of((rows, width), BF16),
        shape_of((3, rows, width), BF16),
        shape_of((rows, width), BF16),
        shape_of((rows, width), F32),
    ]
    return call(
        body, (1,), ins, [whole(a) for a in ins], outs, [whole(o) for o in outs], name="messages"
    )


def messages_backward(messages, mixed, token_grads, gain, weight, out_weight, in_weight):
    rows, width = messages.shape
    heads = width // HD

    def body(m_ref, mixed_ref, t_ref, gain_ref, w_ref, ow_ref, iw_ref, g_ref, low_ref, c_ref, s_ref):
        token = t_ref[...]
        grad_attended = nt(token.astype(BF16), ow_ref[...]).astype(BF16)
        query_rows, probs = message_probs(mixed_ref, heads)
        grad_rows = head_rows(grad_attended.astype(F32), heads)
        grad_probs = nt(grad_rows, mixed_ref[2])
        dots = jnp.sum(probs * grad_probs, axis=-1, keepdims=True)
        grad_scores = (probs * (grad_probs - dots)).astype(BF16)
        grads = (
            fold_heads(mm(grad_scores, mixed_ref[1]), heads, rows) * 0.125,
            tn(grad_scores, query_rows),
            tn(probs.astype(BF16), grad_rows),
        )
        normed_grad = jnp.zeros((rows, width), F32)
        for part in range(3):
            low = grads[part].astype(BF16)
            g_ref[part] = low
            normed_grad = normed_grad + nt(low, w_ref[part])
        s_ref[0:1, :] = column_sum(g_ref[0].astype(F32))
        s_ref[1:2, :] = column_sum(g_ref[2].astype(F32))
        unit, inverse = unit_of(m_ref[...])
        s_ref[2:3, :] = column_sum(normed_grad * unit)
        s_ref[3:4, :] = column_sum(normed_grad)
        grad = token + norm_back(normed_grad, unit, inverse, gain_ref[...])
        s_ref[4:5, :] = column_sum(grad)
        s_ref[5:6, :] = column_sum(token)
        low = grad.astype(BF16)
        low_ref[...] = low
        c_ref[...] = nt(low, iw_ref[...])

    ins = (messages, mixed, token_grads, gain, weight, out_weight, in_weight)
    outs = [
        shape_of((3, rows, width), BF16),
        shape_of((rows, width), BF16),
        shape_of((rows, width), F32),
        shape_of((6, width), F32),
    ]
    return call(
        body,
        (1,),
        ins,
        [whole(a) for a in ins],
        outs,
        [whole(o) for o in outs],
        name="messages_back",
    )


def swap(value):
    return lax.ppermute(value, "tensor", [(0, 1), (1, 0)])


def in_order(own, other, axis=0):
    first = lax.axis_index("tensor") == 0
    return jnp.where(
        first, jnp.concatenate([own, other], axis), jnp.concatenate([other, own], axis)
    )


def own_part(values, size, axis=0):
    return lax.dynamic_slice_in_dim(values, lax.axis_index("tensor") * size, size, axis)


def row_of(vector):
    return vector.astype(F32).reshape(1, -1)


def qkv_bias(flat):
    rows = flat.astype(F32).reshape(2, -1)
    return jnp.stack([rows[0], jnp.zeros_like(rows[0]), rows[1]])


def reduce_bucket(own, other):
    received = [swap(value) for value in other]
    sums = [
        (mine.astype(F32) + theirs.astype(F32)).astype(BF16) for mine, theirs in zip(own, received)
    ]
    return [value.astype(F32) for value in lax.psum(tuple(sums), "dp")]


def on_device(
    video_input,
    text_input,
    caption_lengths,
    video_first_gain,
    video_first_shift,
    video_message_weight,
    video_message_bias,
    video_message_gain,
    video_message_shift,
    video_message_attend_weight,
    video_message_attend_bias,
    video_message_out_weight,
    video_message_out_bias,
    video_attend_weight,
    video_attend_bias,
    video_output_weight,
    video_output_bias,
    video_final_gain,
    video_final_shift,
    video_expand_weight,
    video_expand_bias,
    video_reduce_weight,
    video_reduce_bias,
    text_first_gain,
    text_first_shift,
    text_attend_weight,
    text_attend_bias,
    text_output_weight,
    text_output_bias,
    text_final_gain,
    text_final_shift,
    text_expand_weight,
    text_expand_bias,
    text_reduce_weight,
    text_reduce_bias,
    video_out_grad,
    message_out_grad,
    text_out_grad,
):
    core = lax.axis_index("tensor")
    frames, tokens, width = video_input.shape[1:]
    frame_rows = -(-(tokens + 1) // 16) * 16
    spare = ((0, 0), (0, frame_rows - tokens), (0, 0))
    text_count, text_width = text_input.shape
    halo = -(-(MAXLEN - 1) // LANES) * LANES

    class_rows = video_input[0, :, 0, :]
    messages_here = (
        jnp.dot(class_rows, video_message_weight, preferred_element_type=F32)
        + video_message_bias.astype(F32)
    )
    messages_there = swap(messages_here)
    text_qkv = (text_attend_weight.transpose(1, 0, 2),)
    video_qkv = (video_attend_weight.transpose(1, 0, 2),)
    small = (video_attend_bias, video_expand_bias, text_attend_bias, text_expand_bias)
    packed = jnp.concatenate([value.reshape(-1) for value in small])
    packed_there = swap(packed)
    biases = []
    begin = 0
    for value in small:
        biases.append((packed[begin : begin + value.size], packed_there[begin : begin + value.size]))
        begin += value.size
    text_ahead = lax.ppermute(text_input[text_count - halo :], "tensor", [(0, 1)])
    text_qkv += (swap(text_qkv[0]),)
    video_qkv += (swap(video_qkv[0]),)
    text_out = (text_output_weight, swap(text_output_weight))
    video_out = (video_output_weight, swap(video_output_weight))
    video_expand = (video_expand_weight, swap(video_expand_weight))
    video_reduce = (video_reduce_weight, swap(video_reduce_weight))
    text_expand = (text_expand_weight, swap(text_expand_weight))
    text_reduce = (text_reduce_weight, swap(text_reduce_weight))
    video_qkv_bias = [qkv_bias(flat) for flat in biases[0]]
    text_qkv_bias = [qkv_bias(flat) for flat in biases[2]]
    sides = (0, 1)

    text_rows = jnp.concatenate([text_ahead, text_input])
    rows_all = text_count + halo
    caption_ends = jnp.cumsum(caption_lengths[0])
    positions = core * text_count - halo + jnp.arange(rows_all, dtype=jnp.int32)
    segment = jnp.sum((positions[:, None] >= caption_ends[None, :]).astype(jnp.int32), axis=1)
    segment = jnp.where(positions < 0, -1, segment)
    segments = (segment.reshape(-1, 1), segment.reshape(1, -1))
    text_plan = {
        "groups": [
            (halo + start, LANES, start, halo + LANES, start)
            for start in range(0, text_count, LANES)
        ],
        "keys": None,
        "out_rows": text_count,
    }
    text_gain, text_gain_two = row_of(text_first_gain), row_of(text_final_gain)
    text_normed = text_first(text_rows, text_gain, row_of(text_first_shift), LANES)
    text_attention = [
        attention_forward(
            text_normed, text_qkv[side], text_qkv_bias[side], text_plan, segments, "text_attention"
        )
        for side in sides
    ]
    text_resid, text_second = project_norm(
        [text_attention[side][1] for side in sides],
        text_out,
        text_rows,
        row_of(text_output_bias),
        text_gain_two,
        row_of(text_final_shift),
        LANES,
        halo // LANES,
        "text_project",
    )

    messages = in_order(messages_here, messages_there)
    message_weight = video_message_attend_weight.transpose(1, 0, 2)
    message_gain = row_of(video_message_gain)
    message_normed, message_mixed, message_attended, message_tokens = messages_forward(
        messages,
        message_gain,
        row_of(video_message_shift),
        message_weight,
        qkv_bias(video_message_attend_bias),
        video_message_out_weight,
        row_of(video_message_out_bias),
    )
    tokens_here = own_part(message_tokens, frames)

    video_gain, video_gain_two = row_of(video_first_gain), row_of(video_final_gain)
    video_rows, video_normed = video_first(
        jnp.pad(video_input[0], spare),
        tokens_here[:, None],
        video_gain,
        row_of(video_first_shift),
        tokens,
    )
    video_plan = {
        "groups": [
            (start, frame_rows, start, frame_rows, start)
            for start in range(0, frames * frame_rows, frame_rows)
        ],
        "keys": tokens + 1,
        "out_rows": frames * frame_rows,
    }
    video_attention = [
        attention_forward(
            video_normed, video_qkv[side], video_qkv_bias[side], video_plan, (), "video_attention"
        )
        for side in sides
    ]
    video_resid, video_second = project_norm(
        [video_attention[side][1] for side in sides],
        video_out,
        video_rows,
        row_of(video_output_bias),
        video_gain_two,
        row_of(video_final_shift),
        frame_rows,
        0,
        "video_project",
    )
    message_output = video_resid.reshape(frames, frame_rows, width)[:, tokens].astype(BF16)[None]

    video_cot = jnp.pad(video_out_grad[0], spare).reshape(-1, width)
    video_units = {}
    text_units = {}
    for side in (1, 0):
        video_units[side] = feed_forward(
            video_second,
            video_cot,
            video_expand[side],
            row_of(biases[1][side]),
            video_reduce[side],
            video_expand[side].shape[1] // 3,
            "video_units",
        )
    for side in (1, 0):
        text_units[side] = feed_forward(
            text_second,
            text_out_grad,
            text_expand[side],
            row_of(biases[3][side]),
            text_reduce[side],
            text_expand[side].shape[1] // 2,
            "text_units",
        )
    grad_video_expand_weight, grad_video_reduce_weight = reduce_bucket(
        video_units[0][:2], video_units[1][:2]
    )
    grad_text_expand_weight, grad_text_reduce_weight = reduce_bucket(
        text_units[0][:2], text_units[1][:2]
    )
    video_final, video_grad_resid, video_low, video_sums = resid_back(
        video_resid,
        [video_units[side][3] for side in sides],
        [video_units[side][4] for side in sides],
        video_cot,
        message_out_grad[0].astype(F32)[:, None],
        video_gain_two,
        row_of(video_reduce_bias),
        frame_rows,
        tokens,
        "video_resid_back",
    )
    text_final, text_grad_resid, text_low, text_sums = resid_back(
        text_resid,
        [text_units[side][3] for side in sides],
        [text_units[side][4] for side in sides],
        text_out_grad,
        None,
        text_gain_two,
        row_of(text_reduce_bias),
        LANES,
        None,
        "text_resid_back",
    )
    video_output = video_final.reshape(1, frames, frame_rows, width)[:, :, :tokens]

    video_back, text_back = {}, {}
    for side in (1, 0):
        video_back[side] = attention_backward(
            video_low,
            video_out[side],
            video_attention[side][1],
            video_normed,
            video_qkv[side],
            video_attention[side][0],
            video_attention[side][2],
            video_plan,
            (),
            "video_attention_back",
        )
    for side in (1, 0):
        text_back[side] = attention_backward(
            text_low,
            text_out[side],
            text_attention[side][1],
            text_normed,
            text_qkv[side],
            text_attention[side][0],
            text_attention[side][2],
            text_plan,
            segments,
            "text_attention_back",
        )
    grad_video_output_weight, grad_video_attend_weight = reduce_bucket(
        video_back[0][:2], video_back[1][:2]
    )
    grad_text_output_weight, grad_text_attend_weight = reduce_bucket(
        text_back[0][:2], text_back[1][:2]
    )
    video_grads, video_edges, video_sums_one = video_rows_back(
        video_rows,
        [video_back[side][3] for side in sides],
        video_grad_resid,
        video_gain,
        frame_rows,
        tokens,
    )
    text_grads, text_sums_one = text_rows_back(
        text_rows, [text_back[side][3] for side in sides], text_grad_resid, text_gain, LANES
    )
    text_later = lax.ppermute(text_grads[:halo], "tensor", [(1, 0)])
    text_own = text_grads[halo:]
    text_input_grad = jnp.concatenate(
        [text_own[: text_count - halo], text_own[text_count - halo :] + text_later]
    ).astype(BF16)

    token_here = video_edges[:, 1]
    token_grads = in_order(token_here, swap(token_here))
    message_grads, message_low, class_grads, message_sums = messages_backward(
        messages,
        message_mixed,
        token_grads,
        message_gain,
        message_weight,
        video_message_out_weight,
        video_message_weight,
    )
    class_row = (video_edges[:, 0] + own_part(class_grads, frames)).astype(BF16)
    video_input_grad = (
        video_grads.reshape(frames, frame_rows, width)[:, :tokens].at[:, 0].set(class_row)[None]
    )
    factors = jnp.concatenate(
        [
            class_rows,
            own_part(message_normed, frames),
            own_part(message_attended, frames),
            token_here.astype(BF16),
            own_part(message_low, frames),
        ]
        + [own_part(message_grads[part], frames) for part in range(3)],
        axis=1,
    )
    factors = lax.all_gather(factors, ("dp", "tensor"), axis=0, tiled=True)
    factors = [factors[:, at * width : (at + 1) * width] for at in range(8)]
    contract = functools.partial(jnp.einsum, "rd,re->de", preferred_element_type=F32)
    grad_video_message_weight = contract(factors[0], factors[4])
    grad_video_message_out_weight = contract(factors[2], factors[3])
    grad_video_message_attend_weight = jnp.stack(
        [contract(factors[1], factors[5 + part]) for part in range(3)]
    ).transpose(1, 0, 2)

    vectors = [
        video_sums_one[0],
        video_sums_one[1],
        message_sums[4] * 0.5,
        message_sums[2] * 0.5,
        message_sums[3] * 0.5,
        message_sums[0] * 0.5,
        message_sums[1] * 0.5,
        message_sums[5] * 0.5,
        video_sums[3],
        video_sums[1],
        video_sums[2],
        video_sums[0],
        text_sums_one[0],
        text_sums_one[1],
        text_sums[3],
        text_sums[1],
        text_sums[2],
        text_sums[0],
        in_order(video_back[0][2][0], video_back[1][2][0]),
        in_order(video_back[0][2][1], video_back[1][2][1]),
        in_order(video_units[0][2][0], video_units[1][2][0]),
        in_order(text_back[0][2][0], text_back[1][2][0]),
        in_order(text_back[0][2][1], text_back[1][2][1]),
        in_order(text_units[0][2][0], text_units[1][2][0]),
    ]
    summed = lax.psum(jnp.concatenate(vectors), ("dp", "tensor"))
    done = []
    begin = 0
    for value in vectors:
        done.append(summed[begin : begin + value.size])
        begin += value.size
    half = [own_part(value, value.size // 2) for value in done[18:]]
    return (
        video_output,
        message_output,
        text_final,
        video_input_grad,
        text_input_grad,
        done[0],
        done[1],
        grad_video_message_weight,
        done[2],
        done[3],
        done[4],
        grad_video_message_attend_weight,
        jnp.stack([done[5], done[6]]),
        grad_video_message_out_weight,
        done[7],
        grad_video_attend_weight.transpose(1, 0, 2),
        jnp.stack([half[0], half[1]]),
        grad_video_output_weight,
        done[8],
        done[9],
        done[10],
        grad_video_expand_weight,
        half[2],
        grad_video_reduce_weight,
        done[11],
        done[12],
        done[13],
        grad_text_attend_weight.transpose(1, 0, 2),
        jnp.stack([half[3], half[4]]),
        grad_text_output_weight,
        done[14],
        done[15],
        done[16],
        grad_text_expand_weight,
        half[5],
        grad_text_reduce_weight,
        done[17],
    )


def solution(mesh):
    in_specs = (
        P("dp", "tensor", None, None),
        P(("dp", "tensor"), None),
        P("dp", None),
        P(),
        P(),
        P(),
        P(),
        P(),
        P(),
        P(),
        P(),
        P(),
        P(),
        P(None, None, "tensor"),
        P(None, "tensor"),
        P("tensor", None),
        P(),
        P(),
        P(),
        P(None, "tensor"),
        P("tensor"),
        P("tensor", None),
        P(),
        P(),
        P(),
        P(None, None, "tensor"),
        P(None, "tensor"),
        P("tensor", None),
        P(),
        P(),
        P(),
        P(None, "tensor"),
        P("tensor"),
        P("tensor", None),
        P(),
        P("dp", "tensor", None, None),
        P("dp", "tensor", None),
        P(("dp", "tensor"), None),
    )
    out_specs = (
        P("dp", "tensor", None, None),
        P("dp", "tensor", None),
        P(("dp", "tensor"), None),
        P("dp", "tensor", None, None),
        P(("dp", "tensor"), None),
        P(),
        P(),
        P(),
        P(),
        P(),
        P(),
        P(),
        P(),
        P(),
        P(),
        P(None, None, "tensor"),
        P(None, "tensor"),
        P("tensor", None),
        P(),
        P(),
        P(),
        P(None, "tensor"),
        P("tensor"),
        P("tensor", None),
        P(),
        P(),
        P(),
        P(None, None, "tensor"),
        P(None, "tensor"),
        P("tensor", None),
        P(),
        P(),
        P(),
        P(None, "tensor"),
        P("tensor"),
        P("tensor", None),
        P(),
    )
    return jax.shard_map(
        on_device, mesh=mesh, in_specs=in_specs, out_specs=out_specs, check_vma=False
    )
```

```python
import functools
import jax
import jax.numpy as jnp
from jax import lax
from jax.experimental import pallas as pl
from jax.experimental.pallas import tpu as pltpu
from jax.sharding import PartitionSpec as P

HD = 64
MAXLEN = 77
LANES = 128
VIDEO_CHUNKS = 2
TEXT_CHUNKS = 2
NEGATIVE = -1000000000.0
F32 = jnp.float32
BF16 = jnp.bfloat16
PARAMS = pltpu.CompilerParams(vmem_limit_bytes=60 << 20)


def nt(left, right):
    return lax.dot_general(left, right, (((1,), (1,)), ((), ())), preferred_element_type=F32)


def tn(left, right):
    return lax.dot_general(left, right, (((0,), (0,)), ((), ())), preferred_element_type=F32)


def mm(left, right):
    return jnp.dot(left, right, preferred_element_type=F32)


def unit_of(rows):
    centre = rows - jnp.mean(rows, axis=-1, keepdims=True)
    inverse = lax.rsqrt(jnp.mean(centre * centre, axis=-1, keepdims=True) + 1e-05)
    return centre * inverse, inverse


def norm_back(grad_out, unit_rows, inverse, gain_row):
    scaled = grad_out * gain_row
    return inverse * (
        scaled
        - jnp.mean(scaled, axis=-1, keepdims=True)
        - unit_rows * jnp.mean(scaled * unit_rows, axis=-1, keepdims=True)
    )


def column_sum(values):
    return jnp.sum(values, axis=0, keepdims=True)


def row_is(shape, row):
    return lax.broadcasted_iota(jnp.int32, shape, 0) == row


def low_half():
    return lax.broadcasted_iota(jnp.int32, (1, LANES), 1) < HD


def head_masks():
    first = low_half().astype(F32)
    return first.astype(BF16), (1.0 - first).astype(BF16)


def whole(array):
    return pl.BlockSpec(array.shape, lambda *_: (0,) * array.ndim)


def rows_block(rows, columns, offset=0):
    return pl.BlockSpec((rows, columns), lambda i: (i + offset, 0))


def cost(flops, arrays, outs):
    moved = sum(a.size * a.dtype.itemsize for a in arrays) + sum(
        a.size * jnp.dtype(a.dtype).itemsize for a in outs
    )
    return pl.CostEstimate(flops=int(flops), transcendentals=0, bytes_accessed=int(moved))


def call(body, grid, ins, in_specs, outs, out_specs, scratch=(), flops=0, name=None):
    return pl.pallas_call(
        body,
        grid=grid,
        in_specs=in_specs,
        out_specs=out_specs,
        out_shape=outs,
        scratch_shapes=list(scratch),
        compiler_params=PARAMS,
        cost_estimate=cost(flops, ins, outs),
        name=name,
    )(*ins)


def shape_of(shape, dtype):
    return jax.ShapeDtypeStruct(shape, dtype)


def video_first(frames_rows, tokens, gain, shift, token_row):
    frames, rows, width = frames_rows.shape

    def body(x_ref, token_ref, gain_ref, shift_ref, rows_ref, first_ref):
        x = x_ref[0].astype(F32)
        x = jnp.where(row_is(x.shape, token_row), token_ref[0], x)
        rows_ref[...] = x
        unit, _ = unit_of(x)
        first_ref[...] = (unit * gain_ref[...] + shift_ref[...]).astype(BF16)

    ins = (frames_rows, tokens, gain, shift)
    return call(
        body,
        (frames,),
        ins,
        [
            pl.BlockSpec((1, rows, width), lambda i: (i, 0, 0)),
            pl.BlockSpec((1, 1, width), lambda i: (i, 0, 0)),
            whole(gain),
            whole(shift),
        ],
        [shape_of((frames * rows, width), F32), shape_of((frames * rows, width), BF16)],
        [rows_block(rows, width), rows_block(rows, width)],
        name="video_first",
    )


def text_first(rows_in, gain, shift, block):
    rows, width = rows_in.shape

    def body(x_ref, gain_ref, shift_ref, first_ref):
        unit, _ = unit_of(x_ref[...].astype(F32))
        first_ref[...] = (unit * gain_ref[...] + shift_ref[...]).astype(BF16)

    ins = (rows_in, gain, shift)
    return call(
        body,
        (rows // block,),
        ins,
        [rows_block(block, width), whole(gain), whole(shift)],
        [shape_of((rows, width), BF16)],
        [rows_block(block, width)],
        name="text_first",
    )[0]


def masked(scores, plan, group, segments):
    if plan["keys"] is not None:
        columns = lax.broadcasted_iota(jnp.int32, scores.shape, 1)
        return jnp.where(columns < plan["keys"], scores, NEGATIVE)
    query_start, queries, key_start, keys, _ = group
    column_ref, row_ref = segments
    same = (
        column_ref[query_start : query_start + queries, :]
        == row_ref[:, key_start : key_start + keys]
    )
    columns = lax.broadcasted_iota(jnp.int32, scores.shape, 1) + key_start
    positions = lax.broadcasted_iota(jnp.int32, scores.shape, 0) + query_start
    return jnp.where(same & (columns <= positions), scores, NEGATIVE)


def attention_forward(first, weight, bias, plan, segments, name):
    rows, width = first.shape
    heads_width = weight.shape[2]
    steps = heads_width // LANES
    out_rows = plan["out_rows"]

    def body(x_ref, w_ref, b_ref, *rest):
        segment_refs, (mixed_ref, out_ref, lse_ref, wide_ref) = rest[:-4], rest[-4:]
        for part in range(3):
            wide_ref[:, part * LANES : (part + 1) * LANES] = w_ref[part]
        mixed = mm(x_ref[...], wide_ref[...])
        for part in range(3):
            mixed_ref[part] = (
                mixed[:, part * LANES : (part + 1) * LANES] + b_ref[part : part + 1, :]
            ).astype(BF16)
        masks = head_masks()
        lower = low_half()
        for group in plan["groups"]:
            query_start, queries, key_start, keys, out_start = group
            q = mixed_ref[0, query_start : query_start + queries, :] * jnp.asarray(0.125, BF16)
            k = mixed_ref[1, key_start : key_start + keys, :]
            v = mixed_ref[2, key_start : key_start + keys, :]
            outs, sums = [], []
            for mask in masks:
                scores = masked(nt(q * mask, k), plan, group, segment_refs)
                top = jnp.max(scores, axis=-1, keepdims=True)
                powers = jnp.exp(scores - top)
                total = jnp.sum(powers, axis=-1, keepdims=True)
                probs = (powers * (1.0 / total)).astype(BF16)
                outs.append(mm(probs, v))
                sums.append(top + jnp.log(total))
            out_ref[out_start : out_start + queries, :] = jnp.where(lower, outs[0], outs[1]).astype(
                BF16
            )
            lse_ref[out_start : out_start + queries, :] = jnp.where(lower, sums[0], sums[1])

    ins = (first, weight, bias) + segments
    return call(
        body,
        (steps,),
        ins,
        [
            whole(first),
            pl.BlockSpec((3, width, LANES), lambda i: (0, 0, i)),
            pl.BlockSpec((3, LANES), lambda i: (0, i)),
        ]
        + [whole(s) for s in segments],
        [
            shape_of((3, rows, heads_width), BF16),
            shape_of((out_rows, heads_width), BF16),
            shape_of((out_rows, heads_width), F32),
        ],
        [
            pl.BlockSpec((3, rows, LANES), lambda i: (0, 0, i)),
            pl.BlockSpec((out_rows, LANES), lambda i: (0, i)),
            pl.BlockSpec((out_rows, LANES), lambda i: (0, i)),
        ],
        scratch=[pltpu.VMEM((width, 3 * LANES), BF16)],
        flops=2 * rows * width * 3 * heads_width * 2,
        name=name,
    )


def attention_backward(
    low, out_weight, attended, first, weight, mixed, lse, plan, segments, name
):
    rows, width = first.shape
    out_rows = plan["out_rows"]
    heads_width = weight.shape[2]
    steps = heads_width // LANES
    shared = plan["keys"] is None

    def body(low_ref, ow_ref, att_ref, x_ref, w_ref, mixed_ref, lse_ref, *rest):
        segment_refs = rest[: len(segments)]
        (
            flat_ref,
            bias_ref,
            first_grad_ref,
            wide_ref,
            turned_ref,
            grad_ref,
            key_ref,
            value_ref,
        ) = rest[len(segments) :]
        step = pl.program_id(0)

        @pl.when(step == 0)
        def _():
            turned_ref[...] = x_ref[...].T
            first_grad_ref[...] = jnp.zeros_like(first_grad_ref)

        for part in range(3):
            wide_ref[:, part * LANES : (part + 1) * LANES] = w_ref[part]
        low_rows = low_ref[...]
        grad_out = nt(low_rows, ow_ref[...]).astype(BF16)
        out_grad = tn(att_ref[...], low_rows).astype(BF16)
        for part in range(width // LANES):
            flat_ref[3, 0, part * LANES : (part + 1) * LANES, :] = out_grad[
                :, part * LANES : (part + 1) * LANES
            ]
        if shared:
            grad_ref[...] = jnp.zeros_like(grad_ref)
            key_ref[...] = jnp.zeros_like(key_ref)
            value_ref[...] = jnp.zeros_like(value_ref)
        masks = head_masks()
        lower = low_half()
        for group in plan["groups"]:
            query_start, queries, key_start, keys, out_start = group
            q = mixed_ref[0, query_start : query_start + queries, :] * jnp.asarray(0.125, BF16)
            k = mixed_ref[1, key_start : key_start + keys, :]
            v = mixed_ref[2, key_start : key_start + keys, :]
            g = grad_out[out_start : out_start + queries, :]
            query_grads, key_grad, value_grad = [], None, None
            for head, mask in enumerate(masks):
                query_head, grad_head = q * mask, g * mask
                scores = masked(nt(query_head, k), plan, group, segment_refs)
                column = lse_ref[out_start : out_start + queries, head * HD : head * HD + 1]
                probs = jnp.exp(scores - column)
                grad_probs = nt(grad_head, v)
                dots = jnp.sum(probs * grad_probs, axis=-1, keepdims=True)
                grad_scores = (probs * (grad_probs - dots)).astype(BF16)
                query_grads.append(mm(grad_scores, k))
                key_term = tn(grad_scores, query_head)
                value_term = tn(probs.astype(BF16), grad_head)
                key_grad = key_term if key_grad is None else key_grad + key_term
                value_grad = value_term if value_grad is None else value_grad + value_term
            query_grad = jnp.where(lower, query_grads[0], query_grads[1]) * 0.125
            grad_ref[query_start : query_start + queries, :LANES] = query_grad.astype(BF16)
            span = slice(key_start, key_start + keys)
            if shared:
                key_ref[span, :] += key_grad
                value_ref[span, :] += value_grad
            else:
                grad_ref[span, LANES : 2 * LANES] = key_grad.astype(BF16)
                grad_ref[span, 2 * LANES :] = value_grad.astype(BF16)
        if shared:
            grad_ref[:, LANES : 2 * LANES] = key_ref[...].astype(BF16)
            grad_ref[:, 2 * LANES :] = value_ref[...].astype(BF16)
        grads = grad_ref[...]
        weight_grads = mm(turned_ref[...], grads)
        sums = column_sum(grads.astype(F32))
        for part in range(3):
            flat_ref[part, 0] = weight_grads[:, part * LANES : (part + 1) * LANES].astype(BF16)
        bias_ref[0:1, :] = sums[:, :LANES]
        bias_ref[1:2, :] = sums[:, 2 * LANES :]
        first_grad_ref[...] += nt(grads, wide_ref[...])

    ins = (low, out_weight, attended, first, weight, mixed, lse) + segments
    return call(
        body,
        (steps,),
        ins,
        [
            whole(low),
            pl.BlockSpec((LANES, width), lambda i: (i, 0)),
            pl.BlockSpec((out_rows, LANES), lambda i: (0, i)),
            whole(first),
            pl.BlockSpec((3, width, LANES), lambda i: (0, 0, i)),
            pl.BlockSpec((3, rows, LANES), lambda i: (0, 0, i)),
            pl.BlockSpec((out_rows, LANES), lambda i: (0, i)),
        ]
        + [whole(s) for s in segments],
        [
            shape_of((4, steps, width, LANES), BF16),
            shape_of((2, heads_width), F32),
            shape_of((rows, width), F32),
        ],
        [
            pl.BlockSpec((4, 1, width, LANES), lambda i: (0, i, 0, 0)),
            pl.BlockSpec((2, LANES), lambda i: (0, i)),
            pl.BlockSpec((rows, width), lambda i: (0, 0)),
        ],
        scratch=[
            pltpu.VMEM((width, 3 * LANES), BF16),
            pltpu.VMEM((width, rows), BF16),
            pltpu.VMEM((rows, 3 * LANES), BF16),
            pltpu.VMEM((rows, LANES), F32),
            pltpu.VMEM((rows, LANES), F32),
        ],
        flops=2 * rows * width * 8 * heads_width * 2,
        name=name,
    )


def project_norm(parts, weights, rows_in, bias, gain, shift, block, offset, name):
    out_rows, half = parts[0].shape
    width = bias.shape[1]

    def body(a_ref, b_ref, wa_ref, wb_ref, rows_ref, bias_ref, gain_ref, shift_ref, res_ref, out_ref):
        resid = (
            rows_ref[...].astype(F32)
            + mm(a_ref[...], wa_ref[...])
            + mm(b_ref[...], wb_ref[...])
            + bias_ref[...]
        )
        res_ref[...] = resid
        unit, _ = unit_of(resid)
        out_ref[...] = (unit * gain_ref[...] + shift_ref[...]).astype(BF16)

    ins = (*parts, *weights, rows_in, bias, gain, shift)
    return call(
        body,
        (out_rows // block,),
        ins,
        [
            rows_block(block, half),
            rows_block(block, half),
            whole(weights[0]),
            whole(weights[1]),
            rows_block(block, width, offset),
            whole(bias),
            whole(gain),
            whole(shift),
        ],
        [shape_of((out_rows, width), F32), shape_of((out_rows, width), BF16)],
        [rows_block(block, width), rows_block(block, width)],
        flops=4 * out_rows * half * width,
        name=name,
    )


def feed_forward(second, cot, expand, expand_bias, reduce, chunk, name):
    rows, width = second.shape
    units = expand.shape[1]
    size = width * chunk // LANES

    def body(x_ref, cot_ref, e_ref, b_ref, r_ref, *rest):
        flat_ref, gb_ref, out_ref, back_ref, turned_ref = rest

        @pl.when(pl.program_id(0) == 0)
        def _():
            turned_ref[...] = x_ref[...].T
            out_ref[...] = jnp.zeros_like(out_ref)
            back_ref[...] = jnp.zeros_like(back_ref)

        cot_rows = cot_ref[...]
        hidden = mm(x_ref[...], e_ref[...]) + b_ref[...]
        grad_active = nt(cot_rows, r_ref[...])
        logistic = 1.0 / (1.0 + jnp.exp(-1.702 * hidden))
        active = (hidden * logistic).astype(BF16)
        slope = logistic + 1.702 * hidden * logistic * (1.0 - logistic)
        grad_hidden = grad_active * slope
        grad_low = grad_hidden.astype(BF16)
        gb_ref[...] = column_sum(grad_low.astype(F32))
        out_ref[...] += mm(active, r_ref[...])
        back_ref[...] += nt(grad_low, e_ref[...])
        reduce_grad = tn(active, cot_rows).astype(BF16)
        expand_grad = mm(turned_ref[...], grad_low).astype(BF16)
        for part in range(chunk // LANES):
            flat_ref[0, 0, part * width : (part + 1) * width, :] = expand_grad[
                :, part * LANES : (part + 1) * LANES
            ]
        for part in range(width // LANES):
            flat_ref[1, 0, part * chunk : (part + 1) * chunk, :] = reduce_grad[
                :, part * LANES : (part + 1) * LANES
            ]

    ins = (second, cot, expand, expand_bias, reduce)
    return call(
        body,
        (units // chunk,),
        ins,
        [
            whole(second),
            whole(cot),
            pl.BlockSpec((width, chunk), lambda i: (0, i)),
            pl.BlockSpec((1, chunk), lambda i: (0, i)),
            pl.BlockSpec((chunk, width), lambda i: (i, 0)),
        ],
        [
            shape_of((2, units // chunk, size, LANES), BF16),
            shape_of((1, units), F32),
            shape_of((rows, width), F32),
            shape_of((rows, width), F32),
        ],
        [
            pl.BlockSpec((2, 1, size, LANES), lambda i: (0, i, 0, 0)),
            pl.BlockSpec((1, chunk), lambda i: (0, i)),
            pl.BlockSpec((rows, width), lambda i: (0, 0)),
            pl.BlockSpec((rows, width), lambda i: (0, 0)),
        ],
        scratch=[pltpu.VMEM((width, rows), BF16)],
        flops=12 * rows * width * units,
        name=name,
    )


def resid_back(resid, outs, backs, cot, token_grads, gain, reduce_bias, block, token_row, name):
    rows, width = resid.shape

    def body(res_ref, oa_ref, ob_ref, ba_ref, bb_ref, cot_ref, *rest):
        if token_row is None:
            gain_ref, rb_ref, final_ref, grad_ref, low_ref, sums_ref = rest
        else:
            token_ref, gain_ref, rb_ref, final_ref, grad_ref, low_ref, sums_ref = rest

        @pl.when(pl.program_id(0) == 0)
        def _():
            sums_ref[...] = jnp.zeros_like(sums_ref)

        resid_rows = res_ref[...]
        final_ref[...] = (resid_rows + oa_ref[...] + ob_ref[...] + rb_ref[...]).astype(BF16)
        back = ba_ref[...] + bb_ref[...]
        unit, inverse = unit_of(resid_rows)
        cot_rows = cot_ref[...].astype(F32)
        sums_ref[0:1, :] += column_sum(cot_rows)
        sums_ref[1:2, :] += column_sum(back * unit)
        sums_ref[2:3, :] += column_sum(back)
        if token_row is not None:
            cot_rows = jnp.where(row_is(cot_rows.shape, token_row), token_ref[0], cot_rows)
        grad = cot_rows + norm_back(back, unit, inverse, gain_ref[...])
        sums_ref[3:4, :] += column_sum(grad)
        grad_ref[...] = grad
        low_ref[...] = grad.astype(BF16)

    ins = (resid, *outs, *backs, cot)
    specs = [rows_block(block, width)] * 6
    if token_row is not None:
        ins += (token_grads,)
        specs.append(pl.BlockSpec((1, 1, width), lambda i: (i, 0, 0)))
    ins += (gain, reduce_bias)
    specs += [whole(gain), whole(reduce_bias)]
    return call(
        body,
        (rows // block,),
        ins,
        specs,
        [
            shape_of((rows, width), BF16),
            shape_of((rows, width), F32),
            shape_of((rows, width), BF16),
            shape_of((4, width), F32),
        ],
        [rows_block(block, width)] * 3 + [pl.BlockSpec((4, width), lambda i: (0, 0))],
        name=name,
    )


def video_rows_back(rows_in, firsts, grad_resid, gain, block, token_row):
    rows, width = rows_in.shape
    frames = rows // block

    def body(rows_ref, fa_ref, fb_ref, grad_ref, gain_ref, out_ref, edge_ref, sums_ref):
        @pl.when(pl.program_id(0) == 0)
        def _():
            sums_ref[...] = jnp.zeros_like(sums_ref)

        unit, inverse = unit_of(rows_ref[...])
        back = fa_ref[...] + fb_ref[...]
        sums_ref[0:1, :] += column_sum(back * unit)
        sums_ref[1:2, :] += column_sum(back)
        grad = grad_ref[...] + norm_back(back, unit, inverse, gain_ref[...])
        out_ref[...] = grad.astype(BF16)
        edge_ref[0, 0:1, :] = grad[0:1, :]
        edge_ref[0, 1:2, :] = grad[token_row : token_row + 1, :]

    ins = (rows_in, *firsts, grad_resid, gain)
    return call(
        body,
        (frames,),
        ins,
        [rows_block(block, width)] * 4 + [whole(gain)],
        [
            shape_of((rows, width), BF16),
            shape_of((frames, 2, width), F32),
            shape_of((2, width), F32),
        ],
        [
            rows_block(block, width),
            pl.BlockSpec((1, 2, width), lambda i: (i, 0, 0)),
            pl.BlockSpec((2, width), lambda i: (0, 0)),
        ],
        name="video_rows_back",
    )


def text_rows_back(rows_in, firsts, grad_resid, gain, block):
    rows, width = rows_in.shape
    ahead = (rows - grad_resid.shape[0]) // block

    def body(rows_ref, fa_ref, fb_ref, grad_ref, gain_ref, out_ref, sums_ref):
        step = pl.program_id(0)

        @pl.when(step == 0)
        def _():
            sums_ref[...] = jnp.zeros_like(sums_ref)

        unit, inverse = unit_of(rows_ref[...].astype(F32))
        back = fa_ref[...] + fb_ref[...]
        sums_ref[0:1, :] += column_sum(back * unit)
        sums_ref[1:2, :] += column_sum(back)
        own = jnp.where(step >= ahead, 1.0, 0.0)
        out_ref[...] = grad_ref[...] * own + norm_back(back, unit, inverse, gain_ref[...])

    ins = (rows_in, *firsts, grad_resid, gain)
    return call(
        body,
        (rows // block,),
        ins,
        [rows_block(block, width)] * 3
        + [
            pl.BlockSpec((block, width), lambda i: (jnp.maximum(i - ahead, 0), 0)),
            whole(gain),
        ],
        [shape_of((rows, width), F32), shape_of((2, width), F32)],
        [rows_block(block, width), pl.BlockSpec((2, width), lambda i: (0, 0))],
        name="text_rows_back",
    )


def head_rows(values, heads):
    lanes = lax.broadcasted_iota(jnp.int32, values.shape, 1) // HD
    return jnp.concatenate(
        [jnp.where(lanes == head, values, 0.0) for head in range(heads)], axis=0
    ).astype(BF16)


def fold_heads(values, heads, rows):
    lanes = lax.broadcasted_iota(jnp.int32, (rows, values.shape[1]), 1) // HD
    total = jnp.zeros((rows, values.shape[1]), F32)
    for head in range(heads):
        total = total + jnp.where(lanes == head, values[head * rows : (head + 1) * rows], 0.0)
    return total


def message_probs(mixed_ref, heads):
    query_rows = head_rows(mixed_ref[0].astype(F32) * 0.125, heads)
    scores = nt(query_rows, mixed_ref[1])
    top = jnp.max(scores, axis=-1, keepdims=True)
    powers = jnp.exp(scores - top)
    return query_rows, powers * (1.0 / jnp.sum(powers, axis=-1, keepdims=True))


def messages_forward(messages, gain, shift, weight, bias, out_weight, out_bias):
    rows, width = messages.shape
    heads = width // HD

    def body(m_ref, gain_ref, shift_ref, w_ref, b_ref, ow_ref, ob_ref, n_ref, mixed_ref, a_ref, t_ref):
        messages_now = m_ref[...]
        unit, _ = unit_of(messages_now)
        normed = (unit * gain_ref[...] + shift_ref[...]).astype(BF16)
        n_ref[...] = normed
        for part in range(3):
            mixed_ref[part] = (mm(normed, w_ref[part]) + b_ref[part : part + 1, :]).astype(BF16)
        _, probs = message_probs(mixed_ref, heads)
        attended = fold_heads(mm(probs.astype(BF16), mixed_ref[2]), heads, rows).astype(BF16)
        a_ref[...] = attended
        t_ref[...] = messages_now + mm(attended, ow_ref[...]) + ob_ref[...]

    ins = (messages, gain, shift, weight, bias, out_weight, out_bias)
    outs = [
        shape_of((rows, width), BF16),
        shape_of((3, rows, width), BF16),
        shape_of((rows, width), BF16),
        shape_of((rows, width), F32),
    ]
    return call(
        body, (1,), ins, [whole(a) for a in ins], outs, [whole(o) for o in outs], name="messages"
    )


def messages_backward(messages, mixed, token_grads, gain, weight, out_weight, in_weight):
    rows, width = messages.shape
    heads = width // HD

    def body(m_ref, mixed_ref, t_ref, gain_ref, w_ref, ow_ref, iw_ref, g_ref, low_ref, c_ref, s_ref):
        token = t_ref[...]
        grad_attended = nt(token.astype(BF16), ow_ref[...]).astype(BF16)
        query_rows, probs = message_probs(mixed_ref, heads)
        grad_rows = head_rows(grad_attended.astype(F32), heads)
        grad_probs = nt(grad_rows, mixed_ref[2])
        dots = jnp.sum(probs * grad_probs, axis=-1, keepdims=True)
        grad_scores = (probs * (grad_probs - dots)).astype(BF16)
        grads = (
            fold_heads(mm(grad_scores, mixed_ref[1]), heads, rows) * 0.125,
            tn(grad_scores, query_rows),
            tn(probs.astype(BF16), grad_rows),
        )
        normed_grad = jnp.zeros((rows, width), F32)
        for part in range(3):
            low = grads[part].astype(BF16)
            g_ref[part] = low
            normed_grad = normed_grad + nt(low, w_ref[part])
        s_ref[0:1, :] = column_sum(g_ref[0].astype(F32))
        s_ref[1:2, :] = column_sum(g_ref[2].astype(F32))
        unit, inverse = unit_of(m_ref[...])
        s_ref[2:3, :] = column_sum(normed_grad * unit)
        s_ref[3:4, :] = column_sum(normed_grad)
        grad = token + norm_back(normed_grad, unit, inverse, gain_ref[...])
        s_ref[4:5, :] = column_sum(grad)
        s_ref[5:6, :] = column_sum(token)
        low = grad.astype(BF16)
        low_ref[...] = low
        c_ref[...] = nt(low, iw_ref[...])

    ins = (messages, mixed, token_grads, gain, weight, out_weight, in_weight)
    outs = [
        shape_of((3, rows, width), BF16),
        shape_of((rows, width), BF16),
        shape_of((rows, width), F32),
        shape_of((6, width), F32),
    ]
    return call(
        body,
        (1,),
        ins,
        [whole(a) for a in ins],
        outs,
        [whole(o) for o in outs],
        name="messages_back",
    )


def swap(value):
    return lax.ppermute(value, "tensor", [(0, 1), (1, 0)])


def in_order(own, other, axis=0):
    first = lax.axis_index("tensor") == 0
    return jnp.where(
        first, jnp.concatenate([own, other], axis), jnp.concatenate([other, own], axis)
    )


def own_part(values, size, axis=0):
    return lax.dynamic_slice_in_dim(values, lax.axis_index("tensor") * size, size, axis)


def row_of(vector):
    return vector.astype(F32).reshape(1, -1)


def qkv_bias(flat):
    rows = flat.astype(F32).reshape(2, -1)
    return jnp.stack([rows[0], jnp.zeros_like(rows[0]), rows[1]])


def exchange(value, away):
    size = lax.axis_size("dp")
    return lax.ppermute(value, "dp", [(at, at ^ away) for at in range(size)])


def bit_of(bit):
    return (lax.axis_index("dp") >> bit) & 1


def add(*values):
    return sum(value.astype(F32) for value in values).astype(BF16)


def dp_bits():
    return lax.axis_size("dp").bit_length() - 1


def by_bit(own, other, mine):
    return jnp.where(
        mine == 0, jnp.concatenate([own, other], 0), jnp.concatenate([other, own], 0)
    )


class Steps:
    def __init__(self, make, *ins):
        self.after = ()
        self.steps = make(self, *ins)
        self.result = None

    def step(self, *after):
        self.after = after
        try:
            return next(self.steps)
        except StopIteration as stop:
            self.result = stop.value
            return ()

    def hold(self, values):
        return tie(values, self.after) if self.after else values


def tie(value, *waited):
    return lax.optimization_barrier((value, waited))[0]


def take(rows, part, size):
    return lax.dynamic_slice_in_dim(rows, part * size, size)


def bucket_steps(steps, own, received):
    orders = (0, 1), (1, 0)
    bits = [bit_of(bit) for bit in orders[0]]
    half = own.shape[0] // 2
    spans = slice(0, half), slice(half, None)
    parts = [[own[span], received[span]] for span in spans]
    for at in range(2):
        kept, arrived = [], []
        for values, order in zip(parts, orders):
            size = values[0].shape[0] // 2
            mine = bits[order[at]]
            send = [take(value, 1 - mine, size) for value in values]
            kept.append([take(value, mine, size) for value in values])
            arrived.append(exchange(add(*send) if at == 0 else send[0], 1 << order[at]))
        yield arrived
        arrived = steps.hold(arrived)
        parts = [[add(*keep, there)] for keep, there in zip(kept, arrived)]
    rows = jnp.concatenate([values[0] for values in parts])
    count = lax.axis_size("dp") // 4
    here = lax.axis_index("dp") >> 2
    size = rows.shape[0] // count
    arrived = [exchange(take(rows, here ^ away, size), away << 2) for away in range(1, count)]
    yield arrived
    arrived = steps.hold(arrived)
    rows = add(take(rows, here, size), *arrived)
    arrived = [exchange(rows, away << 2) for away in range(1, count)]
    yield arrived
    arrived = steps.hold(arrived)
    pieces = jnp.concatenate([rows] + arrived)
    rows = jnp.concatenate([take(pieces, at ^ here, size) for at in range(count)])
    half = rows.shape[0] // 2
    parts = [rows[:half], rows[half:]]
    for at in (1, 0):
        arrived = [exchange(value, 1 << order[at]) for value, order in zip(parts, orders)]
        yield arrived
        arrived = steps.hold(arrived)
        parts = [jnp.concatenate(pair) for pair in zip(parts, arrived)]
    return jnp.concatenate(parts), jnp.stack([bits[0] * 2 + bits[1], bits[1] * 2 + bits[0]])


def place(at, blocks, here_ref):
    part = blocks // 8
    piece = at // part
    return ((piece ^ here_ref[piece // 4]) * part + at % part, 0)


def vector_steps(steps, vectors):
    total = jnp.concatenate(vectors).reshape(-1, LANES)
    there = swap(total)
    yield there
    total = total + steps.hold(there)
    for bit in range(dp_bits()):
        there = exchange(total, 1 << bit)
        yield there
        total = total + steps.hold(there)
    total = total.reshape(-1)
    done = []
    begin = 0
    for value in vectors:
        done.append(total[begin : begin + value.size])
        begin += value.size
    return done


def gather_steps(steps, values):
    for bit in reversed(range(dp_bits())):
        there = exchange(values, 1 << bit)
        yield there
        values = by_bit(values, steps.hold(there), bit_of(bit))
    there = swap(values)
    yield there
    return in_order(values, steps.hold(there))


def unpack(summed, first, count, block, out_shape, out_block, out_index, name):
    rows, here = summed
    blocks = rows.shape[0] // block

    def in_index(i, here_ref):
        return place(first + i, blocks, here_ref)

    def body(here_ref, rows_ref, out_ref):
        out_ref[...] = rows_ref[...].astype(F32).reshape(out_ref.shape)

    out = shape_of(out_shape, F32)
    return pl.pallas_call(
        body,
        grid_spec=pltpu.PrefetchScalarGridSpec(
            num_scalar_prefetch=1,
            grid=(count,),
            in_specs=[pl.BlockSpec((block, LANES), in_index)],
            out_specs=pl.BlockSpec(out_block, lambda i, here_ref: out_index(i)),
        ),
        out_shape=out,
        compiler_params=PARAMS,
        cost_estimate=cost(0, (rows,), (out,)),
        name=name,
    )(here, rows)


def unpack_units(summed, width, units, chunk, name):
    across = width // LANES
    count = units // LANES
    expand = unpack(
        summed, 0, count, width, (width, units), (width, LANES), lambda i: (0, i), name
    )
    reduce = unpack(
        summed,
        count,
        count,
        chunk,
        (units, width),
        (chunk, LANES),
        lambda i: (i // across, i % across),
        name,
    )
    return expand, reduce


def unpack_attention(summed, first, width, steps, name):
    rows, here = summed
    block = width // 2
    blocks = rows.shape[0] // block

    def body(here_ref, *refs):
        attend_ref, out_ref = refs[8:]
        for at in range(8):
            values = refs[at][...].astype(F32)
            start = at % 2 * block
            if at < 6:
                attend_ref[at // 2, start : start + block, :] = values
                continue
            for part in range(block // LANES):
                begin = start + part * LANES
                out_ref[:, begin : begin + LANES] = values[part * LANES : (part + 1) * LANES, :]

    def in_spec(at):
        return pl.BlockSpec(
            (block, LANES),
            lambda i, here_ref: place(
                (first + at // 2 * steps + i) * 2 + at % 2, blocks, here_ref
            ),
        )

    outs = [shape_of((3, width, steps * LANES), F32), shape_of((steps * LANES, width), F32)]
    return pl.pallas_call(
        body,
        grid_spec=pltpu.PrefetchScalarGridSpec(
            num_scalar_prefetch=1,
            grid=(steps,),
            in_specs=[in_spec(at) for at in range(8)],
            out_specs=[
                pl.BlockSpec((3, width, LANES), lambda i, here_ref: (0, 0, i)),
                pl.BlockSpec((LANES, width), lambda i, here_ref: (i, 0)),
            ],
        ),
        out_shape=outs,
        compiler_params=PARAMS,
        cost_estimate=cost(0, (rows,), outs),
        name=name,
    )(here, *([rows] * 8))


def on_device(
    video_input,
    text_input,
    caption_lengths,
    video_first_gain,
    video_first_shift,
    video_message_weight,
    video_message_bias,
    video_message_gain,
    video_message_shift,
    video_message_attend_weight,
    video_message_attend_bias,
    video_message_out_weight,
    video_message_out_bias,
    video_attend_weight,
    video_attend_bias,
    video_output_weight,
    video_output_bias,
    video_final_gain,
    video_final_shift,
    video_expand_weight,
    video_expand_bias,
    video_reduce_weight,
    video_reduce_bias,
    text_first_gain,
    text_first_shift,
    text_attend_weight,
    text_attend_bias,
    text_output_weight,
    text_output_bias,
    text_final_gain,
    text_final_shift,
    text_expand_weight,
    text_expand_bias,
    text_reduce_weight,
    text_reduce_bias,
    video_out_grad,
    message_out_grad,
    text_out_grad,
):
    core = lax.axis_index("tensor")
    frames, tokens, width = video_input.shape[1:]
    frame_rows = -(-(tokens + 1) // 16) * 16
    spare = ((0, 0), (0, frame_rows - tokens), (0, 0))
    text_count, text_width = text_input.shape
    halo = -(-(MAXLEN - 1) // LANES) * LANES

    class_rows = video_input[0, :, 0, :]
    messages_here = (
        jnp.dot(class_rows, video_message_weight, preferred_element_type=F32)
        + video_message_bias.astype(F32)
    )
    messages_there = swap(messages_here)
    text_qkv = (text_attend_weight.transpose(1, 0, 2),)
    video_qkv = (video_attend_weight.transpose(1, 0, 2),)
    small = (video_attend_bias, video_expand_bias, text_attend_bias, text_expand_bias)
    packed = jnp.concatenate([value.reshape(-1) for value in small])
    packed_there = swap(packed)
    biases = []
    begin = 0
    for value in small:
        biases.append((packed[begin : begin + value.size], packed_there[begin : begin + value.size]))
        begin += value.size
    text_ahead = lax.ppermute(text_input[text_count - halo :], "tensor", [(0, 1)])
    text_qkv += (swap(text_qkv[0]),)
    video_qkv += (swap(video_qkv[0]),)
    text_out = (text_output_weight, swap(text_output_weight))
    video_out = (video_output_weight, swap(video_output_weight))
    video_expand = (video_expand_weight, swap(video_expand_weight))
    video_reduce = (video_reduce_weight, swap(video_reduce_weight))
    text_expand = (text_expand_weight, swap(text_expand_weight))
    text_reduce = (text_reduce_weight, swap(text_reduce_weight))
    video_qkv_bias = [qkv_bias(flat) for flat in biases[0]]
    text_qkv_bias = [qkv_bias(flat) for flat in biases[2]]
    sides = (0, 1)

    messages = in_order(messages_here, messages_there)
    message_weight = video_message_attend_weight.transpose(1, 0, 2)
    message_gain = row_of(video_message_gain)
    message_normed, message_mixed, message_attended, message_tokens = messages_forward(
        messages,
        message_gain,
        row_of(video_message_shift),
        message_weight,
        qkv_bias(video_message_attend_bias),
        video_message_out_weight,
        row_of(video_message_out_bias),
    )
    tokens_here = own_part(message_tokens, frames)

    video_gain, video_gain_two = row_of(video_first_gain), row_of(video_final_gain)
    video_rows, video_normed = video_first(
        jnp.pad(video_input[0], spare),
        tokens_here[:, None],
        video_gain,
        row_of(video_first_shift),
        tokens,
    )
    video_plan = {
        "groups": [
            (start, frame_rows, start, frame_rows, start)
            for start in range(0, frames * frame_rows, frame_rows)
        ],
        "keys": tokens + 1,
        "out_rows": frames * frame_rows,
    }
    video_attention = [
        attention_forward(
            video_normed, video_qkv[side], video_qkv_bias[side], video_plan, (), "video_attention"
        )
        for side in sides
    ]
    video_resid, video_second = project_norm(
        [video_attention[side][1] for side in sides],
        video_out,
        video_rows,
        row_of(video_output_bias),
        video_gain_two,
        row_of(video_final_shift),
        frame_rows,
        0,
        "video_project",
    )
    message_output = video_resid.reshape(frames, frame_rows, width)[:, tokens].astype(BF16)[None]

    video_cot = jnp.pad(video_out_grad[0], spare).reshape(-1, width)
    video_units = {}
    for side in (1, 0):
        video_units[side] = feed_forward(
            video_second,
            video_cot,
            video_expand[side],
            row_of(biases[1][side]),
            video_reduce[side],
            video_expand[side].shape[1] // VIDEO_CHUNKS,
            "video_units",
        )
    units_bucket = Steps(
        bucket_steps,
        video_units[0][0].reshape(-1, LANES),
        swap(video_units[1][0].reshape(-1, LANES)),
    )
    units_there = units_bucket.step()
    text_rows = jnp.concatenate([text_ahead, text_input])
    rows_all = text_count + halo
    caption_ends = jnp.cumsum(caption_lengths[0])
    positions = core * text_count - halo + jnp.arange(rows_all, dtype=jnp.int32)
    segment = jnp.sum((positions[:, None] >= caption_ends[None, :]).astype(jnp.int32), axis=1)
    segment = jnp.where(positions < 0, -1, segment)
    segments = (segment.reshape(-1, 1), segment.reshape(1, -1))
    text_plan = {
        "groups": [
            (halo + start, LANES, start, halo + LANES, start)
            for start in range(0, text_count, LANES)
        ],
        "keys": None,
        "out_rows": text_count,
    }
    text_gain, text_gain_two = row_of(text_first_gain), row_of(text_final_gain)
    text_normed = text_first(
        tie(text_rows, video_units[0][1]), text_gain, row_of(text_first_shift), LANES
    )
    text_attention = {}
    for side in (0, 1):
        text_attention[side] = attention_forward(
            text_normed,
            text_qkv[side],
            text_qkv_bias[side],
            text_plan,
            segments,
            "text_attention",
        )
    text_resid, text_second = project_norm(
        [text_attention[side][1] for side in sides],
        text_out,
        text_rows,
        row_of(text_output_bias),
        text_gain_two,
        row_of(text_final_shift),
        LANES,
        halo // LANES,
        "text_project",
    )
    text_units = {}
    for side in (1, 0):
        text_units[side] = feed_forward(
            tie(text_second, units_there) if side == 0 else text_second,
            text_out_grad,
            text_expand[side],
            row_of(biases[3][side]),
            text_reduce[side],
            text_expand[side].shape[1] // TEXT_CHUNKS,
            "text_units",
        )
    units_there = units_bucket.step(text_units[1][1])
    text_final, text_grad_resid, text_low, text_sums = resid_back(
        text_resid,
        [text_units[side][2] for side in sides],
        [text_units[side][3] for side in sides],
        text_out_grad,
        None,
        text_gain_two,
        row_of(text_reduce_bias),
        LANES,
        None,
        "text_resid_back",
    )
    text_back = {}
    for side in (1, 0):
        text_back[side] = attention_backward(
            tie(text_low, units_there) if side == 1 else text_low,
            text_out[side],
            text_attention[side][1],
            text_normed,
            text_qkv[side],
            text_attention[side][0],
            text_attention[side][2],
            text_plan,
            segments,
            "text_attention_back",
        )
    text_flat, text_flat_there = (
        jnp.concatenate(
            [grads.reshape(-1, LANES) for grads in (text_units[side][0], text_back[side][0])]
        )
        for side in sides
    )
    text_flat_there = swap(text_flat_there)
    text_bucket = Steps(bucket_steps, text_flat, text_flat_there)
    units_there = units_bucket.step(text_low)
    text_grads, text_sums_one = text_rows_back(
        text_rows,
        [text_back[side][2] for side in sides],
        text_grad_resid,
        text_gain,
        LANES,
    )
    text_later = lax.ppermute(text_grads[:halo], "tensor", [(1, 0)])
    text_own = text_grads[halo:]
    text_input_grad = jnp.concatenate(
        [text_own[: text_count - halo], text_own[text_count - halo :] + text_later]
    ).astype(BF16)
    video_final, video_grad_resid, video_low, video_sums = resid_back(
        tie(video_resid, units_there, text_flat_there, text_grads),
        [video_units[side][2] for side in sides],
        [video_units[side][3] for side in sides],
        video_cot,
        message_out_grad[0].astype(F32)[:, None],
        video_gain_two,
        row_of(video_reduce_bias),
        frame_rows,
        tokens,
        "video_resid_back",
    )
    video_output = video_final.reshape(1, frames, frame_rows, width)[:, :, :tokens]

    text_there = text_bucket.step()
    units_there = units_bucket.step(video_low)
    video_back = {}
    for side in (1, 0):
        video_back[side] = attention_backward(
            tie(video_low, units_there, text_there) if side == 0 else video_low,
            video_out[side],
            video_attention[side][1],
            video_normed,
            video_qkv[side],
            video_attention[side][0],
            video_attention[side][2],
            video_plan,
            (),
            "video_attention_back",
        )
    video_flat = video_back[0][0].reshape(-1, LANES)
    video_flat_there = swap(video_back[1][0].reshape(-1, LANES))
    video_bucket = Steps(bucket_steps, video_flat, video_flat_there)
    text_there = text_bucket.step(video_back[1][1])
    units_there = units_bucket.step(video_back[1][1])
    video_grads, video_edges, video_sums_one = video_rows_back(
        tie(video_rows, video_flat_there, units_there, text_there),
        [video_back[side][2] for side in sides],
        video_grad_resid,
        video_gain,
        frame_rows,
        tokens,
    )

    arrivals = (text_bucket.step(video_back[0][1]), units_bucket.step(video_back[0][1]))

    token_here = video_edges[:, 1]
    token_there = swap(token_here)
    token_grads = in_order(token_here, token_there)
    message_grads, message_low, class_grads, message_sums = messages_backward(
        messages,
        message_mixed,
        token_grads,
        message_gain,
        message_weight,
        video_message_out_weight,
        video_message_weight,
    )
    class_row = (video_edges[:, 0] + own_part(class_grads, frames)).astype(BF16)
    video_input_grad = (
        video_grads.reshape(frames, frame_rows, width)[:, :tokens].at[:, 0].set(class_row)[None]
    )
    factors = jnp.concatenate(
        [
            class_rows,
            own_part(message_normed, frames),
            own_part(message_attended, frames),
            token_here.astype(BF16),
            own_part(message_low, frames),
        ]
        + [own_part(message_grads[part], frames) for part in range(3)],
        axis=1,
    )
    factor_rows = Steps(gather_steps, factors)
    vectors = [
        video_sums_one[0],
        video_sums_one[1],
        message_sums[4] * 0.5,
        message_sums[2] * 0.5,
        message_sums[3] * 0.5,
        message_sums[0] * 0.5,
        message_sums[1] * 0.5,
        message_sums[5] * 0.5,
        video_sums[3],
        video_sums[1],
        video_sums[2],
        video_sums[0],
        text_sums_one[0],
        text_sums_one[1],
        text_sums[3],
        text_sums[1],
        text_sums[2],
        text_sums[0],
        in_order(video_back[0][1][0], video_back[1][1][0]),
        in_order(video_back[0][1][1], video_back[1][1][1]),
        in_order(video_units[0][1][0], video_units[1][1][0]),
        in_order(text_back[0][1][0], text_back[1][1][0]),
        in_order(text_back[0][1][1], text_back[1][1][1]),
        in_order(text_units[0][1][0], text_units[1][1][0]),
    ]
    vector_sums = Steps(vector_steps, vectors)
    chains = (units_bucket, text_bucket, video_bucket, factor_rows, vector_sums)
    while any(chain.result is None for chain in chains):
        waited = (message_low, arrivals)
        arrivals = tuple(chain.step(*waited) for chain in chains if chain.result is None)
    done = vector_sums.result

    factors = factor_rows.result
    factors = [factors[:, at * width : (at + 1) * width] for at in range(8)]
    contract = functools.partial(jnp.einsum, "rd,re->de", preferred_element_type=F32)
    grad_video_message_weight = contract(factors[0], factors[4])
    grad_video_message_out_weight = contract(factors[2], factors[3])
    grad_video_message_attend_weight = jnp.stack(
        [contract(factors[1], factors[5 + part]) for part in range(3)]
    ).transpose(1, 0, 2)
    grad_video_attend_weight, grad_video_output_weight = unpack_attention(
        video_bucket.result, 0, width, video_attend_weight.shape[2] // LANES, "video_attention_grads"
    )
    text_summed = text_bucket.result
    units = text_expand_weight.shape[1]
    grad_text_expand_weight, grad_text_reduce_weight = unpack_units(
        text_summed, text_width, units, units // TEXT_CHUNKS, "text_units_grads"
    )
    grad_text_attend_weight, grad_text_output_weight = unpack_attention(
        text_summed,
        2 * units // LANES,
        text_width,
        text_attend_weight.shape[2] // LANES,
        "text_attention_grads",
    )
    units = video_expand_weight.shape[1]
    grad_video_expand_weight, grad_video_reduce_weight = unpack_units(
        units_bucket.result, width, units, units // VIDEO_CHUNKS, "video_units_grads"
    )
    half = [own_part(value, value.size // 2) for value in done[18:]]
    return (
        video_output,
        message_output,
        text_final,
        video_input_grad,
        text_input_grad,
        done[0],
        done[1],
        grad_video_message_weight,
        done[2],
        done[3],
        done[4],
        grad_video_message_attend_weight,
        jnp.stack([done[5], done[6]]),
        grad_video_message_out_weight,
        done[7],
        grad_video_attend_weight.transpose(1, 0, 2),
        jnp.stack([half[0], half[1]]),
        grad_video_output_weight,
        done[8],
        done[9],
        done[10],
        grad_video_expand_weight,
        half[2],
        grad_video_reduce_weight,
        done[11],
        done[12],
        done[13],
        grad_text_attend_weight.transpose(1, 0, 2),
        jnp.stack([half[3], half[4]]),
        grad_text_output_weight,
        done[14],
        done[15],
        done[16],
        grad_text_expand_weight,
        half[5],
        grad_text_reduce_weight,
        done[17],
    )


def solution(mesh):
    in_specs = (
        P("dp", "tensor", None, None),
        P(("dp", "tensor"), None),
        P("dp", None),
        P(),
        P(),
        P(),
        P(),
        P(),
        P(),
        P(),
        P(),
        P(),
        P(),
        P(None, None, "tensor"),
        P(None, "tensor"),
        P("tensor", None),
        P(),
        P(),
        P(),
        P(None, "tensor"),
        P("tensor"),
        P("tensor", None),
        P(),
        P(),
        P(),
        P(None, None, "tensor"),
        P(None, "tensor"),
        P("tensor", None),
        P(),
        P(),
        P(),
        P(None, "tensor"),
        P("tensor"),
        P("tensor", None),
        P(),
        P("dp", "tensor", None, None),
        P("dp", "tensor", None),
        P(("dp", "tensor"), None),
    )
    out_specs = (
        P("dp", "tensor", None, None),
        P("dp", "tensor", None),
        P(("dp", "tensor"), None),
        P("dp", "tensor", None, None),
        P(("dp", "tensor"), None),
        P(),
        P(),
        P(),
        P(),
        P(),
        P(),
        P(),
        P(),
        P(),
        P(),
        P(None, None, "tensor"),
        P(None, "tensor"),
        P("tensor", None),
        P(),
        P(),
        P(),
        P(None, "tensor"),
        P("tensor"),
        P("tensor", None),
        P(),
        P(),
        P(),
        P(None, None, "tensor"),
        P(None, "tensor"),
        P("tensor", None),
        P(),
        P(),
        P(),
        P(None, "tensor"),
        P("tensor"),
        P("tensor", None),
        P(),
    )
    return jax.shard_map(
        on_device, mesh=mesh, in_specs=in_specs, out_specs=out_specs, check_vma=False
    )
```

```python
import functools
import jax
import jax.numpy as jnp
from jax import lax
from jax.experimental import pallas as pl
from jax.experimental.pallas import tpu as pltpu
from jax.sharding import PartitionSpec as P

HD = 64
MAXLEN = 77
LANES = 128
VIDEO_CHUNKS = 3
TEXT_CHUNKS = 2
NEGATIVE = -1000000000.0
F32 = jnp.float32
BF16 = jnp.bfloat16
PARAMS = pltpu.CompilerParams(vmem_limit_bytes=60 << 20)


def nt(left, right):
    return lax.dot_general(left, right, (((1,), (1,)), ((), ())), preferred_element_type=F32)


def tn(left, right):
    return lax.dot_general(left, right, (((0,), (0,)), ((), ())), preferred_element_type=F32)


def mm(left, right):
    return jnp.dot(left, right, preferred_element_type=F32)


def unit_of(rows):
    centre = rows - jnp.mean(rows, axis=-1, keepdims=True)
    inverse = lax.rsqrt(jnp.mean(centre * centre, axis=-1, keepdims=True) + 1e-05)
    return centre * inverse, inverse


def norm_back(grad_out, unit_rows, inverse, gain_row):
    scaled = grad_out * gain_row
    return inverse * (
        scaled
        - jnp.mean(scaled, axis=-1, keepdims=True)
        - unit_rows * jnp.mean(scaled * unit_rows, axis=-1, keepdims=True)
    )


def column_sum(values):
    return jnp.sum(values, axis=0, keepdims=True)


def row_is(shape, row):
    return lax.broadcasted_iota(jnp.int32, shape, 0) == row


def low_half():
    return lax.broadcasted_iota(jnp.int32, (1, LANES), 1) < HD


def head_masks():
    first = low_half().astype(F32)
    return first.astype(BF16), (1.0 - first).astype(BF16)


def whole(array):
    return pl.BlockSpec(array.shape, lambda *_: (0,) * array.ndim)


def rows_block(rows, columns, offset=0):
    return pl.BlockSpec((rows, columns), lambda i: (i + offset, 0))


def cost(flops, arrays, outs):
    moved = sum(a.size * a.dtype.itemsize for a in arrays) + sum(
        a.size * jnp.dtype(a.dtype).itemsize for a in outs
    )
    return pl.CostEstimate(flops=int(flops), transcendentals=0, bytes_accessed=int(moved))


def call(body, grid, ins, in_specs, outs, out_specs, scratch=(), flops=0, name=None):
    return pl.pallas_call(
        body,
        grid=grid,
        in_specs=in_specs,
        out_specs=out_specs,
        out_shape=outs,
        scratch_shapes=list(scratch),
        compiler_params=PARAMS,
        cost_estimate=cost(flops, ins, outs),
        name=name,
    )(*ins)


def shape_of(shape, dtype):
    return jax.ShapeDtypeStruct(shape, dtype)


def video_first(frames_rows, tokens, gain, shift, token_row):
    frames, rows, width = frames_rows.shape

    def body(x_ref, token_ref, gain_ref, shift_ref, rows_ref, first_ref):
        x = x_ref[0].astype(F32)
        x = jnp.where(row_is(x.shape, token_row), token_ref[0], x)
        rows_ref[...] = x
        unit, _ = unit_of(x)
        first_ref[...] = (unit * gain_ref[...] + shift_ref[...]).astype(BF16)

    ins = (frames_rows, tokens, gain, shift)
    return call(
        body,
        (frames,),
        ins,
        [
            pl.BlockSpec((1, rows, width), lambda i: (i, 0, 0)),
            pl.BlockSpec((1, 1, width), lambda i: (i, 0, 0)),
            whole(gain),
            whole(shift),
        ],
        [shape_of((frames * rows, width), F32), shape_of((frames * rows, width), BF16)],
        [rows_block(rows, width), rows_block(rows, width)],
        name="video_first",
    )


def text_first(rows_in, gain, shift, block):
    rows, width = rows_in.shape

    def body(x_ref, gain_ref, shift_ref, first_ref):
        unit, _ = unit_of(x_ref[...].astype(F32))
        first_ref[...] = (unit * gain_ref[...] + shift_ref[...]).astype(BF16)

    ins = (rows_in, gain, shift)
    return call(
        body,
        (rows // block,),
        ins,
        [rows_block(block, width), whole(gain), whole(shift)],
        [shape_of((rows, width), BF16)],
        [rows_block(block, width)],
        name="text_first",
    )[0]


def masked(scores, plan, group, segments):
    if plan["keys"] is not None:
        columns = lax.broadcasted_iota(jnp.int32, scores.shape, 1)
        return jnp.where(columns < plan["keys"], scores, NEGATIVE)
    query_start, queries, key_start, keys, _ = group
    column_ref, row_ref = segments
    same = (
        column_ref[query_start : query_start + queries, :]
        == row_ref[:, key_start : key_start + keys]
    )
    columns = lax.broadcasted_iota(jnp.int32, scores.shape, 1) + key_start
    positions = lax.broadcasted_iota(jnp.int32, scores.shape, 0) + query_start
    return jnp.where(same & (columns <= positions), scores, NEGATIVE)


def attention_forward(first, weight, bias, plan, segments, name):
    rows, width = first.shape
    heads_width = weight.shape[2]
    steps = heads_width // LANES
    out_rows = plan["out_rows"]

    def body(x_ref, w_ref, b_ref, *rest):
        segment_refs, (mixed_ref, out_ref, lse_ref, wide_ref) = rest[:-4], rest[-4:]
        for part in range(3):
            wide_ref[:, part * LANES : (part + 1) * LANES] = w_ref[part]
        mixed = mm(x_ref[...], wide_ref[...])
        for part in range(3):
            mixed_ref[part] = (
                mixed[:, part * LANES : (part + 1) * LANES] + b_ref[part : part + 1, :]
            ).astype(BF16)
        masks = head_masks()
        lower = low_half()
        for group in plan["groups"]:
            query_start, queries, key_start, keys, out_start = group
            q = mixed_ref[0, query_start : query_start + queries, :] * jnp.asarray(0.125, BF16)
            k = mixed_ref[1, key_start : key_start + keys, :]
            v = mixed_ref[2, key_start : key_start + keys, :]
            outs, sums = [], []
            for mask in masks:
                scores = masked(nt(q * mask, k), plan, group, segment_refs)
                top = jnp.max(scores, axis=-1, keepdims=True)
                powers = jnp.exp(scores - top)
                total = jnp.sum(powers, axis=-1, keepdims=True)
                probs = (powers * (1.0 / total)).astype(BF16)
                outs.append(mm(probs, v))
                sums.append(top + jnp.log(total))
            out_ref[out_start : out_start + queries, :] = jnp.where(lower, outs[0], outs[1]).astype(
                BF16
            )
            lse_ref[out_start : out_start + queries, :] = jnp.where(lower, sums[0], sums[1])

    ins = (first, weight, bias) + segments
    return call(
        body,
        (steps,),
        ins,
        [
            whole(first),
            pl.BlockSpec((3, width, LANES), lambda i: (0, 0, i)),
            pl.BlockSpec((3, LANES), lambda i: (0, i)),
        ]
        + [whole(s) for s in segments],
        [
            shape_of((3, rows, heads_width), BF16),
            shape_of((out_rows, heads_width), BF16),
            shape_of((out_rows, heads_width), F32),
        ],
        [
            pl.BlockSpec((3, rows, LANES), lambda i: (0, 0, i)),
            pl.BlockSpec((out_rows, LANES), lambda i: (0, i)),
            pl.BlockSpec((out_rows, LANES), lambda i: (0, i)),
        ],
        scratch=[pltpu.VMEM((width, 3 * LANES), BF16)],
        flops=2 * rows * width * 3 * heads_width * 2,
        name=name,
    )


def attention_backward(
    low, out_weight, attended, first, weight, mixed, lse, plan, segments, name
):
    rows, width = first.shape
    out_rows = plan["out_rows"]
    heads_width = weight.shape[2]
    steps = heads_width // LANES
    shared = plan["keys"] is None

    def body(low_ref, ow_ref, att_ref, x_ref, w_ref, mixed_ref, lse_ref, *rest):
        segment_refs = rest[: len(segments)]
        (
            flat_ref,
            bias_ref,
            first_grad_ref,
            wide_ref,
            turned_ref,
            grad_ref,
            key_ref,
            value_ref,
        ) = rest[len(segments) :]
        step = pl.program_id(0)

        @pl.when(step == 0)
        def _():
            turned_ref[...] = x_ref[...].T
            first_grad_ref[...] = jnp.zeros_like(first_grad_ref)

        for part in range(3):
            wide_ref[:, part * LANES : (part + 1) * LANES] = w_ref[part]
        low_rows = low_ref[...]
        grad_out = nt(low_rows, ow_ref[...]).astype(BF16)
        out_grad = tn(att_ref[...], low_rows).astype(BF16)
        for part in range(width // LANES):
            flat_ref[3, 0, part * LANES : (part + 1) * LANES, :] = out_grad[
                :, part * LANES : (part + 1) * LANES
            ]
        if shared:
            grad_ref[...] = jnp.zeros_like(grad_ref)
            key_ref[...] = jnp.zeros_like(key_ref)
            value_ref[...] = jnp.zeros_like(value_ref)
        masks = head_masks()
        lower = low_half()
        for group in plan["groups"]:
            query_start, queries, key_start, keys, out_start = group
            q = mixed_ref[0, query_start : query_start + queries, :] * jnp.asarray(0.125, BF16)
            k = mixed_ref[1, key_start : key_start + keys, :]
            v = mixed_ref[2, key_start : key_start + keys, :]
            g = grad_out[out_start : out_start + queries, :]
            query_grads, key_grad, value_grad = [], None, None
            for head, mask in enumerate(masks):
                query_head, grad_head = q * mask, g * mask
                scores = masked(nt(query_head, k), plan, group, segment_refs)
                column = lse_ref[out_start : out_start + queries, head * HD : head * HD + 1]
                probs = jnp.exp(scores - column)
                grad_probs = nt(grad_head, v)
                dots = jnp.sum(probs * grad_probs, axis=-1, keepdims=True)
                grad_scores = (probs * (grad_probs - dots)).astype(BF16)
                query_grads.append(mm(grad_scores, k))
                key_term = tn(grad_scores, query_head)
                value_term = tn(probs.astype(BF16), grad_head)
                key_grad = key_term if key_grad is None else key_grad + key_term
                value_grad = value_term if value_grad is None else value_grad + value_term
            query_grad = jnp.where(lower, query_grads[0], query_grads[1]) * 0.125
            grad_ref[query_start : query_start + queries, :LANES] = query_grad.astype(BF16)
            span = slice(key_start, key_start + keys)
            if shared:
                key_ref[span, :] += key_grad
                value_ref[span, :] += value_grad
            else:
                grad_ref[span, LANES : 2 * LANES] = key_grad.astype(BF16)
                grad_ref[span, 2 * LANES :] = value_grad.astype(BF16)
        if shared:
            grad_ref[:, LANES : 2 * LANES] = key_ref[...].astype(BF16)
            grad_ref[:, 2 * LANES :] = value_ref[...].astype(BF16)
        grads = grad_ref[...]
        weight_grads = mm(turned_ref[...], grads)
        sums = column_sum(grads.astype(F32))
        for part in range(3):
            flat_ref[part, 0] = weight_grads[:, part * LANES : (part + 1) * LANES].astype(BF16)
        bias_ref[0:1, :] = sums[:, :LANES]
        bias_ref[1:2, :] = sums[:, 2 * LANES :]
        first_grad_ref[...] += nt(grads, wide_ref[...])

    ins = (low, out_weight, attended, first, weight, mixed, lse) + segments
    return call(
        body,
        (steps,),
        ins,
        [
            whole(low),
            pl.BlockSpec((LANES, width), lambda i: (i, 0)),
            pl.BlockSpec((out_rows, LANES), lambda i: (0, i)),
            whole(first),
            pl.BlockSpec((3, width, LANES), lambda i: (0, 0, i)),
            pl.BlockSpec((3, rows, LANES), lambda i: (0, 0, i)),
            pl.BlockSpec((out_rows, LANES), lambda i: (0, i)),
        ]
        + [whole(s) for s in segments],
        [
            shape_of((4, steps, width, LANES), BF16),
            shape_of((2, heads_width), F32),
            shape_of((rows, width), F32),
        ],
        [
            pl.BlockSpec((4, 1, width, LANES), lambda i: (0, i, 0, 0)),
            pl.BlockSpec((2, LANES), lambda i: (0, i)),
            pl.BlockSpec((rows, width), lambda i: (0, 0)),
        ],
        scratch=[
            pltpu.VMEM((width, 3 * LANES), BF16),
            pltpu.VMEM((width, rows), BF16),
            pltpu.VMEM((rows, 3 * LANES), BF16),
            pltpu.VMEM((rows, LANES), F32),
            pltpu.VMEM((rows, LANES), F32),
        ],
        flops=2 * rows * width * 8 * heads_width * 2,
        name=name,
    )


def project_norm(parts, weights, rows_in, bias, gain, shift, block, offset, name):
    out_rows, half = parts[0].shape
    width = bias.shape[1]

    def body(a_ref, b_ref, wa_ref, wb_ref, rows_ref, bias_ref, gain_ref, shift_ref, res_ref, out_ref):
        resid = (
            rows_ref[...].astype(F32)
            + mm(a_ref[...], wa_ref[...])
            + mm(b_ref[...], wb_ref[...])
            + bias_ref[...]
        )
        res_ref[...] = resid
        unit, _ = unit_of(resid)
        out_ref[...] = (unit * gain_ref[...] + shift_ref[...]).astype(BF16)

    ins = (*parts, *weights, rows_in, bias, gain, shift)
    return call(
        body,
        (out_rows // block,),
        ins,
        [
            rows_block(block, half),
            rows_block(block, half),
            whole(weights[0]),
            whole(weights[1]),
            rows_block(block, width, offset),
            whole(bias),
            whole(gain),
            whole(shift),
        ],
        [shape_of((out_rows, width), F32), shape_of((out_rows, width), BF16)],
        [rows_block(block, width), rows_block(block, width)],
        flops=4 * out_rows * half * width,
        name=name,
    )


def feed_forward(second, cot, expand, expand_bias, reduce, chunk, flat, name):
    rows, width = second.shape
    units = expand.shape[1]
    size = width * chunk // LANES

    def body(x_ref, cot_ref, e_ref, b_ref, r_ref, *rest):
        *grad_refs, gb_ref, out_ref, back_ref, turned_ref = rest

        @pl.when(pl.program_id(0) == 0)
        def _():
            turned_ref[...] = x_ref[...].T
            out_ref[...] = jnp.zeros_like(out_ref)
            back_ref[...] = jnp.zeros_like(back_ref)

        cot_rows = cot_ref[...]
        hidden = mm(x_ref[...], e_ref[...]) + b_ref[...]
        grad_active = nt(cot_rows, r_ref[...])
        logistic = 1.0 / (1.0 + jnp.exp(-1.702 * hidden))
        active = (hidden * logistic).astype(BF16)
        slope = logistic + 1.702 * hidden * logistic * (1.0 - logistic)
        grad_hidden = grad_active * slope
        grad_low = grad_hidden.astype(BF16)
        gb_ref[...] = column_sum(grad_low.astype(F32))
        out_ref[...] += mm(active, r_ref[...])
        back_ref[...] += nt(grad_low, e_ref[...])
        reduce_grad = tn(active, cot_rows).astype(BF16)
        expand_grad = mm(turned_ref[...], grad_low).astype(BF16)
        if not flat:
            grad_refs[0][...] = expand_grad
            grad_refs[1][...] = reduce_grad
            return
        for part in range(chunk // LANES):
            grad_refs[0][0, 0, part * width : (part + 1) * width, :] = expand_grad[
                :, part * LANES : (part + 1) * LANES
            ]
        for part in range(width // LANES):
            grad_refs[0][1, 0, part * chunk : (part + 1) * chunk, :] = reduce_grad[
                :, part * LANES : (part + 1) * LANES
            ]

    if flat:
        grads = [shape_of((2, units // chunk, size, LANES), BF16)]
        grad_specs = [pl.BlockSpec((2, 1, size, LANES), lambda i: (0, i, 0, 0))]
    else:
        grads = [shape_of((width, units), BF16), shape_of((units, width), BF16)]
        grad_specs = [
            pl.BlockSpec((width, chunk), lambda i: (0, i)),
            pl.BlockSpec((chunk, width), lambda i: (i, 0)),
        ]
    ins = (second, cot, expand, expand_bias, reduce)
    return call(
        body,
        (units // chunk,),
        ins,
        [
            whole(second),
            whole(cot),
            pl.BlockSpec((width, chunk), lambda i: (0, i)),
            pl.BlockSpec((1, chunk), lambda i: (0, i)),
            pl.BlockSpec((chunk, width), lambda i: (i, 0)),
        ],
        grads
        + [
            shape_of((1, units), F32),
            shape_of((rows, width), F32),
            shape_of((rows, width), F32),
        ],
        grad_specs
        + [
            pl.BlockSpec((1, chunk), lambda i: (0, i)),
            pl.BlockSpec((rows, width), lambda i: (0, 0)),
            pl.BlockSpec((rows, width), lambda i: (0, 0)),
        ],
        scratch=[pltpu.VMEM((width, rows), BF16)],
        flops=12 * rows * width * units,
        name=name,
    )


def resid_back(resid, outs, backs, cot, token_grads, gain, reduce_bias, block, token_row, name):
    rows, width = resid.shape

    def body(res_ref, oa_ref, ob_ref, ba_ref, bb_ref, cot_ref, *rest):
        if token_row is None:
            gain_ref, rb_ref, final_ref, grad_ref, low_ref, sums_ref = rest
        else:
            token_ref, gain_ref, rb_ref, final_ref, grad_ref, low_ref, sums_ref = rest

        @pl.when(pl.program_id(0) == 0)
        def _():
            sums_ref[...] = jnp.zeros_like(sums_ref)

        resid_rows = res_ref[...]
        final_ref[...] = (resid_rows + oa_ref[...] + ob_ref[...] + rb_ref[...]).astype(BF16)
        back = ba_ref[...] + bb_ref[...]
        unit, inverse = unit_of(resid_rows)
        cot_rows = cot_ref[...].astype(F32)
        sums_ref[0:1, :] += column_sum(cot_rows)
        sums_ref[1:2, :] += column_sum(back * unit)
        sums_ref[2:3, :] += column_sum(back)
        if token_row is not None:
            cot_rows = jnp.where(row_is(cot_rows.shape, token_row), token_ref[0], cot_rows)
        grad = cot_rows + norm_back(back, unit, inverse, gain_ref[...])
        sums_ref[3:4, :] += column_sum(grad)
        grad_ref[...] = grad
        low_ref[...] = grad.astype(BF16)

    ins = (resid, *outs, *backs, cot)
    specs = [rows_block(block, width)] * 6
    if token_row is not None:
        ins += (token_grads,)
        specs.append(pl.BlockSpec((1, 1, width), lambda i: (i, 0, 0)))
    ins += (gain, reduce_bias)
    specs += [whole(gain), whole(reduce_bias)]
    return call(
        body,
        (rows // block,),
        ins,
        specs,
        [
            shape_of((rows, width), BF16),
            shape_of((rows, width), F32),
            shape_of((rows, width), BF16),
            shape_of((4, width), F32),
        ],
        [rows_block(block, width)] * 3 + [pl.BlockSpec((4, width), lambda i: (0, 0))],
        name=name,
    )


def video_rows_back(rows_in, firsts, grad_resid, gain, block, token_row):
    rows, width = rows_in.shape
    frames = rows // block

    def body(rows_ref, fa_ref, fb_ref, grad_ref, gain_ref, out_ref, edge_ref, sums_ref):
        @pl.when(pl.program_id(0) == 0)
        def _():
            sums_ref[...] = jnp.zeros_like(sums_ref)

        unit, inverse = unit_of(rows_ref[...])
        back = fa_ref[...] + fb_ref[...]
        sums_ref[0:1, :] += column_sum(back * unit)
        sums_ref[1:2, :] += column_sum(back)
        grad = grad_ref[...] + norm_back(back, unit, inverse, gain_ref[...])
        out_ref[...] = grad.astype(BF16)
        edge_ref[0, 0:1, :] = grad[0:1, :]
        edge_ref[0, 1:2, :] = grad[token_row : token_row + 1, :]

    ins = (rows_in, *firsts, grad_resid, gain)
    return call(
        body,
        (frames,),
        ins,
        [rows_block(block, width)] * 4 + [whole(gain)],
        [
            shape_of((rows, width), BF16),
            shape_of((frames, 2, width), F32),
            shape_of((2, width), F32),
        ],
        [
            rows_block(block, width),
            pl.BlockSpec((1, 2, width), lambda i: (i, 0, 0)),
            pl.BlockSpec((2, width), lambda i: (0, 0)),
        ],
        name="video_rows_back",
    )


def text_rows_back(rows_in, firsts, grad_resid, gain, block):
    rows, width = rows_in.shape
    ahead = (rows - grad_resid.shape[0]) // block

    def body(rows_ref, fa_ref, fb_ref, grad_ref, gain_ref, out_ref, sums_ref):
        step = pl.program_id(0)

        @pl.when(step == 0)
        def _():
            sums_ref[...] = jnp.zeros_like(sums_ref)

        unit, inverse = unit_of(rows_ref[...].astype(F32))
        back = fa_ref[...] + fb_ref[...]
        sums_ref[0:1, :] += column_sum(back * unit)
        sums_ref[1:2, :] += column_sum(back)
        own = jnp.where(step >= ahead, 1.0, 0.0)
        out_ref[...] = grad_ref[...] * own + norm_back(back, unit, inverse, gain_ref[...])

    ins = (rows_in, *firsts, grad_resid, gain)
    return call(
        body,
        (rows // block,),
        ins,
        [rows_block(block, width)] * 3
        + [
            pl.BlockSpec((block, width), lambda i: (jnp.maximum(i - ahead, 0), 0)),
            whole(gain),
        ],
        [shape_of((rows, width), F32), shape_of((2, width), F32)],
        [rows_block(block, width), pl.BlockSpec((2, width), lambda i: (0, 0))],
        name="text_rows_back",
    )


def head_rows(values, heads):
    lanes = lax.broadcasted_iota(jnp.int32, values.shape, 1) // HD
    return jnp.concatenate(
        [jnp.where(lanes == head, values, 0.0) for head in range(heads)], axis=0
    ).astype(BF16)


def fold_heads(values, heads, rows):
    lanes = lax.broadcasted_iota(jnp.int32, (rows, values.shape[1]), 1) // HD
    total = jnp.zeros((rows, values.shape[1]), F32)
    for head in range(heads):
        total = total + jnp.where(lanes == head, values[head * rows : (head + 1) * rows], 0.0)
    return total


def message_probs(mixed_ref, heads):
    query_rows = head_rows(mixed_ref[0].astype(F32) * 0.125, heads)
    scores = nt(query_rows, mixed_ref[1])
    top = jnp.max(scores, axis=-1, keepdims=True)
    powers = jnp.exp(scores - top)
    return query_rows, powers * (1.0 / jnp.sum(powers, axis=-1, keepdims=True))


def messages_forward(messages, gain, shift, weight, bias, out_weight, out_bias):
    rows, width = messages.shape
    heads = width // HD

    def body(m_ref, gain_ref, shift_ref, w_ref, b_ref, ow_ref, ob_ref, n_ref, mixed_ref, a_ref, t_ref):
        messages_now = m_ref[...]
        unit, _ = unit_of(messages_now)
        normed = (unit * gain_ref[...] + shift_ref[...]).astype(BF16)
        n_ref[...] = normed
        for part in range(3):
            mixed_ref[part] = (mm(normed, w_ref[part]) + b_ref[part : part + 1, :]).astype(BF16)
        _, probs = message_probs(mixed_ref, heads)
        attended = fold_heads(mm(probs.astype(BF16), mixed_ref[2]), heads, rows).astype(BF16)
        a_ref[...] = attended
        t_ref[...] = messages_now + mm(attended, ow_ref[...]) + ob_ref[...]

    ins = (messages, gain, shift, weight, bias, out_weight, out_bias)
    outs = [
        shape_of((rows, width), BF16),
        shape_of((3, rows, width), BF16),
        shape_of((rows, width), BF16),
        shape_of((rows, width), F32),
    ]
    return call(
        body, (1,), ins, [whole(a) for a in ins], outs, [whole(o) for o in outs], name="messages"
    )


def messages_backward(messages, mixed, token_grads, gain, weight, out_weight, in_weight):
    rows, width = messages.shape
    heads = width // HD

    def body(m_ref, mixed_ref, t_ref, gain_ref, w_ref, ow_ref, iw_ref, g_ref, low_ref, c_ref, s_ref):
        token = t_ref[...]
        grad_attended = nt(token.astype(BF16), ow_ref[...]).astype(BF16)
        query_rows, probs = message_probs(mixed_ref, heads)
        grad_rows = head_rows(grad_attended.astype(F32), heads)
        grad_probs = nt(grad_rows, mixed_ref[2])
        dots = jnp.sum(probs * grad_probs, axis=-1, keepdims=True)
        grad_scores = (probs * (grad_probs - dots)).astype(BF16)
        grads = (
            fold_heads(mm(grad_scores, mixed_ref[1]), heads, rows) * 0.125,
            tn(grad_scores, query_rows),
            tn(probs.astype(BF16), grad_rows),
        )
        normed_grad = jnp.zeros((rows, width), F32)
        for part in range(3):
            low = grads[part].astype(BF16)
            g_ref[part] = low
            normed_grad = normed_grad + nt(low, w_ref[part])
        s_ref[0:1, :] = column_sum(g_ref[0].astype(F32))
        s_ref[1:2, :] = column_sum(g_ref[2].astype(F32))
        unit, inverse = unit_of(m_ref[...])
        s_ref[2:3, :] = column_sum(normed_grad * unit)
        s_ref[3:4, :] = column_sum(normed_grad)
        grad = token + norm_back(normed_grad, unit, inverse, gain_ref[...])
        s_ref[4:5, :] = column_sum(grad)
        s_ref[5:6, :] = column_sum(token)
        low = grad.astype(BF16)
        low_ref[...] = low
        c_ref[...] = nt(low, iw_ref[...])

    ins = (messages, mixed, token_grads, gain, weight, out_weight, in_weight)
    outs = [
        shape_of((3, rows, width), BF16),
        shape_of((rows, width), BF16),
        shape_of((rows, width), F32),
        shape_of((6, width), F32),
    ]
    return call(
        body,
        (1,),
        ins,
        [whole(a) for a in ins],
        outs,
        [whole(o) for o in outs],
        name="messages_back",
    )


def swap(value):
    return lax.ppermute(value, "tensor", [(0, 1), (1, 0)])


def in_order(own, other, axis=0):
    first = lax.axis_index("tensor") == 0
    return jnp.where(
        first, jnp.concatenate([own, other], axis), jnp.concatenate([other, own], axis)
    )


def own_part(values, size, axis=0):
    return lax.dynamic_slice_in_dim(values, lax.axis_index("tensor") * size, size, axis)


def row_of(vector):
    return vector.astype(F32).reshape(1, -1)


def qkv_bias(flat):
    rows = flat.astype(F32).reshape(2, -1)
    return jnp.stack([rows[0], jnp.zeros_like(rows[0]), rows[1]])


def exchange(value, away):
    size = lax.axis_size("dp")
    return lax.ppermute(value, "dp", [(at, at ^ away) for at in range(size)])


def bit_of(bit):
    return (lax.axis_index("dp") >> bit) & 1


def add(*values):
    return sum(value.astype(F32) for value in values).astype(BF16)


def dp_bits():
    return lax.axis_size("dp").bit_length() - 1


def by_bit(own, other, mine):
    return jnp.where(
        mine == 0, jnp.concatenate([own, other], 0), jnp.concatenate([other, own], 0)
    )


class Steps:
    def __init__(self, make, *ins):
        self.after = ()
        self.steps = make(self, *ins)
        self.result = None

    def step(self, *after):
        self.after = after
        try:
            return next(self.steps)
        except StopIteration as stop:
            self.result = stop.value
            return ()

    def hold(self, values):
        return tie(values, self.after) if self.after else values


def tie(value, *waited):
    return lax.optimization_barrier((value, waited))[0]


def take(rows, part, size):
    return lax.dynamic_slice_in_dim(rows, part * size, size)


def bucket_steps(steps, own, received):
    orders = (0, 1), (1, 0)
    bits = [bit_of(bit) for bit in orders[0]]
    parts = [
        [mine.reshape(-1, LANES), theirs.reshape(-1, LANES)] for mine, theirs in zip(own, received)
    ]
    for at in range(2):
        kept, arrived = [], []
        for values, order in zip(parts, orders):
            size = values[0].shape[0] // 2
            mine = bits[order[at]]
            send = [take(value, 1 - mine, size) for value in values]
            kept.append([take(value, mine, size) for value in values])
            arrived.append(exchange(add(*send) if at == 0 else send[0], 1 << order[at]))
        yield arrived
        arrived = steps.hold(arrived)
        parts = [[add(*keep, there)] for keep, there in zip(kept, arrived)]
    first = parts[0][0].shape[0]
    rows = jnp.concatenate([values[0] for values in parts])
    count = lax.axis_size("dp") // 4
    here = lax.axis_index("dp") >> 2
    size = rows.shape[0] // count
    arrived = [exchange(take(rows, here ^ away, size), away << 2) for away in range(1, count)]
    yield arrived
    arrived = steps.hold(arrived)
    rows = add(take(rows, here, size), *arrived)
    arrived = [exchange(rows, away << 2) for away in range(1, count)]
    yield arrived
    arrived = steps.hold(arrived)
    pieces = jnp.concatenate([rows] + arrived)
    rows = jnp.concatenate([take(pieces, at ^ here, size) for at in range(count)])
    parts = [rows[:first], rows[first:]]
    for at in (1, 0):
        arrived = [exchange(value, 1 << order[at]) for value, order in zip(parts, orders)]
        yield arrived
        arrived = steps.hold(arrived)
        parts = [jnp.concatenate(pair) for pair in zip(parts, arrived)]
    return [
        (part, (bits[one] * 2 + bits[two]).reshape(1)) for part, (one, two) in zip(parts, orders)
    ]


def place(at, blocks, here_ref):
    part = blocks // 4
    return ((at // part) ^ here_ref[0]) * part + at % part, 0


def pack_vectors(common, own, other):
    rows = sum(value.size for value in common + own) // LANES

    def body(*refs):
        ins, outs = refs[:-2], refs[-2:]
        counts = len(common), len(common) + len(own)
        for out, parts in zip(outs, (ins[: counts[1]], ins[: counts[0]] + ins[counts[1] :])):
            begin = 0
            for ref in parts:
                across = ref.shape[1] // LANES
                for row in range(ref.shape[0]):
                    for part in range(across):
                        out[begin : begin + 1, :] = ref[
                            row : row + 1, part * LANES : (part + 1) * LANES
                        ]
                        begin += 1

    ins = (*common, *own, *other)
    outs = [shape_of((rows, LANES), F32)] * 2
    return call(
        body, (1,), ins, [whole(a) for a in ins], outs, [whole(o) for o in outs], name="vectors"
    )


def vector_steps(steps, common, own, other):
    total, send = pack_vectors(common, own, other)
    there = swap(send)
    yield there
    total = total + steps.hold(there)
    for bit in range(dp_bits()):
        there = exchange(total, 1 << bit)
        yield there
        total = total + steps.hold(there)
    total = total.reshape(-1)
    done = []
    begin = 0
    for value in common + own:
        done.append(total[begin : begin + value.size].reshape(value.shape))
        begin += value.size
    return done


def gather_steps(steps, values):
    for bit in reversed(range(dp_bits())):
        there = exchange(values, 1 << bit)
        yield there
        values = by_bit(values, steps.hold(there), bit_of(bit))
    there = swap(values)
    yield there
    return in_order(values, steps.hold(there))


def unpack_units(summed, width, units, chunk, name):
    rows, here = summed
    block = width
    blocks = rows.shape[0] // block
    across = width // (2 * LANES)
    steps = units // (2 * LANES)

    def body(here_ref, *refs):
        for at in range(2):
            span = slice(at * LANES, (at + 1) * LANES)
            refs[4][:, span] = refs[at][...].astype(F32)
            refs[5][:, span] = refs[2 + at][...].astype(F32)

    def in_spec(at):
        begin = blocks // 2 * (at // 2) + at % 2
        return pl.BlockSpec(
            (block, LANES), lambda i, here_ref: place(begin + 2 * i, blocks, here_ref)
        )

    outs = [shape_of((width, units), F32), shape_of((units, width), F32)]
    return pl.pallas_call(
        body,
        grid_spec=pltpu.PrefetchScalarGridSpec(
            num_scalar_prefetch=1,
            grid=(steps,),
            in_specs=[in_spec(at) for at in range(4)],
            out_specs=[
                pl.BlockSpec((width, 2 * LANES), lambda i, here_ref: (0, i)),
                pl.BlockSpec((chunk, 2 * LANES), lambda i, here_ref: (i // across, i % across)),
            ],
        ),
        out_shape=outs,
        compiler_params=PARAMS,
        cost_estimate=cost(0, (rows,), outs),
        name=name,
    )(here, *([rows] * 4))


def unpack_attention(summed, width, steps, name):
    rows, here = summed
    block = width // 2
    blocks = rows.shape[0] // block

    def body(here_ref, *refs):
        attend_ref, out_ref = refs[8:]
        for at in range(8):
            values = refs[at][...].astype(F32)
            start = at % 2 * block
            if at < 6:
                attend_ref[at // 2, start : start + block, :] = values
                continue
            for part in range(block // LANES):
                begin = start + part * LANES
                out_ref[:, begin : begin + LANES] = values[part * LANES : (part + 1) * LANES, :]

    def in_spec(at):
        return pl.BlockSpec(
            (block, LANES),
            lambda i, here_ref: place(
                (at // 2 * steps + i) * 2 + at % 2, blocks, here_ref
            ),
        )

    outs = [shape_of((3, width, steps * LANES), F32), shape_of((steps * LANES, width), F32)]
    return pl.pallas_call(
        body,
        grid_spec=pltpu.PrefetchScalarGridSpec(
            num_scalar_prefetch=1,
            grid=(steps,),
            in_specs=[in_spec(at) for at in range(8)],
            out_specs=[
                pl.BlockSpec((3, width, LANES), lambda i, here_ref: (0, 0, i)),
                pl.BlockSpec((LANES, width), lambda i, here_ref: (i, 0)),
            ],
        ),
        out_shape=outs,
        compiler_params=PARAMS,
        cost_estimate=cost(0, (rows,), outs),
        name=name,
    )(here, *([rows] * 8))


def on_device(
    video_input,
    text_input,
    caption_lengths,
    video_first_gain,
    video_first_shift,
    video_message_weight,
    video_message_bias,
    video_message_gain,
    video_message_shift,
    video_message_attend_weight,
    video_message_attend_bias,
    video_message_out_weight,
    video_message_out_bias,
    video_attend_weight,
    video_attend_bias,
    video_output_weight,
    video_output_bias,
    video_final_gain,
    video_final_shift,
    video_expand_weight,
    video_expand_bias,
    video_reduce_weight,
    video_reduce_bias,
    text_first_gain,
    text_first_shift,
    text_attend_weight,
    text_attend_bias,
    text_output_weight,
    text_output_bias,
    text_final_gain,
    text_final_shift,
    text_expand_weight,
    text_expand_bias,
    text_reduce_weight,
    text_reduce_bias,
    video_out_grad,
    message_out_grad,
    text_out_grad,
):
    core = lax.axis_index("tensor")
    frames, tokens, width = video_input.shape[1:]
    frame_rows = -(-(tokens + 1) // 16) * 16
    spare = ((0, 0), (0, frame_rows - tokens), (0, 0))
    text_count, text_width = text_input.shape
    halo = -(-(MAXLEN - 1) // LANES) * LANES

    class_rows = video_input[0, :, 0, :]
    messages_here = (
        jnp.dot(class_rows, video_message_weight, preferred_element_type=F32)
        + video_message_bias.astype(F32)
    )
    messages_there = swap(messages_here)
    text_qkv = (text_attend_weight.transpose(1, 0, 2),)
    video_qkv = (video_attend_weight.transpose(1, 0, 2),)
    small = (video_attend_bias, video_expand_bias, text_attend_bias, text_expand_bias)
    packed = jnp.concatenate([value.reshape(-1) for value in small])
    packed_there = swap(packed)
    biases = []
    begin = 0
    for value in small:
        biases.append((packed[begin : begin + value.size], packed_there[begin : begin + value.size]))
        begin += value.size
    text_ahead = lax.ppermute(text_input[text_count - halo :], "tensor", [(0, 1)])
    text_qkv += (swap(text_qkv[0]),)
    video_qkv += (swap(video_qkv[0]),)
    text_out = (text_output_weight, swap(text_output_weight))
    video_out = (video_output_weight, swap(video_output_weight))
    video_expand = (video_expand_weight, swap(video_expand_weight))
    video_reduce = (video_reduce_weight, swap(video_reduce_weight))
    text_expand = (text_expand_weight, swap(text_expand_weight))
    text_reduce = (text_reduce_weight, swap(text_reduce_weight))
    video_qkv_bias = [qkv_bias(flat) for flat in biases[0]]
    text_qkv_bias = [qkv_bias(flat) for flat in biases[2]]
    sides = (0, 1)

    messages = in_order(messages_here, messages_there)
    message_weight = video_message_attend_weight.transpose(1, 0, 2)
    message_gain = row_of(video_message_gain)
    message_normed, message_mixed, message_attended, message_tokens = messages_forward(
        messages,
        message_gain,
        row_of(video_message_shift),
        message_weight,
        qkv_bias(video_message_attend_bias),
        video_message_out_weight,
        row_of(video_message_out_bias),
    )
    tokens_here = own_part(message_tokens, frames)

    video_gain, video_gain_two = row_of(video_first_gain), row_of(video_final_gain)
    video_rows, video_normed = video_first(
        jnp.pad(video_input[0], spare),
        tokens_here[:, None],
        video_gain,
        row_of(video_first_shift),
        tokens,
    )
    video_plan = {
        "groups": [
            (start, frame_rows, start, frame_rows, start)
            for start in range(0, frames * frame_rows, frame_rows)
        ],
        "keys": tokens + 1,
        "out_rows": frames * frame_rows,
    }
    video_attention = [
        attention_forward(
            video_normed, video_qkv[side], video_qkv_bias[side], video_plan, (), "video_attention"
        )
        for side in sides
    ]
    video_resid, video_second = project_norm(
        [video_attention[side][1] for side in sides],
        video_out,
        video_rows,
        row_of(video_output_bias),
        video_gain_two,
        row_of(video_final_shift),
        frame_rows,
        0,
        "video_project",
    )
    message_output = video_resid.reshape(frames, frame_rows, width)[:, tokens].astype(BF16)[None]

    video_cot = jnp.pad(video_out_grad[0], spare).reshape(-1, width)
    video_units = {}
    for side in (1, 0):
        video_units[side] = feed_forward(
            video_second,
            video_cot,
            video_expand[side],
            row_of(biases[1][side]),
            video_reduce[side],
            video_expand[side].shape[1] // VIDEO_CHUNKS,
            False,
            "video_units",
        )
    video_units_sums = tuple(
        add(mine, swap(theirs)) for mine, theirs in zip(video_units[0][:2], video_units[1][:2])
    )

    video_final, video_grad_resid, video_low, video_sums = resid_back(
        tie(video_resid, video_units_sums),
        [video_units[side][-2] for side in sides],
        [video_units[side][-1] for side in sides],
        video_cot,
        message_out_grad[0].astype(F32)[:, None],
        video_gain_two,
        row_of(video_reduce_bias),
        frame_rows,
        tokens,
        "video_resid_back",
    )
    video_output = video_final.reshape(1, frames, frame_rows, width)[:, :, :tokens]

    video_back = {}
    for side in (1, 0):
        video_back[side] = attention_backward(
            video_low,
            video_out[side],
            video_attention[side][1],
            video_normed,
            video_qkv[side],
            video_attention[side][0],
            video_attention[side][2],
            video_plan,
            (),
            "video_attention_back",
        )
    video_flat = add(
        video_back[0][0].reshape(-1, LANES), swap(video_back[1][0].reshape(-1, LANES))
    )
    video_sum = lax.psum((*video_units_sums, video_flat), "dp")
    video_grads, video_edges, video_sums_one = video_rows_back(
        tie(video_rows, video_flat),
        [video_back[side][2] for side in sides],
        video_grad_resid,
        video_gain,
        frame_rows,
        tokens,
    )

    token_here = video_edges[:, 1]
    token_there = swap(token_here)
    token_grads = in_order(token_here, token_there)
    message_grads, message_low, class_grads, message_sums = messages_backward(
        messages,
        message_mixed,
        token_grads,
        message_gain,
        message_weight,
        video_message_out_weight,
        video_message_weight,
    )
    class_row = (video_edges[:, 0] + own_part(class_grads, frames)).astype(BF16)
    video_input_grad = (
        video_grads.reshape(frames, frame_rows, width)[:, :tokens].at[:, 0].set(class_row)[None]
    )
    factors = jnp.concatenate(
        [
            class_rows,
            own_part(message_normed, frames),
            own_part(message_attended, frames),
            token_here.astype(BF16),
            own_part(message_low, frames),
        ]
        + [own_part(message_grads[part], frames) for part in range(3)],
        axis=1,
    )
    def apart():
        factor_rows = Steps(gather_steps, factors)
        text_rows = jnp.concatenate([text_ahead, text_input])
        rows_all = text_count + halo
        caption_ends = jnp.cumsum(caption_lengths[0])
        positions = core * text_count - halo + jnp.arange(rows_all, dtype=jnp.int32)
        segment = jnp.sum((positions[:, None] >= caption_ends[None, :]).astype(jnp.int32), axis=1)
        segment = jnp.where(positions < 0, -1, segment)
        segments = (segment.reshape(-1, 1), segment.reshape(1, -1))
        text_plan = {
            "groups": [
                (halo + start, LANES, start, halo + LANES, start)
                for start in range(0, text_count, LANES)
            ],
            "keys": None,
            "out_rows": text_count,
        }
        text_gain, text_gain_two = row_of(text_first_gain), row_of(text_final_gain)
        text_normed = text_first(
            tie(text_rows, message_low), text_gain, row_of(text_first_shift), LANES
        )
        text_attention = {}
        for side in (0, 1):
            text_attention[side] = attention_forward(
                text_normed,
                text_qkv[side],
                text_qkv_bias[side],
                text_plan,
                segments,
                "text_attention",
            )
        text_resid, text_second = project_norm(
            [text_attention[side][1] for side in sides],
            text_out,
            text_rows,
            row_of(text_output_bias),
            text_gain_two,
            row_of(text_final_shift),
            LANES,
            halo // LANES,
            "text_project",
        )
        text_units = {}
        for side in (1, 0):
            text_units[side] = feed_forward(
                text_second,
                text_out_grad,
                text_expand[side],
                row_of(biases[3][side]),
                text_reduce[side],
                text_expand[side].shape[1] // TEXT_CHUNKS,
                True,
                "text_units",
            )
        text_there = swap(text_units[1][0])
        text_final, text_grad_resid, text_low, text_sums = resid_back(
            text_resid,
            [text_units[side][2] for side in sides],
            [text_units[side][3] for side in sides],
            text_out_grad,
            None,
            text_gain_two,
            row_of(text_reduce_bias),
            LANES,
            None,
            "text_resid_back",
        )
        text_back = {}
        for side in (1, 0):
            text_back[side] = attention_backward(
                text_low,
                text_out[side],
                text_attention[side][1],
                text_normed,
                text_qkv[side],
                text_attention[side][0],
                text_attention[side][2],
                text_plan,
                segments,
                "text_attention_back",
            )
        text_bucket = Steps(
            bucket_steps, [text_units[0][0], text_back[0][0]], [text_there, swap(text_back[1][0])]
        )
        text_grads, text_sums_one = text_rows_back(
            text_rows,
            [text_back[side][2] for side in sides],
            text_grad_resid,
            text_gain,
            LANES,
        )
        text_later = lax.ppermute(text_grads[:halo], "tensor", [(1, 0)])
        text_own = text_grads[halo:]
        text_input_grad = jnp.concatenate(
            [text_own[: text_count - halo], text_own[text_count - halo :] + text_later]
        ).astype(BF16)
        vector_sums = Steps(
            vector_steps,
            [video_sums_one, video_sums, message_sums * 0.5, text_sums_one, text_sums],
            *(
                [video_back[side][1], video_units[side][2], text_back[side][1], text_units[side][1]]
                for side in sides
            ),
        )
        chains = (text_bucket, factor_rows, vector_sums)
        arrivals = ()
        while any(chain.result is None for chain in chains):
            waited = (text_grads, arrivals)
            arrivals = tuple(chain.step(*waited) for chain in chains if chain.result is None)
        done = vector_sums.result

        gathered = factor_rows.result
        gathered = [gathered[:, at * width : (at + 1) * width] for at in range(8)]
        contract = functools.partial(jnp.einsum, "rd,re->de", preferred_element_type=F32)
        grad_video_message_weight = contract(gathered[0], gathered[4])
        grad_video_message_out_weight = contract(gathered[2], gathered[3])
        grad_video_message_attend_weight = jnp.stack(
            [contract(gathered[1], gathered[5 + part]) for part in range(3)]
        ).transpose(1, 0, 2)
        text_summed = text_bucket.result
        units = text_expand_weight.shape[1]
        grad_text_expand_weight, grad_text_reduce_weight = unpack_units(
            text_summed[0], text_width, units, units // TEXT_CHUNKS, "text_units_grads"
        )
        grad_text_attend_weight, grad_text_output_weight = unpack_attention(
            text_summed[1],
            text_width,
            text_attend_weight.shape[2] // LANES,
            "text_attention_grads",
        )
        return (
            text_final,
            text_input_grad,
            done,
            grad_video_message_weight,
            grad_video_message_out_weight,
            grad_video_message_attend_weight,
            grad_text_expand_weight,
            grad_text_reduce_weight,
            grad_text_attend_weight,
            grad_text_output_weight,
        )

    def never():
        return jax.tree.map(lambda like: jnp.zeros(like.shape, like.dtype), jax.eval_shape(apart))

    (
        text_final,
        text_input_grad,
        done,
        grad_video_message_weight,
        grad_video_message_out_weight,
        grad_video_message_attend_weight,
        grad_text_expand_weight,
        grad_text_reduce_weight,
        grad_text_attend_weight,
        grad_text_output_weight,
    ) = lax.cond(lax.optimization_barrier(jnp.bool_(True)), apart, never)
    grad_video_attend_weight, grad_video_output_weight = unpack_attention(
        (video_sum[2], jnp.zeros(1, jnp.int32)), width, video_attend_weight.shape[2] // LANES, "video_attention_grads"
    )
    grad_video_expand_weight, grad_video_reduce_weight = [
        value.astype(F32) for value in video_sum[:2]
    ]
    first_sums, sums, token_sums, text_first_sums, text_final_sums, *unit_sums = done
    return (
        video_output,
        message_output,
        text_final,
        video_input_grad,
        text_input_grad,
        first_sums[0],
        first_sums[1],
        grad_video_message_weight,
        token_sums[4],
        token_sums[2],
        token_sums[3],
        grad_video_message_attend_weight,
        token_sums[:2],
        grad_video_message_out_weight,
        token_sums[5],
        grad_video_attend_weight.transpose(1, 0, 2),
        unit_sums[0],
        grad_video_output_weight,
        sums[3],
        sums[1],
        sums[2],
        grad_video_expand_weight,
        unit_sums[1][0],
        grad_video_reduce_weight,
        sums[0],
        text_first_sums[0],
        text_first_sums[1],
        grad_text_attend_weight.transpose(1, 0, 2),
        unit_sums[2],
        grad_text_output_weight,
        text_final_sums[3],
        text_final_sums[1],
        text_final_sums[2],
        grad_text_expand_weight,
        unit_sums[3][0],
        grad_text_reduce_weight,
        text_final_sums[0],
    )


def solution(mesh):
    in_specs = (
        P("dp", "tensor", None, None),
        P(("dp", "tensor"), None),
        P("dp", None),
        P(),
        P(),
        P(),
        P(),
        P(),
        P(),
        P(),
        P(),
        P(),
        P(),
        P(None, None, "tensor"),
        P(None, "tensor"),
        P("tensor", None),
        P(),
        P(),
        P(),
        P(None, "tensor"),
        P("tensor"),
        P("tensor", None),
        P(),
        P(),
        P(),
        P(None, None, "tensor"),
        P(None, "tensor"),
        P("tensor", None),
        P(),
        P(),
        P(),
        P(None, "tensor"),
        P("tensor"),
        P("tensor", None),
        P(),
        P("dp", "tensor", None, None),
        P("dp", "tensor", None),
        P(("dp", "tensor"), None),
    )
    out_specs = (
        P("dp", "tensor", None, None),
        P("dp", "tensor", None),
        P(("dp", "tensor"), None),
        P("dp", "tensor", None, None),
        P(("dp", "tensor"), None),
        P(),
        P(),
        P(),
        P(),
        P(),
        P(),
        P(),
        P(),
        P(),
        P(),
        P(None, None, "tensor"),
        P(None, "tensor"),
        P("tensor", None),
        P(),
        P(),
        P(),
        P(None, "tensor"),
        P("tensor"),
        P("tensor", None),
        P(),
        P(),
        P(),
        P(None, None, "tensor"),
        P(None, "tensor"),
        P("tensor", None),
        P(),
        P(),
        P(),
        P(None, "tensor"),
        P("tensor"),
        P("tensor", None),
        P(),
    )
    return jax.shard_map(
        on_device, mesh=mesh, in_specs=in_specs, out_specs=out_specs, check_vma=False
    )
```

```python
import functools
import jax
import jax.numpy as jnp
from jax import lax
from jax.experimental import pallas as pl
from jax.experimental.pallas import tpu as pltpu
from jax.sharding import PartitionSpec as P

HD = 64
MAXLEN = 77
LANES = 128
VIDEO_CHUNKS = 3
TEXT_CHUNKS = 2
NEGATIVE = -1000000000.0
F32 = jnp.float32
BF16 = jnp.bfloat16
PARAMS = pltpu.CompilerParams(vmem_limit_bytes=60 << 20)


def nt(left, right):
    return lax.dot_general(left, right, (((1,), (1,)), ((), ())), preferred_element_type=F32)


def tn(left, right):
    return lax.dot_general(left, right, (((0,), (0,)), ((), ())), preferred_element_type=F32)


def mm(left, right):
    return jnp.dot(left, right, preferred_element_type=F32)


def unit_of(rows):
    centre = rows - jnp.mean(rows, axis=-1, keepdims=True)
    inverse = lax.rsqrt(jnp.mean(centre * centre, axis=-1, keepdims=True) + 1e-05)
    return centre * inverse, inverse


def norm_back(grad_out, unit_rows, inverse, gain_row):
    scaled = grad_out * gain_row
    return inverse * (
        scaled
        - jnp.mean(scaled, axis=-1, keepdims=True)
        - unit_rows * jnp.mean(scaled * unit_rows, axis=-1, keepdims=True)
    )


def column_sum(values):
    return jnp.sum(values, axis=0, keepdims=True)


def row_is(shape, row):
    return lax.broadcasted_iota(jnp.int32, shape, 0) == row


def low_half():
    return lax.broadcasted_iota(jnp.int32, (1, LANES), 1) < HD


def head_masks():
    first = low_half().astype(F32)
    return first.astype(BF16), (1.0 - first).astype(BF16)


def whole(array):
    return pl.BlockSpec(array.shape, lambda *_: (0,) * array.ndim)


def rows_block(rows, columns, offset=0):
    return pl.BlockSpec((rows, columns), lambda i: (i + offset, 0))


def cost(flops, arrays, outs):
    moved = sum(a.size * a.dtype.itemsize for a in arrays) + sum(
        a.size * jnp.dtype(a.dtype).itemsize for a in outs
    )
    return pl.CostEstimate(flops=int(flops), transcendentals=0, bytes_accessed=int(moved))


def call(body, grid, ins, in_specs, outs, out_specs, scratch=(), flops=0, name=None):
    return pl.pallas_call(
        body,
        grid=grid,
        in_specs=in_specs,
        out_specs=out_specs,
        out_shape=outs,
        scratch_shapes=list(scratch),
        compiler_params=PARAMS,
        cost_estimate=cost(flops, ins, outs),
        name=name,
    )(*ins)


def shape_of(shape, dtype):
    return jax.ShapeDtypeStruct(shape, dtype)


def video_first(frames_rows, tokens, gain, shift, token_row):
    frames, rows, width = frames_rows.shape

    def body(x_ref, token_ref, gain_ref, shift_ref, rows_ref, first_ref):
        x = x_ref[0].astype(F32)
        x = jnp.where(row_is(x.shape, token_row), token_ref[0], x)
        rows_ref[...] = x
        unit, _ = unit_of(x)
        first_ref[...] = (unit * gain_ref[...] + shift_ref[...]).astype(BF16)

    ins = (frames_rows, tokens, gain, shift)
    return call(
        body,
        (frames,),
        ins,
        [
            pl.BlockSpec((1, rows, width), lambda i: (i, 0, 0)),
            pl.BlockSpec((1, 1, width), lambda i: (i, 0, 0)),
            whole(gain),
            whole(shift),
        ],
        [shape_of((frames * rows, width), F32), shape_of((frames * rows, width), BF16)],
        [rows_block(rows, width), rows_block(rows, width)],
        name="video_first",
    )


def text_first(rows_in, gain, shift, block):
    rows, width = rows_in.shape

    def body(x_ref, gain_ref, shift_ref, first_ref):
        unit, _ = unit_of(x_ref[...].astype(F32))
        first_ref[...] = (unit * gain_ref[...] + shift_ref[...]).astype(BF16)

    ins = (rows_in, gain, shift)
    return call(
        body,
        (rows // block,),
        ins,
        [rows_block(block, width), whole(gain), whole(shift)],
        [shape_of((rows, width), BF16)],
        [rows_block(block, width)],
        name="text_first",
    )[0]


def masked(scores, plan, group, segments):
    if plan["keys"] is not None:
        columns = lax.broadcasted_iota(jnp.int32, scores.shape, 1)
        return jnp.where(columns < plan["keys"], scores, NEGATIVE)
    query_start, queries, key_start, keys, _ = group
    column_ref, row_ref = segments
    same = (
        column_ref[query_start : query_start + queries, :]
        == row_ref[:, key_start : key_start + keys]
    )
    columns = lax.broadcasted_iota(jnp.int32, scores.shape, 1) + key_start
    positions = lax.broadcasted_iota(jnp.int32, scores.shape, 0) + query_start
    return jnp.where(same & (columns <= positions), scores, NEGATIVE)


def attention_forward(first, weight, bias, plan, segments, name):
    rows, width = first.shape
    heads_width = weight.shape[2]
    steps = heads_width // LANES
    out_rows = plan["out_rows"]

    def body(x_ref, w_ref, b_ref, *rest):
        segment_refs, (mixed_ref, out_ref, lse_ref, wide_ref) = rest[:-4], rest[-4:]
        for part in range(3):
            wide_ref[:, part * LANES : (part + 1) * LANES] = w_ref[part]
        mixed = mm(x_ref[...], wide_ref[...])
        for part in range(3):
            mixed_ref[part] = (
                mixed[:, part * LANES : (part + 1) * LANES] + b_ref[part : part + 1, :]
            ).astype(BF16)
        masks = head_masks()
        lower = low_half()
        for group in plan["groups"]:
            query_start, queries, key_start, keys, out_start = group
            q = mixed_ref[0, query_start : query_start + queries, :] * jnp.asarray(0.125, BF16)
            k = mixed_ref[1, key_start : key_start + keys, :]
            v = mixed_ref[2, key_start : key_start + keys, :]
            outs, sums = [], []
            for mask in masks:
                scores = masked(nt(q * mask, k), plan, group, segment_refs)
                top = jnp.max(scores, axis=-1, keepdims=True)
                powers = jnp.exp(scores - top)
                total = jnp.sum(powers, axis=-1, keepdims=True)
                probs = (powers * (1.0 / total)).astype(BF16)
                outs.append(mm(probs, v))
                sums.append(top + jnp.log(total))
            out_ref[out_start : out_start + queries, :] = jnp.where(lower, outs[0], outs[1]).astype(
                BF16
            )
            lse_ref[out_start : out_start + queries, :] = jnp.where(lower, sums[0], sums[1])

    ins = (first, weight, bias) + segments
    return call(
        body,
        (steps,),
        ins,
        [
            whole(first),
            pl.BlockSpec((3, width, LANES), lambda i: (0, 0, i)),
            pl.BlockSpec((3, LANES), lambda i: (0, i)),
        ]
        + [whole(s) for s in segments],
        [
            shape_of((3, rows, heads_width), BF16),
            shape_of((out_rows, heads_width), BF16),
            shape_of((out_rows, heads_width), F32),
        ],
        [
            pl.BlockSpec((3, rows, LANES), lambda i: (0, 0, i)),
            pl.BlockSpec((out_rows, LANES), lambda i: (0, i)),
            pl.BlockSpec((out_rows, LANES), lambda i: (0, i)),
        ],
        scratch=[pltpu.VMEM((width, 3 * LANES), BF16)],
        flops=2 * rows * width * 3 * heads_width * 2,
        name=name,
    )


def attention_backward(
    low, out_weight, attended, first, weight, mixed, lse, plan, segments, name
):
    rows, width = first.shape
    out_rows = plan["out_rows"]
    heads_width = weight.shape[2]
    steps = heads_width // LANES
    shared = plan["keys"] is None

    def body(low_ref, ow_ref, att_ref, x_ref, w_ref, mixed_ref, lse_ref, *rest):
        segment_refs = rest[: len(segments)]
        (
            flat_ref,
            bias_ref,
            first_grad_ref,
            wide_ref,
            turned_ref,
            grad_ref,
            key_ref,
            value_ref,
        ) = rest[len(segments) :]
        step = pl.program_id(0)

        @pl.when(step == 0)
        def _():
            turned_ref[...] = x_ref[...].T
            first_grad_ref[...] = jnp.zeros_like(first_grad_ref)

        for part in range(3):
            wide_ref[:, part * LANES : (part + 1) * LANES] = w_ref[part]
        low_rows = low_ref[...]
        grad_out = nt(low_rows, ow_ref[...]).astype(BF16)
        out_grad = tn(att_ref[...], low_rows).astype(BF16)
        for part in range(width // LANES):
            flat_ref[3, 0, part * LANES : (part + 1) * LANES, :] = out_grad[
                :, part * LANES : (part + 1) * LANES
            ]
        if shared:
            grad_ref[...] = jnp.zeros_like(grad_ref)
            key_ref[...] = jnp.zeros_like(key_ref)
            value_ref[...] = jnp.zeros_like(value_ref)
        masks = head_masks()
        lower = low_half()
        for group in plan["groups"]:
            query_start, queries, key_start, keys, out_start = group
            q = mixed_ref[0, query_start : query_start + queries, :] * jnp.asarray(0.125, BF16)
            k = mixed_ref[1, key_start : key_start + keys, :]
            v = mixed_ref[2, key_start : key_start + keys, :]
            g = grad_out[out_start : out_start + queries, :]
            query_grads, key_grad, value_grad = [], None, None
            for head, mask in enumerate(masks):
                query_head, grad_head = q * mask, g * mask
                scores = masked(nt(query_head, k), plan, group, segment_refs)
                column = lse_ref[out_start : out_start + queries, head * HD : head * HD + 1]
                probs = jnp.exp(scores - column)
                grad_probs = nt(grad_head, v)
                dots = jnp.sum(probs * grad_probs, axis=-1, keepdims=True)
                grad_scores = (probs * (grad_probs - dots)).astype(BF16)
                query_grads.append(mm(grad_scores, k))
                key_term = tn(grad_scores, query_head)
                value_term = tn(probs.astype(BF16), grad_head)
                key_grad = key_term if key_grad is None else key_grad + key_term
                value_grad = value_term if value_grad is None else value_grad + value_term
            query_grad = jnp.where(lower, query_grads[0], query_grads[1]) * 0.125
            grad_ref[query_start : query_start + queries, :LANES] = query_grad.astype(BF16)
            span = slice(key_start, key_start + keys)
            if shared:
                key_ref[span, :] += key_grad
                value_ref[span, :] += value_grad
            else:
                grad_ref[span, LANES : 2 * LANES] = key_grad.astype(BF16)
                grad_ref[span, 2 * LANES :] = value_grad.astype(BF16)
        if shared:
            grad_ref[:, LANES : 2 * LANES] = key_ref[...].astype(BF16)
            grad_ref[:, 2 * LANES :] = value_ref[...].astype(BF16)
        grads = grad_ref[...]
        weight_grads = mm(turned_ref[...], grads)
        sums = column_sum(grads.astype(F32))
        for part in range(3):
            flat_ref[part, 0] = weight_grads[:, part * LANES : (part + 1) * LANES].astype(BF16)
        bias_ref[0:1, :] = sums[:, :LANES]
        bias_ref[1:2, :] = sums[:, 2 * LANES :]
        first_grad_ref[...] += nt(grads, wide_ref[...])

    ins = (low, out_weight, attended, first, weight, mixed, lse) + segments
    return call(
        body,
        (steps,),
        ins,
        [
            whole(low),
            pl.BlockSpec((LANES, width), lambda i: (i, 0)),
            pl.BlockSpec((out_rows, LANES), lambda i: (0, i)),
            whole(first),
            pl.BlockSpec((3, width, LANES), lambda i: (0, 0, i)),
            pl.BlockSpec((3, rows, LANES), lambda i: (0, 0, i)),
            pl.BlockSpec((out_rows, LANES), lambda i: (0, i)),
        ]
        + [whole(s) for s in segments],
        [
            shape_of((4, steps, width, LANES), BF16),
            shape_of((2, heads_width), F32),
            shape_of((rows, width), F32),
        ],
        [
            pl.BlockSpec((4, 1, width, LANES), lambda i: (0, i, 0, 0)),
            pl.BlockSpec((2, LANES), lambda i: (0, i)),
            pl.BlockSpec((rows, width), lambda i: (0, 0)),
        ],
        scratch=[
            pltpu.VMEM((width, 3 * LANES), BF16),
            pltpu.VMEM((width, rows), BF16),
            pltpu.VMEM((rows, 3 * LANES), BF16),
            pltpu.VMEM((rows, LANES), F32),
            pltpu.VMEM((rows, LANES), F32),
        ],
        flops=2 * rows * width * 8 * heads_width * 2,
        name=name,
    )


def project_norm(parts, weights, rows_in, bias, gain, shift, block, offset, name):
    out_rows, half = parts[0].shape
    width = bias.shape[1]

    def body(a_ref, b_ref, wa_ref, wb_ref, rows_ref, bias_ref, gain_ref, shift_ref, res_ref, out_ref):
        resid = (
            rows_ref[...].astype(F32)
            + mm(a_ref[...], wa_ref[...])
            + mm(b_ref[...], wb_ref[...])
            + bias_ref[...]
        )
        res_ref[...] = resid
        unit, _ = unit_of(resid)
        out_ref[...] = (unit * gain_ref[...] + shift_ref[...]).astype(BF16)

    ins = (*parts, *weights, rows_in, bias, gain, shift)
    return call(
        body,
        (out_rows // block,),
        ins,
        [
            rows_block(block, half),
            rows_block(block, half),
            whole(weights[0]),
            whole(weights[1]),
            rows_block(block, width, offset),
            whole(bias),
            whole(gain),
            whole(shift),
        ],
        [shape_of((out_rows, width), F32), shape_of((out_rows, width), BF16)],
        [rows_block(block, width), rows_block(block, width)],
        flops=4 * out_rows * half * width,
        name=name,
    )


def feed_forward(second, cot, expand, expand_bias, reduce, chunk, flat, name):
    rows, width = second.shape
    units = expand.shape[1]
    size = width * chunk // LANES

    def body(x_ref, cot_ref, e_ref, b_ref, r_ref, *rest):
        *grad_refs, gb_ref, out_ref, back_ref, turned_ref = rest

        @pl.when(pl.program_id(0) == 0)
        def _():
            turned_ref[...] = x_ref[...].T
            out_ref[...] = jnp.zeros_like(out_ref)
            back_ref[...] = jnp.zeros_like(back_ref)

        cot_rows = cot_ref[...]
        hidden = mm(x_ref[...], e_ref[...]) + b_ref[...]
        grad_active = nt(cot_rows, r_ref[...])
        logistic = 1.0 / (1.0 + jnp.exp(-1.702 * hidden))
        active = (hidden * logistic).astype(BF16)
        slope = logistic + 1.702 * hidden * logistic * (1.0 - logistic)
        grad_hidden = grad_active * slope
        grad_low = grad_hidden.astype(BF16)
        gb_ref[...] = column_sum(grad_low.astype(F32))
        out_ref[...] += mm(active, r_ref[...])
        back_ref[...] += nt(grad_low, e_ref[...])
        reduce_grad = tn(active, cot_rows).astype(BF16)
        expand_grad = mm(turned_ref[...], grad_low).astype(BF16)
        if not flat:
            grad_refs[0][...] = expand_grad
            grad_refs[1][...] = reduce_grad
            return
        for part in range(chunk // LANES):
            grad_refs[0][0, 0, part * width : (part + 1) * width, :] = expand_grad[
                :, part * LANES : (part + 1) * LANES
            ]
        for part in range(width // LANES):
            grad_refs[0][1, 0, part * chunk : (part + 1) * chunk, :] = reduce_grad[
                :, part * LANES : (part + 1) * LANES
            ]

    if flat:
        grads = [shape_of((2, units // chunk, size, LANES), BF16)]
        grad_specs = [pl.BlockSpec((2, 1, size, LANES), lambda i: (0, i, 0, 0))]
    else:
        grads = [shape_of((width, units), BF16), shape_of((units, width), BF16)]
        grad_specs = [
            pl.BlockSpec((width, chunk), lambda i: (0, i)),
            pl.BlockSpec((chunk, width), lambda i: (i, 0)),
        ]
    ins = (second, cot, expand, expand_bias, reduce)
    return call(
        body,
        (units // chunk,),
        ins,
        [
            whole(second),
            whole(cot),
            pl.BlockSpec((width, chunk), lambda i: (0, i)),
            pl.BlockSpec((1, chunk), lambda i: (0, i)),
            pl.BlockSpec((chunk, width), lambda i: (i, 0)),
        ],
        grads
        + [
            shape_of((1, units), F32),
            shape_of((rows, width), F32),
            shape_of((rows, width), F32),
        ],
        grad_specs
        + [
            pl.BlockSpec((1, chunk), lambda i: (0, i)),
            pl.BlockSpec((rows, width), lambda i: (0, 0)),
            pl.BlockSpec((rows, width), lambda i: (0, 0)),
        ],
        scratch=[pltpu.VMEM((width, rows), BF16)],
        flops=12 * rows * width * units,
        name=name,
    )


def resid_back(resid, outs, backs, cot, token_grads, gain, reduce_bias, block, token_row, name):
    rows, width = resid.shape

    def body(res_ref, oa_ref, ob_ref, ba_ref, bb_ref, cot_ref, *rest):
        if token_row is None:
            gain_ref, rb_ref, final_ref, grad_ref, low_ref, sums_ref = rest
        else:
            token_ref, gain_ref, rb_ref, final_ref, grad_ref, low_ref, sums_ref = rest

        @pl.when(pl.program_id(0) == 0)
        def _():
            sums_ref[...] = jnp.zeros_like(sums_ref)

        resid_rows = res_ref[...]
        final_ref[...] = (resid_rows + oa_ref[...] + ob_ref[...] + rb_ref[...]).astype(BF16)
        back = ba_ref[...] + bb_ref[...]
        unit, inverse = unit_of(resid_rows)
        cot_rows = cot_ref[...].astype(F32)
        sums_ref[0:1, :] += column_sum(cot_rows)
        sums_ref[1:2, :] += column_sum(back * unit)
        sums_ref[2:3, :] += column_sum(back)
        if token_row is not None:
            cot_rows = jnp.where(row_is(cot_rows.shape, token_row), token_ref[0], cot_rows)
        grad = cot_rows + norm_back(back, unit, inverse, gain_ref[...])
        sums_ref[3:4, :] += column_sum(grad)
        grad_ref[...] = grad
        low_ref[...] = grad.astype(BF16)

    ins = (resid, *outs, *backs, cot)
    specs = [rows_block(block, width)] * 6
    if token_row is not None:
        ins += (token_grads,)
        specs.append(pl.BlockSpec((1, 1, width), lambda i: (i, 0, 0)))
    ins += (gain, reduce_bias)
    specs += [whole(gain), whole(reduce_bias)]
    return call(
        body,
        (rows // block,),
        ins,
        specs,
        [
            shape_of((rows, width), BF16),
            shape_of((rows, width), F32),
            shape_of((rows, width), BF16),
            shape_of((4, width), F32),
        ],
        [rows_block(block, width)] * 3 + [pl.BlockSpec((4, width), lambda i: (0, 0))],
        name=name,
    )


def video_rows_back(rows_in, firsts, grad_resid, gain, block, token_row):
    rows, width = rows_in.shape
    frames = rows // block

    def body(rows_ref, fa_ref, fb_ref, grad_ref, gain_ref, out_ref, edge_ref, sums_ref):
        @pl.when(pl.program_id(0) == 0)
        def _():
            sums_ref[...] = jnp.zeros_like(sums_ref)

        unit, inverse = unit_of(rows_ref[...])
        back = fa_ref[...] + fb_ref[...]
        sums_ref[0:1, :] += column_sum(back * unit)
        sums_ref[1:2, :] += column_sum(back)
        grad = grad_ref[...] + norm_back(back, unit, inverse, gain_ref[...])
        out_ref[...] = grad.astype(BF16)
        edge_ref[0, 0:1, :] = grad[0:1, :]
        edge_ref[0, 1:2, :] = grad[token_row : token_row + 1, :]

    ins = (rows_in, *firsts, grad_resid, gain)
    return call(
        body,
        (frames,),
        ins,
        [rows_block(block, width)] * 4 + [whole(gain)],
        [
            shape_of((rows, width), BF16),
            shape_of((frames, 2, width), F32),
            shape_of((2, width), F32),
        ],
        [
            rows_block(block, width),
            pl.BlockSpec((1, 2, width), lambda i: (i, 0, 0)),
            pl.BlockSpec((2, width), lambda i: (0, 0)),
        ],
        name="video_rows_back",
    )


def text_rows_back(rows_in, firsts, grad_resid, gain, block):
    rows, width = rows_in.shape
    ahead = (rows - grad_resid.shape[0]) // block

    def body(rows_ref, fa_ref, fb_ref, grad_ref, gain_ref, out_ref, sums_ref):
        step = pl.program_id(0)

        @pl.when(step == 0)
        def _():
            sums_ref[...] = jnp.zeros_like(sums_ref)

        unit, inverse = unit_of(rows_ref[...].astype(F32))
        back = fa_ref[...] + fb_ref[...]
        sums_ref[0:1, :] += column_sum(back * unit)
        sums_ref[1:2, :] += column_sum(back)
        own = jnp.where(step >= ahead, 1.0, 0.0)
        out_ref[...] = grad_ref[...] * own + norm_back(back, unit, inverse, gain_ref[...])

    ins = (rows_in, *firsts, grad_resid, gain)
    return call(
        body,
        (rows // block,),
        ins,
        [rows_block(block, width)] * 3
        + [
            pl.BlockSpec((block, width), lambda i: (jnp.maximum(i - ahead, 0), 0)),
            whole(gain),
        ],
        [shape_of((rows, width), F32), shape_of((2, width), F32)],
        [rows_block(block, width), pl.BlockSpec((2, width), lambda i: (0, 0))],
        name="text_rows_back",
    )


def head_rows(values, heads):
    lanes = lax.broadcasted_iota(jnp.int32, values.shape, 1) // HD
    return jnp.concatenate(
        [jnp.where(lanes == head, values, 0.0) for head in range(heads)], axis=0
    ).astype(BF16)


def fold_heads(values, heads, rows):
    lanes = lax.broadcasted_iota(jnp.int32, (rows, values.shape[1]), 1) // HD
    total = jnp.zeros((rows, values.shape[1]), F32)
    for head in range(heads):
        total = total + jnp.where(lanes == head, values[head * rows : (head + 1) * rows], 0.0)
    return total


def message_probs(mixed_ref, heads):
    query_rows = head_rows(mixed_ref[0].astype(F32) * 0.125, heads)
    scores = nt(query_rows, mixed_ref[1])
    top = jnp.max(scores, axis=-1, keepdims=True)
    powers = jnp.exp(scores - top)
    return query_rows, powers * (1.0 / jnp.sum(powers, axis=-1, keepdims=True))


def messages_forward(messages, gain, shift, weight, bias, out_weight, out_bias):
    rows, width = messages.shape
    heads = width // HD

    def body(m_ref, gain_ref, shift_ref, w_ref, b_ref, ow_ref, ob_ref, n_ref, mixed_ref, a_ref, t_ref):
        messages_now = m_ref[...]
        unit, _ = unit_of(messages_now)
        normed = (unit * gain_ref[...] + shift_ref[...]).astype(BF16)
        n_ref[...] = normed
        for part in range(3):
            mixed_ref[part] = (mm(normed, w_ref[part]) + b_ref[part : part + 1, :]).astype(BF16)
        _, probs = message_probs(mixed_ref, heads)
        attended = fold_heads(mm(probs.astype(BF16), mixed_ref[2]), heads, rows).astype(BF16)
        a_ref[...] = attended
        t_ref[...] = messages_now + mm(attended, ow_ref[...]) + ob_ref[...]

    ins = (messages, gain, shift, weight, bias, out_weight, out_bias)
    outs = [
        shape_of((rows, width), BF16),
        shape_of((3, rows, width), BF16),
        shape_of((rows, width), BF16),
        shape_of((rows, width), F32),
    ]
    return call(
        body, (1,), ins, [whole(a) for a in ins], outs, [whole(o) for o in outs], name="messages"
    )


def messages_backward(messages, mixed, token_grads, gain, weight, out_weight, in_weight):
    rows, width = messages.shape
    heads = width // HD

    def body(m_ref, mixed_ref, t_ref, gain_ref, w_ref, ow_ref, iw_ref, g_ref, low_ref, c_ref, s_ref):
        token = t_ref[...]
        grad_attended = nt(token.astype(BF16), ow_ref[...]).astype(BF16)
        query_rows, probs = message_probs(mixed_ref, heads)
        grad_rows = head_rows(grad_attended.astype(F32), heads)
        grad_probs = nt(grad_rows, mixed_ref[2])
        dots = jnp.sum(probs * grad_probs, axis=-1, keepdims=True)
        grad_scores = (probs * (grad_probs - dots)).astype(BF16)
        grads = (
            fold_heads(mm(grad_scores, mixed_ref[1]), heads, rows) * 0.125,
            tn(grad_scores, query_rows),
            tn(probs.astype(BF16), grad_rows),
        )
        normed_grad = jnp.zeros((rows, width), F32)
        for part in range(3):
            low = grads[part].astype(BF16)
            g_ref[part] = low
            normed_grad = normed_grad + nt(low, w_ref[part])
        s_ref[0:1, :] = column_sum(g_ref[0].astype(F32))
        s_ref[1:2, :] = column_sum(g_ref[2].astype(F32))
        unit, inverse = unit_of(m_ref[...])
        s_ref[2:3, :] = column_sum(normed_grad * unit)
        s_ref[3:4, :] = column_sum(normed_grad)
        grad = token + norm_back(normed_grad, unit, inverse, gain_ref[...])
        s_ref[4:5, :] = column_sum(grad)
        s_ref[5:6, :] = column_sum(token)
        low = grad.astype(BF16)
        low_ref[...] = low
        c_ref[...] = nt(low, iw_ref[...])

    ins = (messages, mixed, token_grads, gain, weight, out_weight, in_weight)
    outs = [
        shape_of((3, rows, width), BF16),
        shape_of((rows, width), BF16),
        shape_of((rows, width), F32),
        shape_of((6, width), F32),
    ]
    return call(
        body,
        (1,),
        ins,
        [whole(a) for a in ins],
        outs,
        [whole(o) for o in outs],
        name="messages_back",
    )


def swap(value):
    return lax.ppermute(value, "tensor", [(0, 1), (1, 0)])


def in_order(own, other, axis=0):
    first = lax.axis_index("tensor") == 0
    return jnp.where(
        first, jnp.concatenate([own, other], axis), jnp.concatenate([other, own], axis)
    )


def own_part(values, size, axis=0):
    return lax.dynamic_slice_in_dim(values, lax.axis_index("tensor") * size, size, axis)


def row_of(vector):
    return vector.astype(F32).reshape(1, -1)


def qkv_bias(flat):
    rows = flat.astype(F32).reshape(2, -1)
    return jnp.stack([rows[0], jnp.zeros_like(rows[0]), rows[1]])


def exchange(value, away):
    size = lax.axis_size("dp")
    return lax.ppermute(value, "dp", [(at, at ^ away) for at in range(size)])


def bit_of(bit):
    return (lax.axis_index("dp") >> bit) & 1


def add(*values):
    return sum(value.astype(F32) for value in values).astype(BF16)


def dp_bits():
    return lax.axis_size("dp").bit_length() - 1


def by_bit(own, other, mine):
    return jnp.where(
        mine == 0, jnp.concatenate([own, other], 0), jnp.concatenate([other, own], 0)
    )


class Steps:
    def __init__(self, make, *ins):
        self.after = ()
        self.steps = make(self, *ins)
        self.result = None

    def step(self, *after):
        self.after = after
        try:
            return next(self.steps)
        except StopIteration as stop:
            self.result = stop.value
            return ()

    def hold(self, values):
        return tie(values, self.after) if self.after else values


def tie(value, *waited):
    return lax.optimization_barrier((value, waited))[0]


def take(rows, part, size):
    return lax.dynamic_slice_in_dim(rows, part * size, size)


def bucket_steps(steps, own, received):
    orders = (0, 1), (1, 0)
    bits = [bit_of(bit) for bit in orders[0]]
    parts = [
        [mine.reshape(-1, LANES), theirs.reshape(-1, LANES)] for mine, theirs in zip(own, received)
    ]
    for at in range(2):
        kept, arrived = [], []
        for values, order in zip(parts, orders):
            size = values[0].shape[0] // 2
            mine = bits[order[at]]
            send = [take(value, 1 - mine, size) for value in values]
            kept.append([take(value, mine, size) for value in values])
            arrived.append(exchange(add(*send) if at == 0 else send[0], 1 << order[at]))
        yield arrived
        arrived = steps.hold(arrived)
        parts = [[add(*keep, there)] for keep, there in zip(kept, arrived)]
    first = parts[0][0].shape[0]
    rows = jnp.concatenate([values[0] for values in parts])
    count = lax.axis_size("dp") // 4
    here = lax.axis_index("dp") >> 2
    size = rows.shape[0] // count
    arrived = [exchange(take(rows, here ^ away, size), away << 2) for away in range(1, count)]
    yield arrived
    arrived = steps.hold(arrived)
    rows = add(take(rows, here, size), *arrived)
    arrived = [exchange(rows, away << 2) for away in range(1, count)]
    yield arrived
    arrived = steps.hold(arrived)
    pieces = jnp.concatenate([rows] + arrived)
    rows = jnp.concatenate([take(pieces, at ^ here, size) for at in range(count)])
    parts = [rows[:first], rows[first:]]
    for at in (1, 0):
        arrived = [exchange(value, 1 << order[at]) for value, order in zip(parts, orders)]
        yield arrived
        arrived = steps.hold(arrived)
        parts = [jnp.concatenate(pair) for pair in zip(parts, arrived)]
    return [
        (part, (bits[one] * 2 + bits[two]).reshape(1)) for part, (one, two) in zip(parts, orders)
    ]


def place(at, blocks, here_ref):
    part = blocks // 4
    return ((at // part) ^ here_ref[0]) * part + at % part, 0


def pack_vectors(common, own, other):
    rows = sum(value.size for value in common + own) // LANES

    def body(*refs):
        ins, outs = refs[:-2], refs[-2:]
        counts = len(common), len(common) + len(own)
        for out, parts in zip(outs, (ins[: counts[1]], ins[: counts[0]] + ins[counts[1] :])):
            begin = 0
            for ref in parts:
                across = ref.shape[1] // LANES
                for row in range(ref.shape[0]):
                    for part in range(across):
                        out[begin : begin + 1, :] = ref[
                            row : row + 1, part * LANES : (part + 1) * LANES
                        ]
                        begin += 1

    ins = (*common, *own, *other)
    outs = [shape_of((rows, LANES), F32)] * 2
    return call(
        body, (1,), ins, [whole(a) for a in ins], outs, [whole(o) for o in outs], name="vectors"
    )


def vector_steps(steps, common, own, other):
    total, send = pack_vectors(common, own, other)
    there = swap(send)
    yield there
    total = total + steps.hold(there)
    for bit in range(dp_bits()):
        there = exchange(total, 1 << bit)
        yield there
        total = total + steps.hold(there)
    total = total.reshape(-1)
    done = []
    begin = 0
    for value in common + own:
        done.append(total[begin : begin + value.size].reshape(value.shape))
        begin += value.size
    return done


def gather_steps(steps, values):
    for bit in reversed(range(dp_bits())):
        there = exchange(values, 1 << bit)
        yield there
        values = by_bit(values, steps.hold(there), bit_of(bit))
    there = swap(values)
    yield there
    return in_order(values, steps.hold(there))


def unpack_units(summed, width, units, chunk, name):
    rows, here = summed
    block = width
    blocks = rows.shape[0] // block
    across = width // (2 * LANES)
    steps = units // (2 * LANES)

    def body(here_ref, *refs):
        for at in range(2):
            span = slice(at * LANES, (at + 1) * LANES)
            refs[4][:, span] = refs[at][...].astype(F32)
            refs[5][:, span] = refs[2 + at][...].astype(F32)

    def in_spec(at):
        begin = blocks // 2 * (at // 2) + at % 2
        return pl.BlockSpec(
            (block, LANES), lambda i, here_ref: place(begin + 2 * i, blocks, here_ref)
        )

    outs = [shape_of((width, units), F32), shape_of((units, width), F32)]
    return pl.pallas_call(
        body,
        grid_spec=pltpu.PrefetchScalarGridSpec(
            num_scalar_prefetch=1,
            grid=(steps,),
            in_specs=[in_spec(at) for at in range(4)],
            out_specs=[
                pl.BlockSpec((width, 2 * LANES), lambda i, here_ref: (0, i)),
                pl.BlockSpec((chunk, 2 * LANES), lambda i, here_ref: (i // across, i % across)),
            ],
        ),
        out_shape=outs,
        compiler_params=PARAMS,
        cost_estimate=cost(0, (rows,), outs),
        name=name,
    )(here, *([rows] * 4))


def unpack_attention(summed, width, steps, name):
    rows, here = summed
    block = width // 2
    blocks = rows.shape[0] // block

    def body(here_ref, *refs):
        attend_ref, out_ref = refs[8:]
        for at in range(8):
            values = refs[at][...].astype(F32)
            start = at % 2 * block
            if at < 6:
                attend_ref[at // 2, start : start + block, :] = values
                continue
            for part in range(block // LANES):
                begin = start + part * LANES
                out_ref[:, begin : begin + LANES] = values[part * LANES : (part + 1) * LANES, :]

    def in_spec(at):
        return pl.BlockSpec(
            (block, LANES),
            lambda i, here_ref: place(
                (at // 2 * steps + i) * 2 + at % 2, blocks, here_ref
            ),
        )

    outs = [shape_of((3, width, steps * LANES), F32), shape_of((steps * LANES, width), F32)]
    return pl.pallas_call(
        body,
        grid_spec=pltpu.PrefetchScalarGridSpec(
            num_scalar_prefetch=1,
            grid=(steps,),
            in_specs=[in_spec(at) for at in range(8)],
            out_specs=[
                pl.BlockSpec((3, width, LANES), lambda i, here_ref: (0, 0, i)),
                pl.BlockSpec((LANES, width), lambda i, here_ref: (i, 0)),
            ],
        ),
        out_shape=outs,
        compiler_params=PARAMS,
        cost_estimate=cost(0, (rows,), outs),
        name=name,
    )(here, *([rows] * 8))


def on_device(
    video_input,
    text_input,
    caption_lengths,
    video_first_gain,
    video_first_shift,
    video_message_weight,
    video_message_bias,
    video_message_gain,
    video_message_shift,
    video_message_attend_weight,
    video_message_attend_bias,
    video_message_out_weight,
    video_message_out_bias,
    video_attend_weight,
    video_attend_bias,
    video_output_weight,
    video_output_bias,
    video_final_gain,
    video_final_shift,
    video_expand_weight,
    video_expand_bias,
    video_reduce_weight,
    video_reduce_bias,
    text_first_gain,
    text_first_shift,
    text_attend_weight,
    text_attend_bias,
    text_output_weight,
    text_output_bias,
    text_final_gain,
    text_final_shift,
    text_expand_weight,
    text_expand_bias,
    text_reduce_weight,
    text_reduce_bias,
    video_out_grad,
    message_out_grad,
    text_out_grad,
):
    core = lax.axis_index("tensor")
    frames, tokens, width = video_input.shape[1:]
    frame_rows = -(-(tokens + 1) // 16) * 16
    spare = ((0, 0), (0, frame_rows - tokens), (0, 0))
    text_count, text_width = text_input.shape
    halo = -(-(MAXLEN - 1) // LANES) * LANES

    class_rows = video_input[0, :, 0, :]
    messages_here = (
        jnp.dot(class_rows, video_message_weight, preferred_element_type=F32)
        + video_message_bias.astype(F32)
    )
    messages_there = swap(messages_here)
    text_qkv = (text_attend_weight.transpose(1, 0, 2),)
    video_qkv = (video_attend_weight.transpose(1, 0, 2),)
    small = (video_attend_bias, video_expand_bias, text_attend_bias, text_expand_bias)
    packed = jnp.concatenate([value.reshape(-1) for value in small])
    packed_there = swap(packed)
    biases = []
    begin = 0
    for value in small:
        biases.append((packed[begin : begin + value.size], packed_there[begin : begin + value.size]))
        begin += value.size
    text_ahead = lax.ppermute(text_input[text_count - halo :], "tensor", [(0, 1)])
    text_qkv += (swap(text_qkv[0]),)
    video_qkv += (swap(video_qkv[0]),)
    text_out = (text_output_weight, swap(text_output_weight))
    video_out = (video_output_weight, swap(video_output_weight))
    video_expand = (video_expand_weight, swap(video_expand_weight))
    video_reduce = (video_reduce_weight, swap(video_reduce_weight))
    text_expand = (text_expand_weight, swap(text_expand_weight))
    text_reduce = (text_reduce_weight, swap(text_reduce_weight))
    video_qkv_bias = [qkv_bias(flat) for flat in biases[0]]
    text_qkv_bias = [qkv_bias(flat) for flat in biases[2]]
    sides = (0, 1)

    messages = in_order(messages_here, messages_there)
    message_weight = video_message_attend_weight.transpose(1, 0, 2)
    message_gain = row_of(video_message_gain)
    message_normed, message_mixed, message_attended, message_tokens = messages_forward(
        messages,
        message_gain,
        row_of(video_message_shift),
        message_weight,
        qkv_bias(video_message_attend_bias),
        video_message_out_weight,
        row_of(video_message_out_bias),
    )
    tokens_here = own_part(message_tokens, frames)

    video_gain, video_gain_two = row_of(video_first_gain), row_of(video_final_gain)
    video_rows, video_normed = video_first(
        jnp.pad(video_input[0], spare),
        tokens_here[:, None],
        video_gain,
        row_of(video_first_shift),
        tokens,
    )
    video_plan = {
        "groups": [
            (start, frame_rows, start, frame_rows, start)
            for start in range(0, frames * frame_rows, frame_rows)
        ],
        "keys": tokens + 1,
        "out_rows": frames * frame_rows,
    }
    video_attention = [
        attention_forward(
            video_normed, video_qkv[side], video_qkv_bias[side], video_plan, (), "video_attention"
        )
        for side in sides
    ]
    video_resid, video_second = project_norm(
        [video_attention[side][1] for side in sides],
        video_out,
        video_rows,
        row_of(video_output_bias),
        video_gain_two,
        row_of(video_final_shift),
        frame_rows,
        0,
        "video_project",
    )
    message_output = video_resid.reshape(frames, frame_rows, width)[:, tokens].astype(BF16)[None]

    video_cot = jnp.pad(video_out_grad[0], spare).reshape(-1, width)
    video_units = {}
    for side in (1, 0):
        video_units[side] = feed_forward(
            video_second,
            video_cot,
            video_expand[side],
            row_of(biases[1][side]),
            video_reduce[side],
            video_expand[side].shape[1] // VIDEO_CHUNKS,
            False,
            "video_units",
        )
    video_units_sums = tuple(
        add(mine, swap(theirs)) for mine, theirs in zip(video_units[0][:2], video_units[1][:2])
    )

    video_final, video_grad_resid, video_low, video_sums = resid_back(
        tie(video_resid, video_units_sums),
        [video_units[side][-2] for side in sides],
        [video_units[side][-1] for side in sides],
        video_cot,
        message_out_grad[0].astype(F32)[:, None],
        video_gain_two,
        row_of(video_reduce_bias),
        frame_rows,
        tokens,
        "video_resid_back",
    )
    video_output = video_final.reshape(1, frames, frame_rows, width)[:, :, :tokens]

    video_back = {}
    for side in (1, 0):
        video_back[side] = attention_backward(
            video_low,
            video_out[side],
            video_attention[side][1],
            video_normed,
            video_qkv[side],
            video_attention[side][0],
            video_attention[side][2],
            video_plan,
            (),
            "video_attention_back",
        )
    video_flat = add(
        video_back[0][0].reshape(-1, LANES), swap(video_back[1][0].reshape(-1, LANES))
    )
    video_sum = lax.psum((*video_units_sums, video_flat), "dp")
    video_grads, video_edges, video_sums_one = video_rows_back(
        tie(video_rows, video_flat),
        [video_back[side][2] for side in sides],
        video_grad_resid,
        video_gain,
        frame_rows,
        tokens,
    )

    token_here = video_edges[:, 1]
    token_there = swap(token_here)
    token_grads = in_order(token_here, token_there)
    message_grads, message_low, class_grads, message_sums = messages_backward(
        messages,
        message_mixed,
        token_grads,
        message_gain,
        message_weight,
        video_message_out_weight,
        video_message_weight,
    )
    class_row = (video_edges[:, 0] + own_part(class_grads, frames)).astype(BF16)
    factors = jnp.concatenate(
        [
            class_rows,
            own_part(message_normed, frames),
            own_part(message_attended, frames),
            token_here.astype(BF16),
            own_part(message_low, frames),
        ]
        + [own_part(message_grads[part], frames) for part in range(3)],
        axis=1,
    )
    def apart():
        factor_rows = Steps(gather_steps, factors)
        text_rows = jnp.concatenate([text_ahead, text_input])
        rows_all = text_count + halo
        caption_ends = jnp.cumsum(caption_lengths[0])
        positions = core * text_count - halo + jnp.arange(rows_all, dtype=jnp.int32)
        segment = jnp.sum((positions[:, None] >= caption_ends[None, :]).astype(jnp.int32), axis=1)
        segment = jnp.where(positions < 0, -1, segment)
        segments = (segment.reshape(-1, 1), segment.reshape(1, -1))
        text_plan = {
            "groups": [
                (halo + start, LANES, start, halo + LANES, start)
                for start in range(0, text_count, LANES)
            ],
            "keys": None,
            "out_rows": text_count,
        }
        text_gain, text_gain_two = row_of(text_first_gain), row_of(text_final_gain)
        text_normed = text_first(
            tie(text_rows, message_low), text_gain, row_of(text_first_shift), LANES
        )
        text_attention = {}
        for side in (0, 1):
            text_attention[side] = attention_forward(
                text_normed,
                text_qkv[side],
                text_qkv_bias[side],
                text_plan,
                segments,
                "text_attention",
            )
        text_resid, text_second = project_norm(
            [text_attention[side][1] for side in sides],
            text_out,
            text_rows,
            row_of(text_output_bias),
            text_gain_two,
            row_of(text_final_shift),
            LANES,
            halo // LANES,
            "text_project",
        )
        text_units = {}
        for side in (1, 0):
            text_units[side] = feed_forward(
                text_second,
                text_out_grad,
                text_expand[side],
                row_of(biases[3][side]),
                text_reduce[side],
                text_expand[side].shape[1] // TEXT_CHUNKS,
                True,
                "text_units",
            )
        text_there = swap(text_units[1][0])
        text_final, text_grad_resid, text_low, text_sums = resid_back(
            text_resid,
            [text_units[side][2] for side in sides],
            [text_units[side][3] for side in sides],
            text_out_grad,
            None,
            text_gain_two,
            row_of(text_reduce_bias),
            LANES,
            None,
            "text_resid_back",
        )
        text_back = {}
        for side in (1, 0):
            text_back[side] = attention_backward(
                text_low,
                text_out[side],
                text_attention[side][1],
                text_normed,
                text_qkv[side],
                text_attention[side][0],
                text_attention[side][2],
                text_plan,
                segments,
                "text_attention_back",
            )
        text_bucket = Steps(
            bucket_steps, [text_units[0][0], text_back[0][0]], [text_there, swap(text_back[1][0])]
        )
        text_grads, text_sums_one = text_rows_back(
            text_rows,
            [text_back[side][2] for side in sides],
            text_grad_resid,
            text_gain,
            LANES,
        )
        text_later = lax.ppermute(text_grads[:halo], "tensor", [(1, 0)])
        text_own = text_grads[halo:]
        text_input_grad = jnp.concatenate(
            [text_own[: text_count - halo], text_own[text_count - halo :] + text_later]
        ).astype(BF16)
        vector_sums = Steps(
            vector_steps,
            [video_sums_one, video_sums, message_sums * 0.5, text_sums_one, text_sums],
            *(
                [video_back[side][1], video_units[side][2], text_back[side][1], text_units[side][1]]
                for side in sides
            ),
        )
        late_grads, late_class = tie((video_grads, class_row), text_grads)
        video_input_grad = (
            late_grads.reshape(frames, frame_rows, width)[:, :tokens].at[:, 0].set(late_class)[None]
        )
        chains = (text_bucket, factor_rows, vector_sums)
        arrivals = ()
        while any(chain.result is None for chain in chains):
            waited = (text_grads, arrivals)
            arrivals = tuple(chain.step(*waited) for chain in chains if chain.result is None)
        done = vector_sums.result

        gathered = factor_rows.result
        gathered = [gathered[:, at * width : (at + 1) * width] for at in range(8)]
        contract = functools.partial(jnp.einsum, "rd,re->de", preferred_element_type=F32)
        grad_video_message_weight = contract(gathered[0], gathered[4])
        grad_video_message_out_weight = contract(gathered[2], gathered[3])
        grad_video_message_attend_weight = jnp.stack(
            [contract(gathered[1], gathered[5 + part]) for part in range(3)]
        ).transpose(1, 0, 2)
        text_summed = text_bucket.result
        units = text_expand_weight.shape[1]
        grad_text_expand_weight, grad_text_reduce_weight = unpack_units(
            text_summed[0], text_width, units, units // TEXT_CHUNKS, "text_units_grads"
        )
        grad_text_attend_weight, grad_text_output_weight = unpack_attention(
            text_summed[1],
            text_width,
            text_attend_weight.shape[2] // LANES,
            "text_attention_grads",
        )
        return (
            video_input_grad,
            text_final,
            text_input_grad,
            done,
            grad_video_message_weight,
            grad_video_message_out_weight,
            grad_video_message_attend_weight,
            grad_text_expand_weight,
            grad_text_reduce_weight,
            grad_text_attend_weight,
            grad_text_output_weight,
        )

    def never():
        return jax.tree.map(lambda like: jnp.zeros(like.shape, like.dtype), jax.eval_shape(apart))

    (
        video_input_grad,
        text_final,
        text_input_grad,
        done,
        grad_video_message_weight,
        grad_video_message_out_weight,
        grad_video_message_attend_weight,
        grad_text_expand_weight,
        grad_text_reduce_weight,
        grad_text_attend_weight,
        grad_text_output_weight,
    ) = lax.cond(lax.optimization_barrier(jnp.bool_(True)), apart, never)
    grad_video_attend_weight, grad_video_output_weight = unpack_attention(
        (video_sum[2], jnp.zeros(1, jnp.int32)), width, video_attend_weight.shape[2] // LANES, "video_attention_grads"
    )
    grad_video_expand_weight, grad_video_reduce_weight = [
        value.astype(F32) for value in video_sum[:2]
    ]
    first_sums, sums, token_sums, text_first_sums, text_final_sums, *unit_sums = done
    return (
        video_output,
        message_output,
        text_final,
        video_input_grad,
        text_input_grad,
        first_sums[0],
        first_sums[1],
        grad_video_message_weight,
        token_sums[4],
        token_sums[2],
        token_sums[3],
        grad_video_message_attend_weight,
        token_sums[:2],
        grad_video_message_out_weight,
        token_sums[5],
        grad_video_attend_weight.transpose(1, 0, 2),
        unit_sums[0],
        grad_video_output_weight,
        sums[3],
        sums[1],
        sums[2],
        grad_video_expand_weight,
        unit_sums[1][0],
        grad_video_reduce_weight,
        sums[0],
        text_first_sums[0],
        text_first_sums[1],
        grad_text_attend_weight.transpose(1, 0, 2),
        unit_sums[2],
        grad_text_output_weight,
        text_final_sums[3],
        text_final_sums[1],
        text_final_sums[2],
        grad_text_expand_weight,
        unit_sums[3][0],
        grad_text_reduce_weight,
        text_final_sums[0],
    )


def solution(mesh):
    in_specs = (
        P("dp", "tensor", None, None),
        P(("dp", "tensor"), None),
        P("dp", None),
        P(),
        P(),
        P(),
        P(),
        P(),
        P(),
        P(),
        P(),
        P(),
        P(),
        P(None, None, "tensor"),
        P(None, "tensor"),
        P("tensor", None),
        P(),
        P(),
        P(),
        P(None, "tensor"),
        P("tensor"),
        P("tensor", None),
        P(),
        P(),
        P(),
        P(None, None, "tensor"),
        P(None, "tensor"),
        P("tensor", None),
        P(),
        P(),
        P(),
        P(None, "tensor"),
        P("tensor"),
        P("tensor", None),
        P(),
        P("dp", "tensor", None, None),
        P("dp", "tensor", None),
        P(("dp", "tensor"), None),
    )
    out_specs = (
        P("dp", "tensor", None, None),
        P("dp", "tensor", None),
        P(("dp", "tensor"), None),
        P("dp", "tensor", None, None),
        P(("dp", "tensor"), None),
        P(),
        P(),
        P(),
        P(),
        P(),
        P(),
        P(),
        P(),
        P(),
        P(),
        P(None, None, "tensor"),
        P(None, "tensor"),
        P("tensor", None),
        P(),
        P(),
        P(),
        P(None, "tensor"),
        P("tensor"),
        P("tensor", None),
        P(),
        P(),
        P(),
        P(None, None, "tensor"),
        P(None, "tensor"),
        P("tensor", None),
        P(),
        P(),
        P(),
        P(None, "tensor"),
        P("tensor"),
        P("tensor", None),
        P(),
    )
    return jax.shard_map(
        on_device, mesh=mesh, in_specs=in_specs, out_specs=out_specs, check_vma=False
    )
```
